512 devices in a mesh: slab: 32 (over y, x), sub: 16 (over z, core).
Axes of the slice: x: 4, y: 8, z: 8, core: 2. Of those that a mesh axis runs over, the one named last changes fastest.
Arguments:
- positions: float32 [3, 524288], P(None, 'slab'), may hold values from 0 to 129, as said below
- velocity: float32 [3, 524288], P(None, 'slab'), may hold values from -6 to 6
- density: float32 [524288], P('slab'), may hold values from 0.1 to 10
- pressure: float32 [524288], P('slab'), may hold values from 0.1 to 10
- counts: int32 [4096], P('slab'), may hold values from 8 to 128, as said below
- pair_list: int32 [3, 20480], P(None, ('slab', 'sub')), may hold values from -128 to 4095, as said below
Outputs:
- rates: float32 [5, 524288], P(None, 'slab')
The draws below stay inside these ranges and needn't reach their ends.
Inputs may be any that keep to these rules, and one draw needn't show every extreme that they name: `positions`: particle k of leaf g lies in slab floor(g / 128) along x (x minus that index in [0, 1)), in column g mod 128 along y (likewise), and z in [0, 1). `counts`: at least 8 live particles a leaf; some leaf holds 128. `pair_list`: row 0 is a slot's home leaf, a leaf of this device's part of its slab (columns 8 * i to 8 * i + 7 on the device of index i along sub), or -1 for an empty slot. Row 1 is the other leaf, -1 for an empty slot: the home leaf itself, the leaf of the next column cyclically in the same slab, or a leaf of the next slab cyclically whose column is the home column - 1, + 0 or + 1 plus w, modulo 128; w is 0 for home leaves outside the last slab and one shift common to all pairs headed in the last slab. Row 2 is the image offset along y in units of cell width, 0 for an empty slot and for a pair of a leaf with itself; for a pair into the next slab, minus row 2 modulo 128 equals w. A leaf heads at most 5 pairs, each device holds at most 40 live slots, and some device holds exactly that many.
All inputs are finite; a program needn't handle non-finite values.
Results may differ from the reference program's by a relative error of at most 0.0003.
Values sent between devices are 32-bit elements; how exact they have to be, the bound alone decides.
A program may use at most 64 MiB of HBM per device.

```python
import math
import jax
import jax.numpy as jnp
from jax import lax

LEAF = 128
CAND = 5
LEAF_SUB = 8
SLAB_LEAVES = 128
LEAVES = 4096
PARTICLES = 524288
PAIR_SUB = 40
PAIRS = 20480


def draw_positions(key, part):
    particle = jnp.arange(PARTICLES, dtype=jnp.int32)
    leaf_index = particle // LEAF
    slab_coord = (leaf_index // SLAB_LEAVES).astype(jnp.float32)
    column = (leaf_index % SLAB_LEAVES).astype(jnp.float32)
    spread = jax.random.uniform(key, (3, PARTICLES), jnp.float32)
    return jnp.stack([slab_coord + spread[0], column + spread[1], spread[2]]).astype(jnp.float32)


def draw_counts(key, part):
    groups = LEAVES // LEAF_SUB
    level_key, count_key, peak_key = jax.random.split(jax.random.fold_in(key, 11), 3)
    levels = jax.random.randint(level_key, (groups,), 0, 3)
    floors = jnp.array([8, 48, 112], jnp.int32)[levels]
    floors = jnp.repeat(floors, LEAF_SUB)
    drawn_counts = jax.random.randint(count_key, (LEAVES,), floors, LEAF + 1)
    peak_leaf = jax.random.randint(peak_key, (), 0, LEAVES)
    return jnp.where(jnp.arange(LEAVES, dtype=jnp.int32) == peak_leaf, LEAF, drawn_counts).astype(jnp.int32)


def draw_pair_list(key, part):
    devices = LEAVES // LEAF_SUB
    slab_total = LEAVES // SLAB_LEAVES
    core_total = SLAB_LEAVES // LEAF_SUB
    shear_key, level_key, keep_key, full_key, order_key = jax.random.split(jax.random.fold_in(key, 23), 5)
    shear_cells = jax.random.randint(shear_key, (), LEAF_SUB, SLAB_LEAVES)
    device = jnp.arange(devices, dtype=jnp.int32)[:, None, None]
    local_leaf = jnp.arange(LEAF_SUB, dtype=jnp.int32)[None, :, None]
    candidate = jnp.arange(CAND, dtype=jnp.int32)[None, None, :]
    slab_of = device // core_total
    column = device % core_total * LEAF_SUB + local_leaf
    home_leaf = slab_of * SLAB_LEAVES + column
    same_column = (column + 1) % SLAB_LEAVES
    same_other = slab_of * SLAB_LEAVES + same_column
    same_offset = column + 1 - same_column
    next_slab = (slab_of + 1) % slab_total
    wrapped = (slab_of == slab_total - 1).astype(jnp.int32)
    target = column + candidate - 3
    next_column = (target + wrapped * shear_cells) % SLAB_LEAVES
    next_other = next_slab * SLAB_LEAVES + next_column
    next_offset = target - next_column
    other_leaf = jnp.where(candidate == 0, home_leaf, jnp.where(candidate == 1, same_other, next_other))
    offset = jnp.where(candidate == 0, 0, jnp.where(candidate == 1, same_offset, next_offset))
    levels = jax.random.randint(level_key, (devices, 1, 1), 0, 5)
    full_device = jax.random.randint(full_key, (), 0, devices)
    levels = jnp.where(device == full_device, 4, levels)
    kept_pair = (jax.random.randint(keep_key, (devices, LEAF_SUB, CAND), 0, 4) < levels) | (candidate < 2)
    shape = (devices, LEAF_SUB, CAND)
    pair_rows = jnp.stack([jnp.where(kept_pair, jnp.broadcast_to(home_leaf, shape), -1), jnp.where(kept_pair, jnp.broadcast_to(other_leaf, shape), -1), jnp.where(kept_pair, jnp.broadcast_to(offset, shape), 0)])
    flattened = pair_rows.reshape(3, devices, LEAF_SUB * CAND)
    order_keys = jax.random.split(order_key, devices)
    shuffles = jax.vmap(lambda one_key: jax.random.permutation(one_key, LEAF_SUB * CAND))(order_keys)
    shuffled = jnp.take_along_axis(flattened, shuffles[None].astype(jnp.int32), axis=2)
    return shuffled.reshape(3, devices * LEAF_SUB * CAND).astype(jnp.int32)


def shard_levels(own_key, dims, cuts, smallest, largest):
    def one(dim, shards_of):
        draws = jax.random.uniform(jax.random.fold_in(jax.random.fold_in(own_key, 6), dim), (shards_of,), jnp.float32, smallest / len(cuts), largest / len(cuts))
        return jnp.repeat(jnp.exp(draws), dims[dim] // shards_of).reshape((-1,) + (1,) * (len(dims) - dim - 1))

    level = one(*cuts[0])
    for cut in cuts[1:]:
        level = level * one(*cut)
    return level


def centred(stream_key, extent, width, most, cuts=(), held_as=jnp.bfloat16):
    entries = jax.random.normal(stream_key, extent, jnp.float32) * width
    if len(cuts) > 0:
        entries = shard_levels(stream_key, extent, cuts, -0.22, 0.18) * entries
    return jnp.clip(entries, min=-most, max=most).astype(held_as)


def setup_inputs(seed: int = 0) -> dict:
    arg_keys = jax.random.split(jax.random.key(seed), 7)
    positions = draw_positions(jax.random.fold_in(arg_keys[6], 71), 0)
    velocity = centred(arg_keys[1], (3, PARTICLES), 1.0, 6.0, ((1, 32),), jnp.float32)
    density = jnp.clip(jnp.exp(math.log(10.0) - 4.6051702 * jax.random.uniform(arg_keys[2], (PARTICLES,), jnp.float32) ** shard_levels(arg_keys[2], (PARTICLES,), ((0, 32),), -0.2, 0.2)), 0.1, 10.0)
    pressure = jnp.clip(jnp.exp(math.log(10.0) - 4.6051702 * jax.random.uniform(arg_keys[3], (PARTICLES,), jnp.float32) ** shard_levels(arg_keys[3], (PARTICLES,), ((0, 32),), -0.2, 0.2)), 0.1, 10.0)
    counts = draw_counts(jax.random.fold_in(arg_keys[6], 71), 0)
    pair_list = draw_pair_list(jax.random.fold_in(arg_keys[6], 71), 0)
    return {"positions": positions, "velocity": velocity, "density": density, "pressure": pressure, "counts": counts, "pair_list": pair_list}


GAMMA = 5.0 / 3.0
SUPPORT = 1.5
KERNEL_NORM = 21.0 / (2.0 * math.pi * SUPPORT ** 3)
MOMENT_REG = 0.05
SHEAR_SPEED = 1.0
AREA_FLOOR = 0.0001
SYM_PAIRS = ((0, 0), (0, 1), (0, 2), (1, 1), (1, 2), (2, 2))
UNIT_DIAG = (1.0, 0.0, 0.0, 1.0, 0.0, 1.0)

def kernel(dist_sq):
    scaled = jnp.sqrt(dist_sq) / SUPPORT
    inside = jnp.maximum(1.0 - scaled, 0.0)
    return KERNEL_NORM * inside ** 4 * (1.0 + 4.0 * scaled)

def image_rows(tile, wrapped, offset, box_length):
    zero_row = jnp.zeros_like(offset)
    displace = jnp.stack([wrapped * box_length, offset, zero_row, zero_row, -SHEAR_SPEED * wrapped, zero_row, zero_row, zero_row])
    return tile + displace[:, :, None]

def sym_apply(matrix, vector):
    comp_x = matrix[0] * vector[0] + matrix[1] * vector[1] + matrix[2] * vector[2]
    comp_y = matrix[1] * vector[0] + matrix[3] * vector[1] + matrix[4] * vector[2]
    comp_z = matrix[2] * vector[0] + matrix[4] * vector[1] + matrix[5] * vector[2]
    return [comp_x, comp_y, comp_z]

def sym_inverse(matrix):
    entry_xx, entry_xy, entry_xz, entry_yy, entry_yz, entry_zz = matrix
    minor_xx = entry_yy * entry_zz - entry_yz * entry_yz
    minor_xy = entry_xz * entry_yz - entry_xy * entry_zz
    minor_xz = entry_xy * entry_yz - entry_xz * entry_yy
    minor_yy = entry_xx * entry_zz - entry_xz * entry_xz
    minor_yz = entry_xy * entry_xz - entry_xx * entry_yz
    minor_zz = entry_xx * entry_yy - entry_xy * entry_xy
    determinant = entry_xx * minor_xx + entry_xy * minor_xy + entry_xz * minor_xz
    return [minor / determinant for minor in (minor_xx, minor_xy, minor_xz, minor_yy, minor_yz, minor_zz)]

def moment_tile(near_tile, far_tile, mask_near, mask_far, weight):
    separation = [far_tile[direction][:, None, :] - near_tile[direction][:, :, None] for direction in range(3)]
    dist_sq = separation[0] * separation[0] + separation[1] * separation[1] + separation[2] * separation[2]
    smoothing = kernel(dist_sq) * mask_near[:, :, None] * mask_far[:, None, :] * weight[:, None, None]
    summands = [smoothing] + [smoothing * separation[left_axis] * separation[right_axis] for left_axis, right_axis in SYM_PAIRS]
    for quantity in range(5):
        weighted = smoothing * (far_tile[3 + quantity][:, None, :] - near_tile[3 + quantity][:, :, None])
        summands = summands + [weighted * separation[direction] for direction in range(3)]
    row_sums = jnp.stack([lax.optimization_barrier(jnp.sum(summand, axis=2)) for summand in summands])
    col_sums = jnp.stack([lax.optimization_barrier(jnp.sum(summand, axis=1)) for summand in summands])
    return (row_sums, col_sums)

def finish_moments(moments, live_mask):
    number_density = moments[0] + 1.0 - live_mask
    inverse_density = 1.0 / number_density
    second = [moments[1 + position] * inverse_density + MOMENT_REG * UNIT_DIAG[position] for position in range(6)]
    inverse = sym_inverse(second)
    slopes = []
    for quantity in range(5):
        numerator = [moments[7 + 3 * quantity + direction] * inverse_density for direction in range(3)]
        slopes = slopes + sym_apply(inverse, numerator)
    return jnp.stack([number_density] + inverse + slopes)

def side_flux(density_side, velocity_side, pressure_side, normal, normal_speed, lag_speed, wave_speed, contact):
    energy = pressure_side / (GAMMA - 1.0) + 0.5 * density_side * (velocity_side[0] ** 2 + velocity_side[1] ** 2 + velocity_side[2] ** 2)
    plain_flux = [density_side * normal_speed]
    plain_flux = plain_flux + [density_side * velocity_side[direction] * normal_speed + pressure_side * normal[direction] for direction in range(3)]
    plain_flux = plain_flux + [(energy + pressure_side) * normal_speed]
    conserved = [density_side] + [density_side * velocity_side[direction] for direction in range(3)] + [energy]
    factor = density_side * lag_speed / (wave_speed - contact)
    speed_gap = contact - normal_speed
    star_state = [factor] + [factor * (velocity_side[direction] + speed_gap * normal[direction]) for direction in range(3)]
    star_state = star_state + [factor * (energy / density_side + speed_gap * (contact + pressure_side / (density_side * lag_speed)))]
    starred = [plain_flux[component] + wave_speed * (star_state[component] - conserved[component]) for component in range(5)]
    return (plain_flux, starred)

def hllc_flux(left_state, right_state, normal, face_vel):
    left_vel = [left_state[direction] - face_vel[direction] for direction in range(3)]
    right_vel = [right_state[direction] - face_vel[direction] for direction in range(3)]
    left_density, left_pressure = (left_state[3], left_state[4])
    right_density, right_pressure = (right_state[3], right_state[4])
    left_normal = left_vel[0] * normal[0] + left_vel[1] * normal[1] + left_vel[2] * normal[2]
    right_normal = right_vel[0] * normal[0] + right_vel[1] * normal[1] + right_vel[2] * normal[2]
    left_sound = jnp.sqrt(GAMMA * left_pressure / left_density)
    right_sound = jnp.sqrt(GAMMA * right_pressure / right_density)
    speed_left = jnp.minimum(left_normal - left_sound, right_normal - right_sound)
    speed_right = jnp.maximum(left_normal + left_sound, right_normal + right_sound)
    lag_left = speed_left - left_normal
    lag_right = speed_right - right_normal
    contact = (right_pressure - left_pressure + left_density * left_normal * lag_left - right_density * right_normal * lag_right) / (left_density * lag_left - right_density * lag_right)
    flux_left, star_left = side_flux(left_density, left_vel, left_pressure, normal, left_normal, lag_left, speed_left, contact)
    flux_right, star_right = side_flux(right_density, right_vel, right_pressure, normal, right_normal, lag_right, speed_right, contact)
    moving = [jnp.where(speed_left >= 0.0, flux_left[component], jnp.where(contact >= 0.0, star_left[component], jnp.where(speed_right >= 0.0, star_right[component], flux_right[component]))) for component in range(5)]
    mass_flux = moving[0]
    momentum = [moving[1 + direction] + face_vel[direction] * mass_flux for direction in range(3)]
    face_sq = face_vel[0] ** 2 + face_vel[1] ** 2 + face_vel[2] ** 2
    energy_flux = moving[4] + face_vel[0] * moving[1] + face_vel[1] * moving[2] + face_vel[2] * moving[3] + 0.5 * face_sq * mass_flux
    return [mass_flux] + momentum + [energy_flux]

def flux_tile(near_tile, far_tile, near_pay, far_pay, mask_near, mask_far, weight):
    separation = [far_tile[direction][:, None, :] - near_tile[direction][:, :, None] for direction in range(3)]
    dist_sq = separation[0] * separation[0] + separation[1] * separation[1] + separation[2] * separation[2]
    smoothing = kernel(dist_sq) * mask_near[:, :, None] * mask_far[:, None, :]
    near_density = near_pay[0][:, :, None]
    far_density = far_pay[0][:, None, :]
    near_matrix = [near_pay[1 + position][:, :, None] for position in range(6)]
    far_matrix = [far_pay[1 + position][:, None, :] for position in range(6)]
    toward_near = sym_apply(near_matrix, separation)
    toward_far = sym_apply(far_matrix, separation)
    near_scale = smoothing / (near_density * near_density)
    far_scale = smoothing / (far_density * far_density)
    area = [near_scale * toward_near[direction] + far_scale * toward_far[direction] for direction in range(3)]
    magnitude = jnp.sqrt(area[0] * area[0] + area[1] * area[1] + area[2] * area[2])
    clamp_scale = 1.0 / jnp.maximum(magnitude, AREA_FLOOR)
    normal = [area[direction] * clamp_scale for direction in range(3)]
    left_state = []
    right_state = []
    for quantity in range(5):
        near_value = near_tile[3 + quantity][:, :, None]
        far_value = far_tile[3 + quantity][:, None, :]
        near_change = 0.5 * (near_pay[7 + 3 * quantity][:, :, None] * separation[0] + near_pay[8 + 3 * quantity][:, :, None] * separation[1] + near_pay[9 + 3 * quantity][:, :, None] * separation[2])
        far_change = 0.5 * (far_pay[7 + 3 * quantity][:, None, :] * separation[0] + far_pay[8 + 3 * quantity][:, None, :] * separation[1] + far_pay[9 + 3 * quantity][:, None, :] * separation[2])
        low_bound = jnp.minimum(near_value, far_value)
        high_bound = jnp.maximum(near_value, far_value)
        left_state.append(jnp.clip(near_value + near_change, low_bound, high_bound))
        right_state.append(jnp.clip(far_value - far_change, low_bound, high_bound))
    face_vel = [0.5 * (near_tile[3 + direction][:, :, None] + far_tile[3 + direction][:, None, :]) for direction in range(3)]
    fluxes = hllc_flux(left_state, right_state, normal, face_vel)
    pair_scale = magnitude * weight[:, None, None]
    row_sums = jnp.stack([-lax.optimization_barrier(jnp.sum(pair_scale * face_flux, axis=2)) for face_flux in fluxes])
    col_sums = jnp.stack([lax.optimization_barrier(jnp.sum(pair_scale * face_flux, axis=1)) for face_flux in fluxes])
    return (row_sums, col_sums)

def reference(positions, velocity, density, pressure, counts, pair_list):
    primitive = jnp.concatenate([positions, velocity, density[None], pressure[None]], axis=0).reshape(8, LEAVES, LEAF)
    live_mask = (jnp.arange(LEAF, dtype=jnp.int32)[None, :] < counts[:, None]).astype(jnp.float32)
    box_length = jnp.asarray(LEAVES // SLAB_LEAVES, jnp.float32)
    occupied = pair_list[0] >= 0
    home_leaf = jnp.where(occupied, pair_list[0], 0).astype(jnp.int32)
    other_leaf = jnp.where(occupied, pair_list[1], 0).astype(jnp.int32)
    wrapped = (other_leaf // SLAB_LEAVES < home_leaf // SLAB_LEAVES).astype(jnp.float32)
    offset = pair_list[2].astype(jnp.float32)
    weight = jnp.where(occupied, jnp.where(home_leaf == other_leaf, 0.5, 1.0), 0.0).astype(jnp.float32)
    block_count = PAIRS // PAIR_SUB
    blocked = tuple((column_data.reshape(block_count, PAIR_SUB) for column_data in (home_leaf, other_leaf, wrapped, offset, weight)))

    def moment_step(running, block_data):
        home_part, other_part, wrap_part, offset_part, weight_part = block_data
        near_tile = primitive[:, home_part]
        far_tile = image_rows(primitive[:, other_part], wrap_part, offset_part, box_length)
        row_sums, col_sums = moment_tile(near_tile, far_tile, live_mask[home_part], live_mask[other_part], weight_part)
        running = running.at[:, home_part].add(row_sums).at[:, other_part].add(col_sums)
        return (running, None)
    moments = lax.scan(moment_step, jnp.zeros((22, LEAVES, LEAF), jnp.float32), blocked)[0]
    payload = finish_moments(moments, live_mask)

    def flux_step(running, block_data):
        home_part, other_part, wrap_part, offset_part, weight_part = block_data
        near_tile = primitive[:, home_part]
        far_tile = image_rows(primitive[:, other_part], wrap_part, offset_part, box_length)
        row_sums, col_sums = flux_tile(near_tile, far_tile, payload[:, home_part], payload[:, other_part], live_mask[home_part], live_mask[other_part], weight_part)
        running = running.at[:, home_part].add(row_sums).at[:, other_part].add(col_sums)
        return (running, None)
    flux_sum = lax.scan(flux_step, jnp.zeros((5, LEAVES, LEAF), jnp.float32), blocked)[0]
    return (payload[0][None] * flux_sum).reshape(5, PARTICLES)
```

```python
import functools
import math

import jax
import jax.numpy as jnp
from jax import lax
from jax.experimental import pallas as pl
from jax.experimental.pallas import tpu as pltpu
from jax.sharding import PartitionSpec as P

LEAF = 128
KINDS = 5
WIN = 12
LEVELS = 4
GAMMA = 5.0 / 3.0
SUPPORT = 1.5
KERNEL_NORM = 21.0 / (2.0 * math.pi * SUPPORT**3)
MOMENT_REG = 0.05
AREA_FLOOR = 0.0001
FAR_AWAY = 1.0e6
DEAD_ABOVE = 1.0e5
TINY = 1.2e-38
BLOCK = 2
MESH = pl.DeviceIdType.MESH
VMEM = pl.BlockSpec(memory_space=pltpu.VMEM)
SMEM = pl.BlockSpec(memory_space=pltpu.SMEM)
HIGHEST = lax.Precision.HIGHEST


def around(value, size):
    return lax.rem(value + size, size)


def gather_kernel(slabs, subs, row_ref, out_ref, send_sem, recv_sem, own_sem):
    slab = lax.axis_index("slab")
    sub = lax.axis_index("sub")
    barrier = pltpu.get_barrier_semaphore()

    def greet(shift, first):
        def one(k, carry):
            pl.semaphore_signal(
                barrier,
                inc=1,
                device_id=(around(slab + shift, slabs), around(sub + k, subs)),
                device_id_type=MESH,
            )
            return carry

        lax.fori_loop(first, subs, one, 0)

    for shift in (-2, -1, 0, 1, 2):
        greet(shift, 1 if shift == 0 else 0)
    pl.semaphore_wait(barrier, 5 * subs - 1)

    own_slot = 2 * subs + sub
    own = pltpu.make_async_copy(row_ref, out_ref.at[pl.ds(own_slot, 1)], own_sem)
    own.start()

    def copy(shift, k):
        slot = (shift + 2) * subs + sub
        return pltpu.make_async_remote_copy(
            src_ref=row_ref,
            dst_ref=out_ref.at[pl.ds(slot, 1)],
            send_sem=send_sem.at[(shift + 2) * subs + k],
            recv_sem=recv_sem.at[slot],
            device_id=(around(slab - shift, slabs), around(sub + k, subs)),
            device_id_type=MESH,
        )

    def arrival(shift, k):
        slot = (shift + 2) * subs + around(sub + k, subs)
        return pltpu.make_async_remote_copy(
            src_ref=row_ref,
            dst_ref=out_ref.at[pl.ds(slot, 1)],
            send_sem=send_sem.at[(shift + 2) * subs + k],
            recv_sem=recv_sem.at[slot],
            device_id=(around(slab - shift, slabs), around(sub + k, subs)),
            device_id_type=MESH,
        )

    for shift in (-2, -1, 0, 1):
        first = 1 if shift == 0 else 0

        def send(k, carry, shift=shift):
            copy(shift, k).start()
            return carry

        lax.fori_loop(first, subs, send, 0)
    for shift in (-2, -1, 0, 1):
        first = 1 if shift == 0 else 0

        def settle(k, carry, shift=shift):
            copy(shift, k).wait_send()
            arrival(shift, k).wait_recv()
            return carry

        lax.fori_loop(first, subs, settle, 0)
    own.wait()


def gather_lists(row, slabs, subs):
    return pl.pallas_call(
        functools.partial(gather_kernel, slabs, subs),
        out_shape=jax.ShapeDtypeStruct((4 * subs, 1, LEAF), jnp.int32),
        in_specs=[VMEM],
        out_specs=VMEM,
        scratch_shapes=[
            pltpu.SemaphoreType.DMA((4 * subs,)),
            pltpu.SemaphoreType.DMA((4 * subs,)),
            pltpu.SemaphoreType.DMA,
        ],
        compiler_params=pltpu.CompilerParams(collective_id=0, has_side_effects=True),
        name="gather_lists",
    )(row)


def pair_tables(lists, slab, slabs, slots, slab_leaves):
    subs = lists.shape[0] // 4
    entries = lists.reshape(4, subs, LEAF)
    home = entries[:, :, :slots]
    other = entries[:, :, slots : 2 * slots]
    offset = entries[:, :, 2 * slots : 3 * slots]
    occupied = home >= 0
    home_slab = home // slab_leaves
    other_slab = other // slab_leaves
    crossing = occupied & (home_slab != other_slab)
    shear = jnp.max(
        jnp.where(crossing & (home_slab == slabs - 1), (-offset) % slab_leaves, 0)
    )
    step = (other % slab_leaves - home % slab_leaves + offset + 1) % slab_leaves
    kind = jnp.where(other == home, 0, jnp.where(crossing, 2 + step, 1))
    kind = jnp.where(kind < KINDS, kind, KINDS * slab_leaves)
    homes = slab_leaves // subs
    key = jnp.where(occupied, (home % homes) * KINDS + kind, -1)[1:]
    hot = key[:, :, None, :] == jnp.arange(homes * KINDS, dtype=jnp.int32)[:, None]
    number = jnp.sum(hot.astype(jnp.int32), axis=3)
    moved = jnp.max(jnp.where(hot, offset[1:][:, :, None, :], -(2**20)), axis=3)
    return shear, number.reshape(-1), moved.reshape(-1)


def window_kernel(
    slabs, subs, meta, counts, positions, velocity, density, pressure, own, below, above, beyond
):
    slab, sub, shear = meta[0], meta[1], meta[2]
    slab_leaves = counts.shape[0]
    homes = slab_leaves // subs
    no_shear = jnp.int32(0)
    shifts = (
        no_shear,
        jnp.where(slab == slabs - 1, -shear, no_shear),
        jnp.where(slab == 0, shear, no_shear),
        jnp.where(slab <= 1, shear, no_shear),
    )
    lane = lax.broadcasted_iota(jnp.int32, (1, LEAF), 1)
    row = lax.broadcasted_iota(jnp.int32, (3, LEAF), 0)
    for shift, target in zip(shifts, (own, below, above, beyond)):

        def one(slot, carry, shift=shift, target=target):
            column = lax.rem(sub * homes + slot - 2 + shift + 2 * slab_leaves, slab_leaves)
            start = pl.multiple_of(column * LEAF, LEAF)
            live = lane < counts[column]
            centre = jnp.where(
                row == 0,
                slab.astype(jnp.float32) + 0.5,
                jnp.where(row == 1, column.astype(jnp.float32) + 0.5, 0.5),
            )
            place = positions[:, pl.ds(start, LEAF)] - centre
            place = jnp.where((row > 0) | live, place, FAR_AWAY)
            target[slot, 0:3, :] = place
            target[slot, 3:6, :] = velocity[:, pl.ds(start, LEAF)]
            target[slot, 6:7, :] = density[pl.ds(column, 1), :]
            target[slot, 7:8, :] = pressure[pl.ds(column, 1), :]
            return carry

        lax.fori_loop(0, WIN, one, 0)


def leaf_windows(meta, counts, positions, velocity, density, pressure, slabs, subs):
    window = jax.ShapeDtypeStruct((WIN, 8, LEAF), jnp.float32)
    return pl.pallas_call(
        functools.partial(window_kernel, slabs, subs),
        out_shape=(window,) * 4,
        in_specs=[SMEM, SMEM, VMEM, VMEM, VMEM, VMEM],
        out_specs=(VMEM,) * 4,
        name="leaf_windows",
    )(meta, counts, positions, velocity, density, pressure)


def swap_kernel(
    slabs, below, above, beyond, got_below, got_above, got_beyond, send_sem, recv_sem
):
    slab = lax.axis_index("slab")
    sub = lax.axis_index("sub")
    barrier = pltpu.get_barrier_semaphore()
    for shift in (-2, -1, 1, 2):
        pl.semaphore_signal(
            barrier, inc=1, device_id=(around(slab + shift, slabs), sub), device_id_type=MESH
        )
    pl.semaphore_wait(barrier, 4)
    copies = []
    for k, (shift, source, target) in enumerate(
        ((1, below, got_below), (-1, above, got_above), (-2, beyond, got_beyond))
    ):
        copies.append(
            pltpu.make_async_remote_copy(
                src_ref=source,
                dst_ref=target,
                send_sem=send_sem.at[k],
                recv_sem=recv_sem.at[k],
                device_id=(around(slab + shift, slabs), sub),
                device_id_type=MESH,
            )
        )
        copies[-1].start()
    for one in copies:
        one.wait()


def swap_windows(below, above, beyond, slabs):
    window = jax.ShapeDtypeStruct((WIN, 8, LEAF), jnp.float32)
    return pl.pallas_call(
        functools.partial(swap_kernel, slabs),
        out_shape=(window,) * 3,
        in_specs=[VMEM] * 3,
        out_specs=(VMEM,) * 3,
        scratch_shapes=[pltpu.SemaphoreType.DMA((3,)), pltpu.SemaphoreType.DMA((3,))],
        compiler_params=pltpu.CompilerParams(collective_id=1, has_side_effects=True),
        name="swap_windows",
    )(below, above, beyond)


def rows_of(entries):
    full = jnp.concatenate(
        [
            entries,
            entries[0:1] * entries,
            entries[1:2] * entries,
            entries[2:3] * entries,
            jnp.ones_like(entries),
        ],
        axis=0,
    )
    first = full.astype(jnp.bfloat16).astype(jnp.float32)
    rest = full - first
    second = rest.astype(jnp.bfloat16).astype(jnp.float32)
    third = rest - second
    return jnp.concatenate([first, second, third], axis=0).astype(jnp.bfloat16)


def moment_rows(sums, entries, scale):
    sums = sums[0:40] + sums[40:80] + sums[80:120]
    plain, total = sums[0:8], sums[32:33]
    parts = []
    for k in range(3):
        own = entries[k : k + 1]
        parts.append(
            sums[8 * k + 8 : 8 * k + 16]
            - own * plain
            - entries * sums[k : k + 1]
            + own * (entries * total)
        )
    parts.append(sums[32:40])
    return scale * jnp.concatenate(parts, axis=0)


def displaced(entries, row, gap_x, gap_y, gap_v):
    entries = jnp.where(entries > DEAD_ABOVE, -entries, entries)
    return entries + jnp.where(
        row == 0, gap_x, jnp.where(row == 1, gap_y, jnp.where(row == 4, gap_v, 0.0))
    )


def weights(dx, dy, dz):
    dist_sq = jnp.maximum(dx * dx + dy * dy + dz * dz, TINY)
    scaled = dist_sq * lax.rsqrt(dist_sq) * (1.0 / SUPPORT)
    inside = jnp.maximum(1.0 - scaled, 0.0)
    inside = inside * inside
    return inside * inside * (1.0 + 4.0 * scaled)


def finish(sums, entries):
    live = (entries[0:1] < DEAD_ABOVE).astype(jnp.float32)
    number = sums[24:25] + 1.0 - live
    inverse = 1.0 / number
    xx = sums[0:1] * inverse + MOMENT_REG
    xy = sums[1:2] * inverse
    xz = sums[2:3] * inverse
    yy = sums[9:10] * inverse + MOMENT_REG
    yz = sums[10:11] * inverse
    zz = sums[18:19] * inverse + MOMENT_REG
    minor_xx = yy * zz - yz * yz
    minor_xy = xz * yz - xy * zz
    minor_xz = xy * yz - xz * yy
    minor_yy = xx * zz - xz * xz
    minor_yz = xy * xz - xx * yz
    minor_zz = xx * yy - xy * xy
    unit = 1.0 / (xx * minor_xx + xy * minor_xy + xz * minor_xz)
    ixx, ixy, ixz = minor_xx * unit, minor_xy * unit, minor_xz * unit
    iyy, iyz, izz = minor_yy * unit, minor_yz * unit, minor_zz * unit
    half = 0.5 * inverse
    mx, my, mz = sums[0:8] * half, sums[8:16] * half, sums[16:24] * half
    slope_x = ixx * mx + ixy * my + ixz * mz
    slope_y = ixy * mx + iyy * my + iyz * mz
    slope_z = ixz * mx + iyz * my + izz * mz
    scale = KERNEL_NORM * inverse * inverse
    return jnp.concatenate(
        [
            entries,
            slope_x,
            slope_y,
            slope_z,
            ixx * scale,
            ixy * scale,
            ixz * scale,
            iyy * scale,
            iyz * scale,
            izz * scale,
            number,
            number,
        ],
        axis=0,
    )


FLUX_ROWS = (
    tuple(range(8))
    + tuple(8 * k + 11 + q for q in range(5) for k in range(3))
    + tuple(range(32, 38))
)


def flux_terms(near, far, weight):
    d = [far(k) - near(k) for k in range(3)]
    smooth = weights(d[0], d[1], d[2])
    mxx, mxy, mxz, myy, myz, mzz = [near(23 + k) + far(23 + k) for k in range(6)]
    area = [
        smooth * (mxx * d[0] + mxy * d[1] + mxz * d[2]),
        smooth * (mxy * d[0] + myy * d[1] + myz * d[2]),
        smooth * (mxz * d[0] + myz * d[1] + mzz * d[2]),
    ]
    area_sq = area[0] * area[0] + area[1] * area[1] + area[2] * area[2]
    root = lax.rsqrt(jnp.maximum(area_sq, TINY))
    size = area_sq * root * weight
    root = jnp.minimum(root, 1.0 / AREA_FLOOR)
    normal = [area[k] * root for k in range(3)]

    def slope(side, q):
        return side(8 + 3 * q) * d[0] + side(9 + 3 * q) * d[1] + side(10 + 3 * q) * d[2]

    left_vel, right_vel, face = [], [], []
    for q in range(3):
        a, b = near(3 + q), far(3 + q)
        face.append(a + b)
        gap = b - a
        high = jnp.abs(gap)
        low = -high
        left_vel.append(jnp.minimum(jnp.maximum(slope(near, q) - gap, low), high))
        right_vel.append(jnp.minimum(jnp.maximum(gap - slope(far, q), low), high))
    states = []
    for q in (3, 4):
        a, b = near(3 + q), far(3 + q)
        low, high = jnp.minimum(a, b), jnp.maximum(a, b)
        states.append(jnp.minimum(jnp.maximum(a + slope(near, q), low), high))
        states.append(jnp.minimum(jnp.maximum(b - slope(far, q), low), high))
    left_rho, right_rho, left_p, right_p = states
    left_un = left_vel[0] * normal[0] + left_vel[1] * normal[1] + left_vel[2] * normal[2]
    right_un = right_vel[0] * normal[0] + right_vel[1] * normal[1] + right_vel[2] * normal[2]
    root_gamma = math.sqrt(GAMMA)
    left_c = root_gamma * left_p * lax.rsqrt(left_p * left_rho)
    right_c = root_gamma * right_p * lax.rsqrt(right_p * right_rho)
    speed_left = jnp.minimum(left_un - left_c, right_un - right_c)
    speed_right = jnp.maximum(left_un + left_c, right_un + right_c)
    left_m = left_rho * (speed_left - left_un)
    right_m = right_rho * (speed_right - right_un)
    top = right_p - left_p + left_m * left_un - right_m * right_un
    bottom = left_m - right_m
    is_left = top <= 0.0

    def pick(left, right):
        return jnp.where(is_left, left, right)

    rho, p, un = pick(left_rho, right_rho), pick(left_p, right_p), pick(left_un, right_un)
    m, c, speed = pick(left_m, right_m), pick(left_c, right_c), pick(speed_left, speed_right)
    wave = pick(jnp.minimum(speed_left, 0.0), jnp.maximum(speed_right, 0.0))
    lab = [pick(left_vel[k], right_vel[k]) + face[k] for k in range(3)]
    lead = speed * bottom - top
    joint = 1.0 / (bottom * lead)
    contact = top * (lead * joint)
    spread = bottom * (bottom * joint)
    push = wave * ((contact - un) * spread)
    mass = (rho * un + wave * (m * spread - rho)) * size
    thrust = (p + push * m) * size
    carried = (1.5 / GAMMA) * (c * c) + 0.5 * (
        lab[0] * lab[0] + lab[1] * lab[1] + lab[2] * lab[2]
    )
    drift = face[0] * normal[0] + face[1] * normal[1] + face[2] * normal[2]
    energy = mass * carried + drift * thrust + size * (p * un + push * (m * contact + p))
    return [mass] + [lab[k] * mass + normal[k] * thrust for k in range(3)] + [energy]


def pair_kernel(
    slabs,
    subs,
    meta,
    counts,
    number_tab,
    offset_tab,
    below,
    own,
    above,
    beyond,
    own_out,
    above_out,
    store,
    moments,
    near_xyz,
    finished,
    near_rows,
    far_rows,
    row_sums,
    flux_sums,
):
    slab, sub, shear = meta[0], meta[1], meta[2]
    slab_leaves = counts.shape[0]
    homes = slab_leaves // subs
    row = lax.broadcasted_iota(jnp.int32, (8, LEAF), 0)
    for level, source in enumerate((below, own, above, beyond)):
        store[pl.ds(level * WIN, WIN)] = source[...]
    moments[...] = jnp.zeros_like(moments)
    flux_sums[...] = jnp.zeros_like(flux_sums)

    def home_facts(leaf):
        level = leaf // WIN
        place = leaf - level * WIN - 2
        level_slab = lax.rem(slab - 1 + level + slabs, slabs)
        shift = jnp.where(
            (level == 0) & (slab == 0),
            -shear,
            jnp.where((level == 2) & (slab == slabs - 1), shear, 0),
        )
        column = lax.rem(sub * homes + place + shift + 2 * slab_leaves, slab_leaves)
        return level, place, column, level_slab == slabs - 1

    def pair_facts(leaf, kind, facts):
        level, place, column, last = facts
        entry = (level * slab_leaves + column) * KINDS + kind
        crossing = kind >= 2
        step = jnp.where(crossing, kind - 3, jnp.where(kind == 1, 1, 0))
        wraps = crossing & last
        other_column = lax.rem(
            column + step + jnp.where(wraps, shear, 0) + slab_leaves, slab_leaves
        )
        other = leaf + step + jnp.where(crossing, WIN, 0)
        gap_x = jnp.where(crossing, 1.0, 0.0).astype(jnp.float32)
        gap_y = (other_column + offset_tab[entry] - column).astype(jnp.float32)
        gap_v = jnp.where(wraps, -1.0, 0.0).astype(jnp.float32)
        scale = number_tab[entry].astype(jnp.float32) * jnp.where(kind == 0, 0.5, 1.0).astype(
            jnp.float32
        )
        return number_tab[entry], other, place + step, crossing, gap_x, gap_y, gap_v, scale

    def wanted(level, place):
        return ((level == 1) & (place >= 0) & (place <= homes)) | (
            (level == 2) & (place >= -1) & (place <= homes)
        )

    def moment_home(leaf, carry):
        facts = home_facts(leaf)
        level, place = facts[0], facts[1]
        mine = store[leaf]
        turned = jnp.transpose(mine)
        for k in range(3):
            near_xyz[k] = jnp.broadcast_to(turned[:, k : k + 1], (LEAF, LEAF))

        def one(kind, carry):
            number, other, other_place, crossing, gap_x, gap_y, gap_v, scale = pair_facts(
                leaf, kind, facts
            )
            other_level = level + jnp.where(crossing, 1, 0)
            use = (number > 0) & (wanted(level, place) | wanted(other_level, other_place))

            @pl.when(use)
            def _():
                theirs = displaced(store[other], row, gap_x, gap_y, gap_v)
                smooth = weights(
                    theirs[0:1] - near_xyz[0],
                    theirs[1:2] - near_xyz[1],
                    theirs[2:3] - near_xyz[2],
                )
                high = smooth.astype(jnp.bfloat16)
                low = (smooth - high.astype(jnp.float32)).astype(jnp.bfloat16)
                near_part, far_part = rows_of(mine), rows_of(theirs)
                across = (((1,), (1,)), ((), ()))
                along = (((1,), (0,)), ((), ()))

                def times(part, matrix, dims):
                    return lax.dot_general(
                        part, matrix, dims, preferred_element_type=jnp.float32
                    )

                to_near = times(far_part, high, across) + times(far_part, low, across)
                to_far = times(near_part, high, along) + times(near_part, low, along)
                scaled = scale * KERNEL_NORM
                moments[leaf] = moments[leaf] + moment_rows(to_near, mine, scaled)
                moments[other] = moments[other] + moment_rows(to_far, theirs, scaled)

            return carry

        return lax.fori_loop(0, KINDS, one, carry)

    lax.fori_loop(0, 3 * WIN, moment_home, 0)

    own_first, above_first = WIN + 2, 2 * WIN + 1
    halves = jnp.where((row >= 3) & (row < 6), 0.5, 1.0).astype(jnp.float32)

    def finish_one(k, carry):
        leaf = jnp.where(k <= homes, own_first + k, above_first + k - (homes + 1))
        mine = store[leaf]
        done = finish(moments[leaf], mine)
        finished[leaf] = done
        finished[leaf, 0:8] = mine * halves
        return carry

    lax.fori_loop(0, 2 * homes + 3, finish_one, 0)
    ones = jnp.ones((8, LEAF), jnp.float32)

    def flux_home(place, carry):
        leaf = own_first + place
        facts = home_facts(leaf)
        turned = jnp.transpose(finished[leaf])
        for k, source in enumerate(FLUX_ROWS):
            near_rows[k] = jnp.broadcast_to(turned[:, source : source + 1], (LEAF, LEAF)).reshape(
                LEAF // 8, 8, LEAF
            )
        row_sums[...] = jnp.zeros_like(row_sums)
        steps = (counts[facts[2]] + 8 * BLOCK - 1) // (8 * BLOCK)

        def one(kind, carry):
            number, other, _, _, gap_x, gap_y, gap_v, scale = pair_facts(leaf, kind, facts)

            @pl.when(number > 0)
            def _():
                theirs = finished[other]
                head = displaced(theirs[0:8], row, gap_x, gap_y, 0.5 * gap_v)
                for k, source in enumerate(FLUX_ROWS):
                    part = head if source < 8 else theirs
                    far_rows[k] = jnp.broadcast_to(part[source : source + 1], (8, LEAF))

                def step(group, sums):
                    first = group * BLOCK

                    def near(k):
                        return near_rows[k, pl.ds(first, BLOCK)]

                    def far(k):
                        return far_rows[k][None]

                    terms = flux_terms(near, far, scale)
                    totals = []
                    for k in range(5):
                        row_sums[k, pl.ds(first, BLOCK)] += terms[k]
                        totals.append(sums[k] + jnp.sum(terms[k], axis=0))
                    return tuple(totals)

                empty = jnp.zeros((8, LEAF), jnp.float32)
                sums = lax.fori_loop(0, steps, step, (empty,) * 5)
                added = [jnp.sum(part, axis=0, keepdims=True) for part in sums]
                nothing = jnp.zeros((3, LEAF), jnp.float32)
                flux_sums[other] = flux_sums[other] + jnp.concatenate(added + [nothing], axis=0)

            return carry

        lax.fori_loop(0, KINDS, one, 0)
        taken = []
        for k in range(5):
            total = lax.dot_general(
                ones,
                row_sums[k].reshape(LEAF, LEAF),
                (((1,), (1,)), ((), ())),
                precision=HIGHEST,
                preferred_element_type=jnp.float32,
            )
            taken.append(total[0:1])
        nothing = jnp.zeros((3, LEAF), jnp.float32)
        flux_sums[leaf] = flux_sums[leaf] - jnp.concatenate(taken + [nothing], axis=0)
        return carry

    lax.fori_loop(0, homes, flux_home, 0)
    for k in range(homes + 1):
        own_out[k] = flux_sums[own_first + k]
        own_out[k, 5:6, :] = finished[own_first + k, 38:39, :]
    for k in range(homes + 2):
        above_out[k] = flux_sums[above_first + k]


def pair_sums(meta, counts, number_tab, offset_tab, windows, slabs, subs):
    homes = counts.shape[0] // subs
    leaves = LEVELS * WIN
    return pl.pallas_call(
        functools.partial(pair_kernel, slabs, subs),
        out_shape=(
            jax.ShapeDtypeStruct((homes + 1, 8, LEAF), jnp.float32),
            jax.ShapeDtypeStruct((homes + 2, 8, LEAF), jnp.float32),
        ),
        in_specs=[SMEM] * 4 + [VMEM] * 4,
        out_specs=(VMEM, VMEM),
        scratch_shapes=[
            pltpu.VMEM((leaves, 8, LEAF), jnp.float32),
            pltpu.VMEM((leaves, 32, LEAF), jnp.float32),
            pltpu.VMEM((3, LEAF, LEAF), jnp.float32),
            pltpu.VMEM((leaves, 40, LEAF), jnp.float32),
            pltpu.VMEM((len(FLUX_ROWS), LEAF // 8, 8, LEAF), jnp.float32),
            pltpu.VMEM((len(FLUX_ROWS), 8, LEAF), jnp.float32),
            pltpu.VMEM((5, LEAF // 8, 8, LEAF), jnp.float32),
            pltpu.VMEM((leaves, 8, LEAF), jnp.float32),
        ],
        name="pair_sums",
    )(meta, counts, number_tab, offset_tab, *windows)


def collect_kernel(
    slabs, subs, own, above, all_own, all_below, up_sem, ring_send, ring_recv, core_send, core_recv
):
    slab = lax.axis_index("slab")
    sub = lax.axis_index("sub")
    chips = subs // 2
    chip, core = sub // 2, lax.rem(sub, 2)
    partner = 1 - core
    ahead, behind = around(chip + 1, chips), around(chip - 1, chips)
    right_hops = chips // 2
    left_hops = chips - 1 - right_hops
    barrier = pltpu.get_barrier_semaphore()
    for peer in (
        (around(slab + 1, slabs), sub),
        (around(slab - 1, slabs), sub),
        (slab, 2 * ahead + core),
        (slab, 2 * behind + core),
        (slab, 2 * chip + partner),
    ):
        pl.semaphore_signal(barrier, inc=1, device_id=peer, device_id_type=MESH)
    pl.semaphore_wait(barrier, 5)

    upward = pltpu.make_async_remote_copy(
        src_ref=above,
        dst_ref=all_below.at[sub],
        send_sem=up_sem.at[0],
        recv_sem=up_sem.at[1],
        device_id=(around(slab + 1, slabs), sub),
        device_id_type=MESH,
    )
    upward.start()
    mine = pltpu.make_async_copy(own, all_own.at[sub], up_sem.at[2])
    mine.start()

    def ring(which, source, buffer, owner_chip, hop, to_right):
        slot = 2 * owner_chip + core
        place = (hop - 1) if to_right else (right_hops + hop - 1)
        return pltpu.make_async_remote_copy(
            src_ref=source if source is not None else buffer.at[slot],
            dst_ref=buffer.at[slot],
            send_sem=ring_send.at[which, place],
            recv_sem=ring_recv.at[which, place],
            device_id=(slab, 2 * (ahead if to_right else behind) + core),
            device_id_type=MESH,
        )

    def across(which, source, buffer, owner_chip, place):
        slot = 2 * owner_chip + core
        return pltpu.make_async_remote_copy(
            src_ref=source if source is not None else buffer.at[slot],
            dst_ref=buffer.at[slot],
            send_sem=core_send.at[which, place],
            recv_sem=core_recv.at[which, place],
            device_id=(slab, 2 * chip + partner),
            device_id_type=MESH,
        )

    started, expected = [], []

    def launch(which, source, buffer):
        for to_right, hops in ((True, right_hops), (False, left_hops)):
            if hops > 0:
                one = ring(which, source, buffer, chip, 1, to_right)
                one.start()
                started.append(one)
        one = across(which, source, buffer, chip, 0)
        one.start()
        started.append(one)
        expected.append(one)

    launch(0, own, all_own)
    upward.wait()
    launch(1, None, all_below)
    mine.wait()
    for hop in range(1, right_hops + 1):
        for which, buffer in ((0, all_own), (1, all_below)):
            for to_right, hops in ((True, right_hops), (False, left_hops)):
                if hop > hops:
                    continue
                owner = around(chip - hop, chips) if to_right else around(chip + hop, chips)
                ring(which, None, buffer, owner, hop, to_right).wait_recv()
                if hop < hops:
                    one = ring(which, None, buffer, owner, hop + 1, to_right)
                    one.start()
                    started.append(one)
                place = hop if to_right else right_hops + hop
                one = across(which, None, buffer, owner, place)
                one.start()
                started.append(one)
                expected.append(one)
    for one in expected:
        one.wait_recv()
    for one in started:
        one.wait_send()


def collect_sums(own, above, slabs, subs):
    chips = subs // 2
    return pl.pallas_call(
        functools.partial(collect_kernel, slabs, subs),
        out_shape=(
            jax.ShapeDtypeStruct((subs,) + own.shape, jnp.float32),
            jax.ShapeDtypeStruct((subs,) + above.shape, jnp.float32),
        ),
        in_specs=[VMEM, VMEM],
        out_specs=(VMEM, VMEM),
        scratch_shapes=[
            pltpu.SemaphoreType.DMA((3,)),
            pltpu.SemaphoreType.DMA((2, chips)),
            pltpu.SemaphoreType.DMA((2, chips)),
            pltpu.SemaphoreType.DMA((2, chips)),
            pltpu.SemaphoreType.DMA((2, chips)),
        ],
        compiler_params=pltpu.CompilerParams(collective_id=2, has_side_effects=True),
        name="collect_sums",
    )(own, above)


def total_kernel(subs, meta, all_own, all_below, out):
    slab, shear = meta[0], jnp.where(meta[0] == 0, meta[2], 0)
    homes = all_own.shape[1] - 1
    slab_leaves = subs * homes

    def one(column, carry):
        device, place = column // homes, lax.rem(column, homes)
        mine = all_own[device, place]
        before = all_own[lax.rem(device + subs - 1, subs), homes]
        total = mine + jnp.where(place == 0, 1.0, 0.0).astype(jnp.float32) * before
        source = lax.rem(column - shear + slab_leaves, slab_leaves)
        device, place = source // homes, lax.rem(source, homes)
        total = total + all_below[device, place + 1]
        nearer = all_below[lax.rem(device + subs - 1, subs), homes + 1]
        later = all_below[lax.rem(device + 1, subs), 0]
        total = total + jnp.where(place == 0, 1.0, 0.0).astype(jnp.float32) * nearer
        total = total + jnp.where(place == homes - 1, 1.0, 0.0).astype(jnp.float32) * later
        start = pl.multiple_of(column * LEAF, LEAF)
        out[:, pl.ds(start, LEAF)] = total[0:5] * mine[5:6]
        return carry

    lax.fori_loop(0, slab_leaves, one, 0)


def total_rates(meta, all_own, all_below, subs):
    homes = all_own.shape[1] - 1
    return pl.pallas_call(
        functools.partial(total_kernel, subs),
        out_shape=jax.ShapeDtypeStruct((5, subs * homes * LEAF), jnp.float32),
        in_specs=[SMEM, VMEM, VMEM],
        out_specs=VMEM,
        name="total_rates",
    )(meta, all_own, all_below)


def shards(slabs, subs, positions, velocity, density, pressure, counts, pair_list):
    slab_leaves = counts.shape[0]
    slots = pair_list.shape[1]
    slab, sub = lax.axis_index("slab"), lax.axis_index("sub")
    row = jnp.pad(pair_list.reshape(-1), (0, LEAF - 3 * slots)).reshape(1, 1, LEAF)
    lists = gather_lists(row, slabs, subs)
    shear, number_tab, offset_tab = pair_tables(lists, slab, slabs, slots, slab_leaves)
    meta = jnp.stack([slab, sub, shear, shear]).astype(jnp.int32)
    own, to_up, to_down, to_second = leaf_windows(
        meta,
        counts,
        positions,
        velocity,
        density.reshape(slab_leaves, LEAF),
        pressure.reshape(slab_leaves, LEAF),
        slabs,
        subs,
    )
    below, above, beyond = swap_windows(to_up, to_down, to_second, slabs)
    own_part, above_part = pair_sums(
        meta, counts, number_tab, offset_tab, (below, own, above, beyond), slabs, subs
    )
    all_own, all_below = collect_sums(own_part, above_part, slabs, subs)
    return total_rates(meta, all_own, all_below, subs)


def solution(mesh):
    placed = (
        P(None, "slab"),
        P(None, "slab"),
        P("slab"),
        P("slab"),
        P("slab"),
        P(None, ("slab", "sub")),
    )
    return jax.shard_map(
        functools.partial(shards, mesh.shape["slab"], mesh.shape["sub"]),
        mesh=mesh,
        in_specs=placed,
        out_specs=P(None, "slab"),
        check_vma=False,
    )
```

```python
import functools
import math

import jax
import jax.numpy as jnp
from jax import lax
from jax.experimental import pallas as pl
from jax.experimental.pallas import tpu as pltpu
from jax.sharding import PartitionSpec as P

LEAF = 128
KINDS = 5
WIN = 12
LEVELS = 4
GAMMA = 5.0 / 3.0
SUPPORT = 1.5
KERNEL_NORM = 21.0 / (2.0 * math.pi * SUPPORT**3)
MOMENT_REG = 0.05
AREA_FLOOR = 0.0001
FAR_AWAY = 1.0e6
DEAD_ABOVE = 1.0e5
TINY = 1.2e-38
BLOCK = 2
MESH = pl.DeviceIdType.MESH
VMEM = pl.BlockSpec(memory_space=pltpu.VMEM)
SMEM = pl.BlockSpec(memory_space=pltpu.SMEM)
HIGHEST = lax.Precision.HIGHEST


def around(value, size):
    return lax.rem(value + size, size)


def table_row(pair_list, slab, slabs, slab_leaves, homes):
    home, other, offset = pair_list[0], pair_list[1], pair_list[2]
    occupied = home >= 0
    crossing = occupied & (home // slab_leaves != other // slab_leaves)
    step = (other - home + offset + 1) & (slab_leaves - 1)
    kind = jnp.where(other == home, 0, jnp.where(crossing, 2 + step, 1))
    key = jnp.where(occupied & (kind < KINDS), (home & (homes - 1)) * KINDS + kind, -1)
    shear = jnp.where(crossing & (slab == slabs - 1), (-offset) & (slab_leaves - 1), 0)
    lane = jnp.arange(LEAF, dtype=jnp.int32)[:, None]
    size = homes * KINDS
    number = jnp.where(key[None] == lane, 1, 0)
    moved = jnp.where(key[None] == lane - size, offset[None], 0)
    shears = jnp.where(lane == 2 * size, shear[None], 0)
    signed = jnp.where((lane >= size) & (lane < 2 * size) & (moved < 0), moved, 0)
    row = jnp.sum(number, axis=1) + jnp.max(moved + shears, axis=1) + jnp.min(signed, axis=1)
    return row.reshape(1, 1, LEAF)


def exchange_kernel(
    slabs,
    subs,
    row_ref,
    counts,
    positions,
    velocity,
    density,
    pressure,
    lists,
    own,
    below,
    above,
    beyond,
    to_up,
    to_down,
    to_second,
    records,
    list_sems,
    window_sems,
):
    slab = lax.axis_index("slab")
    sub = lax.axis_index("sub")
    slab_leaves = counts.shape[0]
    homes = slab_leaves // subs
    barrier = pltpu.get_barrier_semaphore()

    def each_sub(first, body):
        def one(k, carry):
            body(k)
            return carry

        lax.fori_loop(first, subs, one, 0, unroll=4 if first == 0 else 5)

    for shift in (-2, -1, 0, 1, 2):
        peer_slab = (slab + shift + slabs) & (slabs - 1)

        def greet(k, peer_slab=peer_slab):
            pl.semaphore_signal(
                barrier,
                inc=1,
                device_id=(peer_slab, (sub + k) & (subs - 1)),
                device_id_type=MESH,
            )

        each_sub(1 if shift == 0 else 0, greet)

    lane = lax.broadcasted_iota(jnp.int32, (1, LEAF), 1)
    row = lax.broadcasted_iota(jnp.int32, (3, LEAF), 0)

    def record(leaf, carry):
        start = pl.multiple_of(leaf * LEAF, LEAF)
        live = lane < counts[leaf]
        centre = jnp.where(
            row == 0,
            slab.astype(jnp.float32) + 0.5,
            jnp.where(row == 1, leaf.astype(jnp.float32) + 0.5, 0.5),
        )
        place = (positions[:, pl.ds(start, LEAF)] - centre) * (1.0 / SUPPORT)
        records[leaf, 0:3, :] = jnp.where((row > 0) | live, place, FAR_AWAY)
        records[leaf, 3:6, :] = velocity[:, pl.ds(start, LEAF)]
        records[leaf, 6:7, :] = density[pl.ds(leaf, 1), :]
        records[leaf, 7:8, :] = pressure[pl.ds(leaf, 1), :]
        return carry

    lax.fori_loop(0, slab_leaves, record, 0, unroll=4)

    def fill(target, shift):
        first = sub * homes - 2 + shift + 2 * slab_leaves
        for slot in range(WIN):
            target[slot] = records[(first + slot) & (slab_leaves - 1)]

    fill(own, 0)
    pl.semaphore_wait(barrier, 5 * subs - 1)
    mine = pltpu.make_async_copy(
        row_ref, lists.at[pl.ds(2 * subs + sub, 1)], list_sems.at[2]
    )
    mine.start()
    for shift in (-2, 1, -1, 0):
        peer_slab = (slab - shift + slabs) & (slabs - 1)

        def send(k, shift=shift, peer_slab=peer_slab):
            pltpu.make_async_remote_copy(
                src_ref=row_ref,
                dst_ref=lists.at[pl.ds((shift + 2) * subs + sub, 1)],
                send_sem=list_sems.at[0],
                recv_sem=list_sems.at[1],
                device_id=(peer_slab, (sub + k) & (subs - 1)),
                device_id_type=MESH,
            ).start()

        each_sub(1 if shift == 0 else 0, send)
    mine.wait()
    rest = lists.at[pl.ds(0, 4 * subs - 1)]
    everything = pltpu.make_async_remote_copy(
        src_ref=rest,
        dst_ref=rest,
        send_sem=list_sems.at[0],
        recv_sem=list_sems.at[1],
        device_id=((slab + 1) & (slabs - 1), sub),
        device_id_type=MESH,
    )
    everything.wait_recv()
    everything.wait_send()
    shear = jnp.max(
        jnp.where(
            lax.broadcasted_iota(jnp.int32, (4 * subs, 1, LEAF), 2) == 2 * homes * KINDS,
            lists[...],
            0,
        )
    )
    copies = []
    for k, (shift, source, target) in enumerate(
        ((-2, to_second, beyond), (-1, to_down, above), (1, to_up, below))
    ):
        copies.append(
            pltpu.make_async_remote_copy(
                src_ref=source,
                dst_ref=target,
                send_sem=window_sems.at[k],
                recv_sem=window_sems.at[3 + k],
                device_id=((slab + shift + slabs) & (slabs - 1), sub),
                device_id_type=MESH,
            )
        )
    none = jnp.int32(0)
    fill(to_second, jnp.where(slab <= 1, shear, none))
    fill(to_down, jnp.where(slab == 0, shear, none))
    copies[0].start()
    fill(to_up, jnp.where(slab == slabs - 1, -shear, none))
    copies[1].start()
    copies[2].start()
    for one in copies:
        one.wait()


def exchange(row, counts, positions, velocity, density, pressure, slabs, subs):
    window = jax.ShapeDtypeStruct((WIN, 8, LEAF), jnp.float32)
    return pl.pallas_call(
        functools.partial(exchange_kernel, slabs, subs),
        out_shape=(jax.ShapeDtypeStruct((4 * subs, 1, LEAF), jnp.int32),) + (window,) * 4,
        in_specs=[VMEM, SMEM, VMEM, VMEM, VMEM, VMEM],
        out_specs=(VMEM,) * 5,
        scratch_shapes=[pltpu.VMEM((WIN, 8, LEAF), jnp.float32)] * 3
        + [pltpu.VMEM((counts.shape[0], 8, LEAF), jnp.float32)]
        + [pltpu.SemaphoreType.DMA((3,)), pltpu.SemaphoreType.DMA((6,))],
        compiler_params=pltpu.CompilerParams(collective_id=0, has_side_effects=True),
        name="exchange",
    )(row, counts, positions, velocity, density, pressure)


def three_parts(full):
    first = full.astype(jnp.bfloat16).astype(jnp.float32)
    rest = full - first
    second = rest.astype(jnp.bfloat16).astype(jnp.float32)
    return first, second, rest - second


def left_stack(full):
    first, second, third = three_parts(full)
    return jnp.concatenate([first, first, second, second, first, third], axis=0).astype(
        jnp.bfloat16
    )


def right_stack(full):
    first, second, third = three_parts(full)
    return jnp.concatenate([first, second, first, second, third, first], axis=0).astype(
        jnp.bfloat16
    )


def features(entries, scale):
    scaled = scale * entries
    full = jnp.concatenate(
        [
            scaled,
            entries[0:1] * scaled,
            entries[1:2] * scaled,
            entries[2:3] * scaled,
            jnp.full_like(entries, scale),
        ],
        axis=0,
    )
    return jnp.concatenate(three_parts(full), axis=0).astype(jnp.bfloat16)


def moment_rows(sums, entries):
    sums = sums[0:40] + sums[40:80] + sums[80:120]
    plain, total = sums[0:8], sums[32:33]
    parts = []
    for k in range(3):
        own = entries[k : k + 1]
        parts.append(
            sums[8 * k + 8 : 8 * k + 16]
            - own * plain
            - entries * sums[k : k + 1]
            + own * (entries * total)
        )
    parts.append(sums[32:40])
    return KERNEL_NORM * jnp.concatenate(parts, axis=0)


def displaced(entries, row, gap_x, gap_y, gap_v):
    entries = jnp.where(entries > DEAD_ABOVE, -entries, entries)
    return entries + jnp.where(
        row == 0, gap_x, jnp.where(row == 1, gap_y, jnp.where(row == 4, gap_v, 0.0))
    )


def length_sq(entries):
    x, y, z = entries[0:1], entries[1:2], entries[2:3]
    return x * x + y * y + z * z


def weights(dist_sq):
    dist_sq = jnp.maximum(dist_sq, TINY)
    inside = jnp.maximum(1.0 - dist_sq * lax.rsqrt(dist_sq), 0.0)
    square = inside * inside
    return square * square * (5.0 - 4.0 * inside)


def finish(sums, entries):
    live = (entries[0:1] < DEAD_ABOVE).astype(jnp.float32)
    number = sums[24:25] + 1.0 - live
    inverse = 1.0 / number
    area = inverse * SUPPORT**2
    xx = sums[0:1] * area + MOMENT_REG
    xy = sums[1:2] * area
    xz = sums[2:3] * area
    yy = sums[9:10] * area + MOMENT_REG
    yz = sums[10:11] * area
    zz = sums[18:19] * area + MOMENT_REG
    minor_xx = yy * zz - yz * yz
    minor_xy = xz * yz - xy * zz
    minor_xz = xy * yz - xz * yy
    minor_yy = xx * zz - xz * xz
    minor_yz = xy * xz - xx * yz
    minor_zz = xx * yy - xy * xy
    unit = 1.0 / (xx * minor_xx + xy * minor_xy + xz * minor_xz)
    ixx, ixy, ixz = minor_xx * unit, minor_xy * unit, minor_xz * unit
    iyy, iyz, izz = minor_yy * unit, minor_yz * unit, minor_zz * unit
    half = 0.5 * area
    mx, my, mz = sums[0:8] * half, sums[8:16] * half, sums[16:24] * half
    slope_x = ixx * mx + ixy * my + ixz * mz
    slope_y = ixy * mx + iyy * my + iyz * mz
    slope_z = ixz * mx + iyz * my + izz * mz
    scale = (KERNEL_NORM * SUPPORT) * inverse * inverse
    return jnp.concatenate(
        [
            entries,
            slope_x,
            slope_y,
            slope_z,
            ixx * scale,
            ixy * scale,
            ixz * scale,
            iyy * scale,
            iyz * scale,
            izz * scale,
            number,
            number,
        ],
        axis=0,
    )


FLUX_ROWS = (
    tuple(range(8))
    + tuple(8 * k + 11 + q for q in range(5) for k in range(3))
    + tuple(range(32, 38))
)


def flux_terms(near, far, weight):
    d = [far(k) - near(k) for k in range(3)]
    smooth = weights(d[0] * d[0] + d[1] * d[1] + d[2] * d[2])
    mxx, mxy, mxz, myy, myz, mzz = [near(23 + k) + far(23 + k) for k in range(6)]
    area = [
        smooth * (mxx * d[0] + mxy * d[1] + mxz * d[2]),
        smooth * (mxy * d[0] + myy * d[1] + myz * d[2]),
        smooth * (mxz * d[0] + myz * d[1] + mzz * d[2]),
    ]
    area_sq = area[0] * area[0] + area[1] * area[1] + area[2] * area[2]
    root = lax.rsqrt(jnp.maximum(area_sq, TINY))
    size = area_sq * root * weight
    root = jnp.minimum(root, 1.0 / AREA_FLOOR)
    normal = [area[k] * root for k in range(3)]

    def slope(side, q):
        return side(8 + 3 * q) * d[0] + side(9 + 3 * q) * d[1] + side(10 + 3 * q) * d[2]

    left_vel, right_vel, face = [], [], []
    for q in range(3):
        a, b = near(3 + q), far(3 + q)
        face.append(a + b)
        gap = b - a
        high = jnp.abs(gap)
        low = -high
        left_vel.append(jnp.minimum(jnp.maximum(slope(near, q) - gap, low), high))
        right_vel.append(jnp.minimum(jnp.maximum(gap - slope(far, q), low), high))
    states = []
    for q in (3, 4):
        a, b = near(3 + q), far(3 + q)
        low, high = jnp.minimum(a, b), jnp.maximum(a, b)
        states.append(jnp.minimum(jnp.maximum(a + slope(near, q), low), high))
        states.append(jnp.minimum(jnp.maximum(b - slope(far, q), low), high))
    left_rho, right_rho, left_p, right_p = states
    left_un = left_vel[0] * normal[0] + left_vel[1] * normal[1] + left_vel[2] * normal[2]
    right_un = right_vel[0] * normal[0] + right_vel[1] * normal[1] + right_vel[2] * normal[2]
    root_gamma = math.sqrt(GAMMA)
    left_c = root_gamma * left_p * lax.rsqrt(left_p * left_rho)
    right_c = root_gamma * right_p * lax.rsqrt(right_p * right_rho)
    speed_left = jnp.minimum(left_un - left_c, right_un - right_c)
    speed_right = jnp.maximum(left_un + left_c, right_un + right_c)
    left_m = left_rho * (speed_left - left_un)
    right_m = right_rho * (speed_right - right_un)
    top = right_p - left_p + left_m * left_un - right_m * right_un
    bottom = left_m - right_m
    is_left = top <= 0.0

    def pick(left, right):
        return jnp.where(is_left, left, right)

    rho, p, un = pick(left_rho, right_rho), pick(left_p, right_p), pick(left_un, right_un)
    m, c, speed = pick(left_m, right_m), pick(left_c, right_c), pick(speed_left, speed_right)
    wave = pick(jnp.minimum(speed_left, 0.0), jnp.maximum(speed_right, 0.0))
    lab = [pick(left_vel[k], right_vel[k]) + face[k] for k in range(3)]
    lead = speed * bottom - top
    joint = 1.0 / (bottom * lead)
    contact = top * (lead * joint)
    spread = bottom * (bottom * joint)
    push = wave * ((contact - un) * spread)
    mass = (rho * un + wave * (m * spread - rho)) * size
    thrust = (p + push * m) * size
    carried = (1.5 / GAMMA) * (c * c) + 0.5 * (
        lab[0] * lab[0] + lab[1] * lab[1] + lab[2] * lab[2]
    )
    drift = face[0] * normal[0] + face[1] * normal[1] + face[2] * normal[2]
    energy = mass * carried + drift * thrust + size * (p * un + push * (m * contact + p))
    return [mass] + [lab[k] * mass + normal[k] * thrust for k in range(3)] + [energy]


def pair_kernel(
    slabs,
    subs,
    tables,
    counts,
    below,
    own,
    above,
    beyond,
    own_out,
    above_out,
    store,
    finished,
    near_rows,
    far_rows,
    row_sums,
    flux_sums,
):
    slab = lax.axis_index("slab")
    sub = lax.axis_index("sub")
    slab_leaves = counts.shape[0]
    homes = slab_leaves // subs
    table_size = homes * KINDS
    row = lax.broadcasted_iota(jnp.int32, (8, LEAF), 0)
    for level, source in enumerate((below, own, above, beyond)):
        store[pl.ds(level * WIN, WIN)] = source[...]
    flux_sums[...] = jnp.zeros_like(flux_sums)

    def most(k, value):
        return jnp.maximum(value, tables[k, 2 * table_size])

    shear = lax.fori_loop(0, 4 * subs, most, jnp.int32(0))

    def home_facts(level, place):
        shift = jnp.where(
            (level == 0) & (slab == 0),
            -shear,
            jnp.where((level == 2) & (slab == slabs - 1), shear, 0),
        )
        column = (sub * homes + place + shift + 2 * slab_leaves) & (slab_leaves - 1)
        level_slab = (slab - 1 + level + slabs) & (slabs - 1)
        return level, column, level_slab == slabs - 1

    def pair_facts(facts, kind):
        level, column, last = facts
        device = (level + 1) * subs + column // homes
        entry = (column & (homes - 1)) * KINDS + kind
        crossing = kind >= 2
        step = jnp.where(crossing, kind - 3, jnp.where(kind == 1, 1, 0))
        wraps = crossing & last
        other_column = (
            column + step + jnp.where(wraps, shear, 0) + slab_leaves
        ) & (slab_leaves - 1)
        gap_x = jnp.where(crossing, 1.0 / SUPPORT, 0.0).astype(jnp.float32)
        gap_y = (other_column + tables[device, table_size + entry] - column).astype(
            jnp.float32
        ) * (1.0 / SUPPORT)
        gap_v = jnp.where(wraps, -1.0, 0.0).astype(jnp.float32)
        return tables[device, entry], step + jnp.where(crossing, WIN, 0), gap_x, gap_y, gap_v

    own_first, above_first = WIN + 2, 2 * WIN + 1
    halves = jnp.where((row >= 3) & (row < 6), 0.5, 1.0).astype(jnp.float32)

    def finish_one(k, carry):
        level = jnp.where(k <= homes, 1, 2)
        place = jnp.where(k <= homes, k, k - (homes + 2))
        leaf = level * WIN + place + 2
        mine = store[leaf]
        near_sq = length_sq(mine)
        left = jnp.where(
            row < 3, -2.0 * mine, jnp.where(row == 3, 1.0, jnp.where(row == 4, near_sq, 0.0))
        )
        left = jnp.transpose(left_stack(left).astype(jnp.float32)).astype(jnp.bfloat16)
        here = home_facts(level, place)
        pairs = [(here, kind, 1) for kind in range(KINDS)]
        pairs.append((home_facts(level, place - 1), 1, -1))
        pairs += [(home_facts(level - 1, place + 3 - kind), kind, -1) for kind in (2, 3, 4)]
        sums = None
        for facts, kind, sign in pairs:
            number, away, gap_x, gap_y, gap_v = pair_facts(facts, kind)
            theirs = displaced(
                store[leaf + sign * away], row, sign * gap_x, sign * gap_y, sign * gap_v
            )
            right = jnp.where(
                row < 3,
                theirs,
                jnp.where(row == 3, length_sq(theirs), jnp.where(row == 4, 1.0, 0.0)),
            )
            smooth = weights(
                lax.dot_general(
                    left,
                    right_stack(right),
                    (((1,), (0,)), ((), ())),
                    preferred_element_type=jnp.float32,
                )
            )
            high = smooth.astype(jnp.bfloat16)
            low = (smooth - high.astype(jnp.float32)).astype(jnp.bfloat16)
            rows = features(theirs, number.astype(jnp.float32))
            part = lax.dot_general(
                jnp.concatenate([rows, rows], axis=1),
                jnp.concatenate([high, low], axis=1),
                (((1,), (1,)), ((), ())),
                preferred_element_type=jnp.float32,
            )
            sums = part if sums is None else sums + part
        finished[leaf] = finish(moment_rows(sums, mine), mine)
        finished[leaf, 0:8] = mine * halves
        return carry

    lax.fori_loop(0, 2 * homes + 3, finish_one, 0)
    ones = jnp.ones((8, LEAF), jnp.float32)

    def flux_home(place, carry):
        leaf = own_first + place
        facts = home_facts(1, place)
        turned = jnp.transpose(finished[leaf])
        for k, source in enumerate(FLUX_ROWS):
            near_rows[k] = jnp.broadcast_to(turned[:, source : source + 1], (LEAF, LEAF)).reshape(
                LEAF // 8, 8, LEAF
            )
        row_sums[...] = jnp.zeros_like(row_sums)
        steps = (counts[facts[1]] + 8 * BLOCK - 1) // (8 * BLOCK)

        def one(kind, carry):
            number, away, gap_x, gap_y, gap_v = pair_facts(facts, kind)
            other = leaf + away
            scale = number.astype(jnp.float32) * jnp.where(kind == 0, 0.5, 1.0).astype(jnp.float32)

            @pl.when(number > 0)
            def _():
                theirs = finished[other]
                head = displaced(theirs[0:8], row, gap_x, gap_y, 0.5 * gap_v)
                for k, source in enumerate(FLUX_ROWS):
                    part = head if source < 8 else theirs
                    far_rows[k] = jnp.broadcast_to(part[source : source + 1], (8, LEAF))

                def step(group, sums):
                    first = group * BLOCK

                    def near(k):
                        return near_rows[k, pl.ds(first, BLOCK)]

                    def far(k):
                        return far_rows[k][None]

                    terms = flux_terms(near, far, scale)
                    totals = []
                    for k in range(5):
                        row_sums[k, pl.ds(first, BLOCK)] += terms[k]
                        totals.append(sums[k] + jnp.sum(terms[k], axis=0))
                    return tuple(totals)

                empty = jnp.zeros((8, LEAF), jnp.float32)
                sums = lax.fori_loop(0, steps, step, (empty,) * 5)
                added = [jnp.sum(part, axis=0, keepdims=True) for part in sums]
                nothing = jnp.zeros((3, LEAF), jnp.float32)
                flux_sums[other] = flux_sums[other] + jnp.concatenate(added + [nothing], axis=0)

            return carry

        lax.fori_loop(0, KINDS, one, 0)
        taken = []
        for k in range(5):
            total = lax.dot_general(
                ones,
                row_sums[k].reshape(LEAF, LEAF),
                (((1,), (1,)), ((), ())),
                precision=HIGHEST,
                preferred_element_type=jnp.float32,
            )
            taken.append(total[0:1])
        nothing = jnp.zeros((3, LEAF), jnp.float32)
        flux_sums[leaf] = flux_sums[leaf] - jnp.concatenate(taken + [nothing], axis=0)
        return carry

    lax.fori_loop(0, homes, flux_home, 0)
    for k in range(homes + 1):
        own_out[k] = flux_sums[own_first + k]
        own_out[k, 5:6, :] = finished[own_first + k, 38:39, :]
    for k in range(homes + 2):
        above_out[k] = flux_sums[above_first + k]


def pair_sums(tables, counts, windows, slabs, subs):
    homes = counts.shape[0] // subs
    leaves = LEVELS * WIN
    return pl.pallas_call(
        functools.partial(pair_kernel, slabs, subs),
        out_shape=(
            jax.ShapeDtypeStruct((homes + 1, 8, LEAF), jnp.float32),
            jax.ShapeDtypeStruct((homes + 2, 8, LEAF), jnp.float32),
        ),
        in_specs=[SMEM] * 2 + [VMEM] * 4,
        out_specs=(VMEM, VMEM),
        scratch_shapes=[
            pltpu.VMEM((leaves, 8, LEAF), jnp.float32),
            pltpu.VMEM((leaves, 40, LEAF), jnp.float32),
            pltpu.VMEM((len(FLUX_ROWS), LEAF // 8, 8, LEAF), jnp.float32),
            pltpu.VMEM((len(FLUX_ROWS), 8, LEAF), jnp.float32),
            pltpu.VMEM((5, LEAF // 8, 8, LEAF), jnp.float32),
            pltpu.VMEM((leaves, 8, LEAF), jnp.float32),
        ],
        name="pair_sums",
    )(tables, counts, *windows)


def collect_kernel(
    slabs, subs, own, above, all_own, all_below, up_sem, ring_send, ring_recv, core_send, core_recv
):
    slab = lax.axis_index("slab")
    sub = lax.axis_index("sub")
    chips = subs // 2
    chip, core = sub // 2, lax.rem(sub, 2)
    partner = 1 - core
    ahead, behind = around(chip + 1, chips), around(chip - 1, chips)
    right_hops = chips // 2
    left_hops = chips - 1 - right_hops
    barrier = pltpu.get_barrier_semaphore()
    for peer in (
        (around(slab + 1, slabs), sub),
        (around(slab - 1, slabs), sub),
        (slab, 2 * ahead + core),
        (slab, 2 * behind + core),
        (slab, 2 * chip + partner),
    ):
        pl.semaphore_signal(barrier, inc=1, device_id=peer, device_id_type=MESH)
    pl.semaphore_wait(barrier, 5)

    upward = pltpu.make_async_remote_copy(
        src_ref=above,
        dst_ref=all_below.at[sub],
        send_sem=up_sem.at[0],
        recv_sem=up_sem.at[1],
        device_id=(around(slab + 1, slabs), sub),
        device_id_type=MESH,
    )
    upward.start()
    mine = pltpu.make_async_copy(own, all_own.at[sub], up_sem.at[2])
    mine.start()

    def ring(which, source, buffer, owner_chip, hop, to_right):
        slot = 2 * owner_chip + core
        place = (hop - 1) if to_right else (right_hops + hop - 1)
        return pltpu.make_async_remote_copy(
            src_ref=source if source is not None else buffer.at[slot],
            dst_ref=buffer.at[slot],
            send_sem=ring_send.at[which, place],
            recv_sem=ring_recv.at[which, place],
            device_id=(slab, 2 * (ahead if to_right else behind) + core),
            device_id_type=MESH,
        )

    def across(which, source, buffer, owner_chip, place):
        slot = 2 * owner_chip + core
        return pltpu.make_async_remote_copy(
            src_ref=source if source is not None else buffer.at[slot],
            dst_ref=buffer.at[slot],
            send_sem=core_send.at[which, place],
            recv_sem=core_recv.at[which, place],
            device_id=(slab, 2 * chip + partner),
            device_id_type=MESH,
        )

    started, expected = [], []

    def launch(which, source, buffer):
        for to_right, hops in ((True, right_hops), (False, left_hops)):
            if hops > 0:
                one = ring(which, source, buffer, chip, 1, to_right)
                one.start()
                started.append(one)
        one = across(which, source, buffer, chip, 0)
        one.start()
        started.append(one)
        expected.append(one)

    launch(0, own, all_own)
    upward.wait()
    launch(1, None, all_below)
    mine.wait()
    for hop in range(1, right_hops + 1):
        for which, buffer in ((0, all_own), (1, all_below)):
            for to_right, hops in ((True, right_hops), (False, left_hops)):
                if hop > hops:
                    continue
                owner = around(chip - hop, chips) if to_right else around(chip + hop, chips)
                ring(which, None, buffer, owner, hop, to_right).wait_recv()
                if hop < hops:
                    one = ring(which, None, buffer, owner, hop + 1, to_right)
                    one.start()
                    started.append(one)
                place = hop if to_right else right_hops + hop
                one = across(which, None, buffer, owner, place)
                one.start()
                started.append(one)
                expected.append(one)
    for one in expected:
        one.wait_recv()
    for one in started:
        one.wait_send()


def collect_sums(own, above, slabs, subs):
    chips = subs // 2
    return pl.pallas_call(
        functools.partial(collect_kernel, slabs, subs),
        out_shape=(
            jax.ShapeDtypeStruct((subs,) + own.shape, jnp.float32),
            jax.ShapeDtypeStruct((subs,) + above.shape, jnp.float32),
        ),
        in_specs=[VMEM, VMEM],
        out_specs=(VMEM, VMEM),
        scratch_shapes=[
            pltpu.SemaphoreType.DMA((3,)),
            pltpu.SemaphoreType.DMA((2, chips)),
            pltpu.SemaphoreType.DMA((2, chips)),
            pltpu.SemaphoreType.DMA((2, chips)),
            pltpu.SemaphoreType.DMA((2, chips)),
        ],
        compiler_params=pltpu.CompilerParams(collective_id=2, has_side_effects=True),
        name="collect_sums",
    )(own, above)


def total_kernel(subs, tables, all_own, all_below, out):
    homes = all_own.shape[1] - 1
    slab_leaves = subs * homes

    def most(k, value):
        return jnp.maximum(value, tables[k, 2 * homes * KINDS])

    shear = lax.fori_loop(0, 4 * subs, most, jnp.int32(0))
    shear = jnp.where(lax.axis_index("slab") == 0, shear, 0)

    def one(column, carry):
        device, place = column // homes, lax.rem(column, homes)
        mine = all_own[device, place]
        before = all_own[lax.rem(device + subs - 1, subs), homes]
        total = mine + jnp.where(place == 0, 1.0, 0.0).astype(jnp.float32) * before
        source = lax.rem(column - shear + slab_leaves, slab_leaves)
        device, place = source // homes, lax.rem(source, homes)
        total = total + all_below[device, place + 1]
        nearer = all_below[lax.rem(device + subs - 1, subs), homes + 1]
        later = all_below[lax.rem(device + 1, subs), 0]
        total = total + jnp.where(place == 0, 1.0, 0.0).astype(jnp.float32) * nearer
        total = total + jnp.where(place == homes - 1, 1.0, 0.0).astype(jnp.float32) * later
        start = pl.multiple_of(column * LEAF, LEAF)
        out[:, pl.ds(start, LEAF)] = total[0:5] * mine[5:6]
        return carry

    lax.fori_loop(0, slab_leaves, one, 0)


def total_rates(tables, all_own, all_below, subs):
    homes = all_own.shape[1] - 1
    return pl.pallas_call(
        functools.partial(total_kernel, subs),
        out_shape=jax.ShapeDtypeStruct((5, subs * homes * LEAF), jnp.float32),
        in_specs=[SMEM, VMEM, VMEM],
        out_specs=VMEM,
        name="total_rates",
    )(tables, all_own, all_below)


def shards(slabs, subs, positions, velocity, density, pressure, counts, pair_list):
    slab_leaves = counts.shape[0]
    slab = lax.axis_index("slab")
    row = table_row(pair_list, slab, slabs, slab_leaves, slab_leaves // subs)
    tables, own, below, above, beyond = exchange(
        row,
        counts,
        positions,
        velocity,
        density.reshape(slab_leaves, LEAF),
        pressure.reshape(slab_leaves, LEAF),
        slabs,
        subs,
    )
    tables = tables.reshape(4 * subs, LEAF)
    own_part, above_part = pair_sums(tables, counts, (below, own, above, beyond), slabs, subs)
    all_own, all_below = collect_sums(own_part, above_part, slabs, subs)
    return total_rates(tables, all_own, all_below, subs)


def solution(mesh):
    placed = (
        P(None, "slab"),
        P(None, "slab"),
        P("slab"),
        P("slab"),
        P("slab"),
        P(None, ("slab", "sub")),
    )
    return jax.shard_map(
        functools.partial(shards, mesh.shape["slab"], mesh.shape["sub"]),
        mesh=mesh,
        in_specs=placed,
        out_specs=P(None, "slab"),
        check_vma=False,
    )
```

```python
import functools
import math

import jax
import jax.numpy as jnp
from jax import lax
from jax.experimental import pallas as pl
from jax.experimental.pallas import tpu as pltpu
from jax.sharding import PartitionSpec as P

LEAF = 128
KINDS = 5
WIN = 12
LEVELS = 4
GAMMA = 5.0 / 3.0
SUPPORT = 1.5
KERNEL_NORM = 21.0 / (2.0 * math.pi * SUPPORT**3)
MOMENT_REG = 0.05
AREA_FLOOR = 0.0001
FAR_AWAY = 1.0e6
DEAD_ABOVE = 1.0e5
TINY = 1.2e-38
BLOCK = 2
MESH = pl.DeviceIdType.MESH
VMEM = pl.BlockSpec(memory_space=pltpu.VMEM)
SMEM = pl.BlockSpec(memory_space=pltpu.SMEM)
HIGHEST = lax.Precision.HIGHEST


def around(value, size):
    return lax.rem(value + size, size)


def table_row(pair_list, slab, slabs, slab_leaves, homes):
    home, other, offset = pair_list[0], pair_list[1], pair_list[2]
    occupied = home >= 0
    crossing = occupied & (home // slab_leaves != other // slab_leaves)
    step = (other - home + offset + 1) & (slab_leaves - 1)
    kind = jnp.where(other == home, 0, jnp.where(crossing, 2 + step, 1))
    key = jnp.where(occupied & (kind < KINDS), (home & (homes - 1)) * KINDS + kind, -1)
    shear = jnp.where(crossing & (slab == slabs - 1), (-offset) & (slab_leaves - 1), 0)
    lane = jnp.arange(LEAF, dtype=jnp.int32)[:, None]
    size = homes * KINDS
    number = jnp.where(key[None] == lane, 1, 0)
    moved = jnp.where(key[None] == lane - size, offset[None], 0)
    shears = jnp.where(lane == 2 * size, shear[None], 0)
    signed = jnp.where((lane >= size) & (lane < 2 * size) & (moved < 0), moved, 0)
    row = jnp.sum(number, axis=1) + jnp.max(moved + shears, axis=1) + jnp.min(signed, axis=1)
    return row.reshape(1, 1, LEAF)


def exchange_kernel(
    slabs,
    subs,
    row_ref,
    counts,
    positions,
    velocity,
    density,
    pressure,
    lists,
    own,
    below,
    above,
    beyond,
    to_up,
    to_down,
    to_second,
    records,
    list_sems,
    window_sems,
):
    slab = lax.axis_index("slab")
    sub = lax.axis_index("sub")
    slab_leaves = counts.shape[0]
    homes = slab_leaves // subs
    barrier = pltpu.get_barrier_semaphore()

    def each_sub(first, body):
        def one(k, carry):
            body(k)
            return carry

        lax.fori_loop(first, subs, one, 0, unroll=4 if first == 0 else 5)

    for shift in (-2, -1, 0, 1, 2):
        peer_slab = (slab + shift + slabs) & (slabs - 1)

        def greet(k, peer_slab=peer_slab):
            pl.semaphore_signal(
                barrier,
                inc=1,
                device_id=(peer_slab, (sub + k) & (subs - 1)),
                device_id_type=MESH,
            )

        each_sub(1 if shift == 0 else 0, greet)

    lane = lax.broadcasted_iota(jnp.int32, (1, LEAF), 1)
    row = lax.broadcasted_iota(jnp.int32, (3, LEAF), 0)

    def record(leaf, carry):
        start = pl.multiple_of(leaf * LEAF, LEAF)
        live = lane < counts[leaf]
        centre = jnp.where(
            row == 0,
            slab.astype(jnp.float32) + 0.5,
            jnp.where(row == 1, leaf.astype(jnp.float32) + 0.5, 0.5),
        )
        place = (positions[:, pl.ds(start, LEAF)] - centre) * (1.0 / SUPPORT)
        records[leaf, 0:3, :] = jnp.where((row > 0) | live, place, FAR_AWAY)
        records[leaf, 3:6, :] = velocity[:, pl.ds(start, LEAF)]
        records[leaf, 6:7, :] = density[pl.ds(leaf, 1), :]
        records[leaf, 7:8, :] = pressure[pl.ds(leaf, 1), :]
        return carry

    lax.fori_loop(0, slab_leaves, record, 0, unroll=4)

    def fill(target, shift):
        first = sub * homes - 2 + shift + 2 * slab_leaves
        for slot in range(WIN):
            target[slot] = records[(first + slot) & (slab_leaves - 1)]

    fill(own, 0)
    pl.semaphore_wait(barrier, 5 * subs - 1)
    mine = pltpu.make_async_copy(
        row_ref, lists.at[pl.ds(2 * subs + sub, 1)], list_sems.at[2]
    )
    mine.start()
    for shift in (-2, 1, -1, 0):
        peer_slab = (slab - shift + slabs) & (slabs - 1)

        def send(k, shift=shift, peer_slab=peer_slab):
            pltpu.make_async_remote_copy(
                src_ref=row_ref,
                dst_ref=lists.at[pl.ds((shift + 2) * subs + sub, 1)],
                send_sem=list_sems.at[0],
                recv_sem=list_sems.at[1],
                device_id=(peer_slab, (sub + k) & (subs - 1)),
                device_id_type=MESH,
            ).start()

        each_sub(1 if shift == 0 else 0, send)
    mine.wait()
    rest = lists.at[pl.ds(0, 4 * subs - 1)]
    everything = pltpu.make_async_remote_copy(
        src_ref=rest,
        dst_ref=rest,
        send_sem=list_sems.at[0],
        recv_sem=list_sems.at[1],
        device_id=((slab + 1) & (slabs - 1), sub),
        device_id_type=MESH,
    )
    everything.wait_recv()
    everything.wait_send()
    shear = jnp.max(
        jnp.where(
            lax.broadcasted_iota(jnp.int32, (4 * subs, 1, LEAF), 2) == 2 * homes * KINDS,
            lists[...],
            0,
        )
    )
    copies = []
    for k, (shift, source, target) in enumerate(
        ((-2, to_second, beyond), (-1, to_down, above), (1, to_up, below))
    ):
        copies.append(
            pltpu.make_async_remote_copy(
                src_ref=source,
                dst_ref=target,
                send_sem=window_sems.at[k],
                recv_sem=window_sems.at[3 + k],
                device_id=((slab + shift + slabs) & (slabs - 1), sub),
                device_id_type=MESH,
            )
        )
    none = jnp.int32(0)
    fill(to_second, jnp.where(slab <= 1, shear, none))
    fill(to_down, jnp.where(slab == 0, shear, none))
    copies[0].start()
    fill(to_up, jnp.where(slab == slabs - 1, -shear, none))
    copies[1].start()
    copies[2].start()
    for one in copies:
        one.wait()


def exchange(row, counts, positions, velocity, density, pressure, slabs, subs):
    window = jax.ShapeDtypeStruct((WIN, 8, LEAF), jnp.float32)
    return pl.pallas_call(
        functools.partial(exchange_kernel, slabs, subs),
        out_shape=(jax.ShapeDtypeStruct((4 * subs, 1, LEAF), jnp.int32),) + (window,) * 4,
        in_specs=[VMEM, SMEM, VMEM, VMEM, VMEM, VMEM],
        out_specs=(VMEM,) * 5,
        scratch_shapes=[pltpu.VMEM((WIN, 8, LEAF), jnp.float32)] * 3
        + [pltpu.VMEM((counts.shape[0], 8, LEAF), jnp.float32)]
        + [pltpu.SemaphoreType.DMA((3,)), pltpu.SemaphoreType.DMA((6,))],
        compiler_params=pltpu.CompilerParams(collective_id=0, has_side_effects=True),
        name="exchange",
    )(row, counts, positions, velocity, density, pressure)


def three_parts(full):
    first = full.astype(jnp.bfloat16).astype(jnp.float32)
    rest = full - first
    second = rest.astype(jnp.bfloat16).astype(jnp.float32)
    return first, second, rest - second


def left_stack(full):
    first, second, third = three_parts(full)
    return jnp.concatenate([first, first, second, second, first, third], axis=0).astype(
        jnp.bfloat16
    )


def right_stack(full):
    first, second, third = three_parts(full)
    return jnp.concatenate([first, second, first, second, third, first], axis=0).astype(
        jnp.bfloat16
    )


def features(entries, scale):
    scaled = scale * entries
    full = jnp.concatenate(
        [
            scaled,
            entries[0:1] * scaled,
            entries[1:2] * scaled,
            entries[2:3] * scaled,
            jnp.full_like(entries, scale),
        ],
        axis=0,
    )
    return jnp.concatenate(three_parts(full), axis=0).astype(jnp.bfloat16)


def moment_rows(sums, entries):
    sums = sums[0:40] + sums[40:80] + sums[80:120]
    plain, total = sums[0:8], sums[32:33]
    parts = []
    for k in range(3):
        own = entries[k : k + 1]
        parts.append(
            sums[8 * k + 8 : 8 * k + 16]
            - own * plain
            - entries * sums[k : k + 1]
            + own * (entries * total)
        )
    parts.append(sums[32:40])
    return KERNEL_NORM * jnp.concatenate(parts, axis=0)


def displaced(entries, row, gap_x, gap_y, gap_v):
    entries = jnp.where(entries > DEAD_ABOVE, -entries, entries)
    return entries + jnp.where(
        row == 0, gap_x, jnp.where(row == 1, gap_y, jnp.where(row == 4, gap_v, 0.0))
    )


def length_sq(entries):
    x, y, z = entries[0:1], entries[1:2], entries[2:3]
    return x * x + y * y + z * z


def weights(dist_sq):
    dist_sq = jnp.maximum(dist_sq, TINY)
    inside = jnp.maximum(1.0 - dist_sq * lax.rsqrt(dist_sq), 0.0)
    square = inside * inside
    return square * square * (5.0 - 4.0 * inside)


def finish(sums, entries):
    live = (entries[0:1] < DEAD_ABOVE).astype(jnp.float32)
    number = sums[24:25] + 1.0 - live
    inverse = 1.0 / number
    area = inverse * SUPPORT**2
    xx = sums[0:1] * area + MOMENT_REG
    xy = sums[1:2] * area
    xz = sums[2:3] * area
    yy = sums[9:10] * area + MOMENT_REG
    yz = sums[10:11] * area
    zz = sums[18:19] * area + MOMENT_REG
    minor_xx = yy * zz - yz * yz
    minor_xy = xz * yz - xy * zz
    minor_xz = xy * yz - xz * yy
    minor_yy = xx * zz - xz * xz
    minor_yz = xy * xz - xx * yz
    minor_zz = xx * yy - xy * xy
    unit = 1.0 / (xx * minor_xx + xy * minor_xy + xz * minor_xz)
    ixx, ixy, ixz = minor_xx * unit, minor_xy * unit, minor_xz * unit
    iyy, iyz, izz = minor_yy * unit, minor_yz * unit, minor_zz * unit
    half = 0.5 * area
    mx, my, mz = sums[0:8] * half, sums[8:16] * half, sums[16:24] * half
    slope_x = ixx * mx + ixy * my + ixz * mz
    slope_y = ixy * mx + iyy * my + iyz * mz
    slope_z = ixz * mx + iyz * my + izz * mz
    scale = (KERNEL_NORM * SUPPORT) * inverse * inverse
    inverse_rows = [k * scale for k in (ixx, ixy, ixz, iyy, iyz, izz)]
    return number, (slope_x, slope_y, slope_z), inverse_rows


def flux_base(entries, row, last):
    return jnp.where(row < 6, entries, jnp.where(row == 6, 1.0, last))


def flux_coefficients(entries, slopes, inverse_rows, row):
    x, y, z = entries[0:1], entries[1:2], entries[2:3]
    constant = entries - slopes[0] * x - slopes[1] * y - slopes[2] * z
    planes = []
    for q in range(5):
        at = slice(3 + q, 4 + q)
        plane = jnp.where(
            row == 0,
            slopes[0][at],
            jnp.where(
                row == 1,
                slopes[1][at],
                jnp.where(row == 2, slopes[2][at], jnp.where(row == 6, constant[at], 0.0)),
            ),
        )
        if q < 3:
            plane = jnp.where(row == 3 + q, -1.0, plane)
        planes.append(plane)
    ixx, ixy, ixz, iyy, iyz, izz = inverse_rows
    for a, b, c in ((ixx, ixy, ixz), (ixy, iyy, iyz), (ixz, iyz, izz)):
        rest = -(a * x + b * y + c * z)
        planes.append(
            jnp.where(
                row == 0,
                a,
                jnp.where(row == 1, b, jnp.where(row == 2, c, jnp.where(row == 6, rest, 0.0))),
            )
        )
    return planes


PLANES = 14


def flux_terms(plane, near, far, weight):
    smooth = weights(plane(13))
    area = [smooth * plane(10 + k) for k in range(3)]
    area_sq = area[0] * area[0] + area[1] * area[1] + area[2] * area[2]
    root = lax.rsqrt(jnp.maximum(area_sq, TINY))
    size = area_sq * root * weight
    root = jnp.minimum(root, 1.0 / AREA_FLOOR)
    normal = [area[k] * root for k in range(3)]
    left_vel, right_vel, face = [], [], []
    for q in range(3):
        a, b = near(q), far(q)
        face.append(a + b)
        high = jnp.abs(b - a)
        low = -high
        left_vel.append(jnp.minimum(jnp.maximum(plane(q), low), high))
        right_vel.append(jnp.minimum(jnp.maximum(plane(5 + q), low), high))
    states = []
    for q in (3, 4):
        a, b = near(q), far(q)
        low, high = jnp.minimum(a, b), jnp.maximum(a, b)
        states.append(jnp.minimum(jnp.maximum(plane(q), low), high))
        states.append(jnp.minimum(jnp.maximum(plane(5 + q), low), high))
    left_rho, right_rho, left_p, right_p = states
    left_un = left_vel[0] * normal[0] + left_vel[1] * normal[1] + left_vel[2] * normal[2]
    right_un = right_vel[0] * normal[0] + right_vel[1] * normal[1] + right_vel[2] * normal[2]
    root_gamma = math.sqrt(GAMMA)
    left_c = root_gamma * left_p * lax.rsqrt(left_p * left_rho)
    right_c = root_gamma * right_p * lax.rsqrt(right_p * right_rho)
    speed_left = jnp.minimum(left_un - left_c, right_un - right_c)
    speed_right = jnp.maximum(left_un + left_c, right_un + right_c)
    left_m = left_rho * (speed_left - left_un)
    right_m = right_rho * (speed_right - right_un)
    top = right_p - left_p + left_m * left_un - right_m * right_un
    bottom = left_m - right_m
    is_left = top <= 0.0

    def pick(left, right):
        return jnp.where(is_left, left, right)

    rho, p, un = pick(left_rho, right_rho), pick(left_p, right_p), pick(left_un, right_un)
    m, c, speed = pick(left_m, right_m), pick(left_c, right_c), pick(speed_left, speed_right)
    wave = pick(jnp.minimum(speed_left, 0.0), jnp.maximum(speed_right, 0.0))
    lab = [pick(left_vel[k], right_vel[k]) + face[k] for k in range(3)]
    lead = speed * bottom - top
    joint = 1.0 / (bottom * lead)
    contact = top * (lead * joint)
    spread = bottom * (bottom * joint)
    push = wave * ((contact - un) * spread)
    mass = (rho * un + wave * (m * spread - rho)) * size
    thrust = (p + push * m) * size
    carried = (1.5 / GAMMA) * (c * c) + 0.5 * (
        lab[0] * lab[0] + lab[1] * lab[1] + lab[2] * lab[2]
    )
    drift = face[0] * normal[0] + face[1] * normal[1] + face[2] * normal[2]
    energy = mass * carried + drift * thrust + size * (p * un + push * (m * contact + p))
    return [mass] + [lab[k] * mass + normal[k] * thrust for k in range(3)] + [energy]


def pair_kernel(
    slabs,
    subs,
    tables,
    counts,
    below,
    own,
    above,
    beyond,
    own_out,
    above_out,
    store,
    numbers,
    coefficients,
    right_parts,
    left_parts,
    near_rows,
    far_rows,
    planes_one,
    planes_two,
    row_sums,
    flux_sums,
    tiles,
):
    slab = lax.axis_index("slab")
    sub = lax.axis_index("sub")
    slab_leaves = counts.shape[0]
    homes = slab_leaves // subs
    table_size = homes * KINDS
    row = lax.broadcasted_iota(jnp.int32, (8, LEAF), 0)
    for level, source in enumerate((below, own, above, beyond)):
        store[pl.ds(level * WIN, WIN)] = source[...]
    flux_sums[...] = jnp.zeros_like(flux_sums)

    def most(k, value):
        return jnp.maximum(value, tables[k, 2 * table_size])

    shear = lax.fori_loop(0, 4 * subs, most, jnp.int32(0))

    def home_facts(level, place):
        shift = jnp.where(
            (level == 0) & (slab == 0),
            -shear,
            jnp.where((level == 2) & (slab == slabs - 1), shear, 0),
        )
        column = (sub * homes + place + shift + 2 * slab_leaves) & (slab_leaves - 1)
        level_slab = (slab - 1 + level + slabs) & (slabs - 1)
        return level, column, level_slab == slabs - 1

    def pair_facts(facts, kind):
        level, column, last = facts
        device = (level + 1) * subs + column // homes
        entry = (column & (homes - 1)) * KINDS + kind
        crossing = kind >= 2
        step = jnp.where(crossing, kind - 3, jnp.where(kind == 1, 1, 0))
        wraps = crossing & last
        other_column = (
            column + step + jnp.where(wraps, shear, 0) + slab_leaves
        ) & (slab_leaves - 1)
        gap_x = jnp.where(crossing, 1.0 / SUPPORT, 0.0).astype(jnp.float32)
        gap_y = (other_column + tables[device, table_size + entry] - column).astype(
            jnp.float32
        ) * (1.0 / SUPPORT)
        gap_v = jnp.where(wraps, -1.0, 0.0).astype(jnp.float32)
        return tables[device, entry], step + jnp.where(crossing, WIN, 0), gap_x, gap_y, gap_v

    own_first, above_first = WIN + 2, 2 * WIN + 1
    halves = jnp.where((row >= 3) & (row < 6), 0.5, 1.0).astype(jnp.float32)

    def finish_one(k, carry):
        level = jnp.where(k <= homes, 1, 2)
        place = jnp.where(k <= homes, k, k - (homes + 2))
        leaf = level * WIN + place + 2
        mine = store[leaf]
        near_sq = length_sq(mine)
        left = jnp.where(
            row < 3, -2.0 * mine, jnp.where(row == 3, 1.0, jnp.where(row == 4, near_sq, 0.0))
        )
        left = jnp.transpose(left_stack(left).astype(jnp.float32)).astype(jnp.bfloat16)
        here = home_facts(level, place)
        pairs = [(here, kind, 1) for kind in range(KINDS)]
        pairs.append((home_facts(level, place - 1), 1, -1))
        pairs += [(home_facts(level - 1, place + 3 - kind), kind, -1) for kind in (2, 3, 4)]
        sums = None
        for facts, kind, sign in pairs:
            number, away, gap_x, gap_y, gap_v = pair_facts(facts, kind)
            theirs = displaced(
                store[leaf + sign * away], row, sign * gap_x, sign * gap_y, sign * gap_v
            )
            right = jnp.where(
                row < 3,
                theirs,
                jnp.where(row == 3, length_sq(theirs), jnp.where(row == 4, 1.0, 0.0)),
            )
            smooth = weights(
                lax.dot_general(
                    left,
                    right_stack(right),
                    (((1,), (0,)), ((), ())),
                    preferred_element_type=jnp.float32,
                )
            )
            high = smooth.astype(jnp.bfloat16)
            low = (smooth - high.astype(jnp.float32)).astype(jnp.bfloat16)
            rows = features(theirs, number.astype(jnp.float32))
            part = lax.dot_general(
                jnp.concatenate([rows, rows], axis=1),
                jnp.concatenate([high, low], axis=1),
                (((1,), (1,)), ((), ())),
                preferred_element_type=jnp.float32,
            )
            sums = part if sums is None else sums + part
        number, slopes, inverse_rows = finish(moment_rows(sums, mine), mine)
        halved = mine * halves
        numbers[leaf] = jnp.broadcast_to(number, (8, LEAF))
        pad = jnp.zeros((16, LEAF), jnp.bfloat16)
        for k, plane in enumerate(flux_coefficients(halved, slopes, inverse_rows, row)):
            coefficients[leaf, k] = plane
            part = right_stack(plane if k < 5 else -plane)
            right_parts[leaf, k] = jnp.concatenate([part, pad], axis=0)
        return carry

    lax.fori_loop(0, 2 * homes + 3, finish_one, 0)

    blank = jnp.zeros((LEAF, LEAF), jnp.float32)

    def turned_left(full, first):
        stack = left_stack(full).astype(jnp.float32)
        parts = ([blank[:first]] if first else []) + [stack, blank[: LEAF - 48 - first]]
        return jnp.transpose(jnp.concatenate(parts, axis=0)).astype(jnp.bfloat16)

    def prepare_home(place, carry):
        leaf = own_first + place
        mine = store[leaf] * halves
        for k in range(8):
            left_parts[place, k] = turned_left(coefficients[leaf, k], 0)
        distance = jnp.where(
            row < 3,
            -2.0 * mine,
            jnp.where(row < 6, 0.0, jnp.where(row == 6, length_sq(mine), 1.0)),
        )
        left_parts[place, 8] = turned_left(distance, 0)
        turned = jnp.transpose(mine)
        for k in range(5):
            near_rows[place, k] = jnp.broadcast_to(
                turned[:, 3 + k : 4 + k], (LEAF, LEAF)
            ).reshape(LEAF // 8, 8, LEAF)
        row_sums[place] = jnp.zeros((5, LEAF // 8, 8, LEAF), jnp.float32)
        return carry

    lax.fori_loop(0, homes, prepare_home, 0)

    own_row = 2 * subs + sub

    def clear(k, carry):
        tiles[k] = 0
        return carry

    lax.fori_loop(0, table_size + 8, clear, 0)

    def list_tile(entry, filled):
        tiles[filled] = entry
        return filled + jnp.where(tables[own_row, entry] > 0, 1, 0)

    filled = lax.fori_loop(0, table_size, list_tile, jnp.int32(0))

    def tile_facts(index):
        entry = tiles[index]
        place = entry // KINDS
        kind = entry - place * KINDS
        number, away, gap_x, gap_y, gap_v = pair_facts(home_facts(1, place), kind)
        number = jnp.where(index < filled, number, 0).astype(jnp.float32)
        scale = number * jnp.where(kind == 0, 0.5, 1.0).astype(jnp.float32)
        leaf = own_first + place
        return place, leaf, leaf + away, gap_x, gap_y, 0.5 * gap_v, scale

    def lay_planes(index, planes):
        place, leaf, other, gap_x, gap_y, gap_v, _ = tile_facts(index)
        theirs = displaced(store[other] * halves, row, gap_x, gap_y, gap_v)
        base = right_stack(flux_base(theirs, row, length_sq(theirs)))
        base = jnp.concatenate([base, jnp.zeros((16, LEAF), jnp.bfloat16)], axis=0)
        mine = store[leaf] * halves - jnp.where(
            row == 0, gap_x, jnp.where(row == 1, gap_y, jnp.where(row == 4, gap_v, 0.0))
        )
        mine = turned_left(flux_base(mine, row, 0.0), 64)
        for k in range(8):
            right = jnp.concatenate([base, right_parts[other, k]], axis=0)
            left = left_parts[place, k]
            if k < 5:
                parts = [left, mine] + ([left_parts[place, 8]] if k == 0 else [])
                targets = [k, 5 + k] + ([13] if k == 0 else [])
            else:
                parts = [left + mine]
                targets = [5 + k]
            for part, target in zip(parts, targets):
                planes[target] = lax.dot_general(
                    part,
                    right,
                    (((1,), (0,)), ((), ())),
                    preferred_element_type=jnp.float32,
                ).reshape(LEAF // 8, 8, LEAF)

    def add_fluxes(index, planes, far_rows):
        place, _, other, gap_x, gap_y, gap_v, scale = tile_facts(index)
        theirs = displaced(store[other] * halves, row, gap_x, gap_y, gap_v)
        for k in range(5):
            far_rows[k] = jnp.broadcast_to(theirs[3 + k : 4 + k], (8, LEAF))
        totals = [None] * 5
        for first in range(0, LEAF // 8, BLOCK):
            terms = flux_terms(
                lambda k: planes[k, first : first + BLOCK],
                lambda k: near_rows[place, k, first : first + BLOCK],
                lambda k: far_rows[k][None],
                scale,
            )
            for k in range(5):
                row_sums[place, k, first : first + BLOCK] += terms[k]
                part = jnp.sum(terms[k], axis=0)
                totals[k] = part if totals[k] is None else totals[k] + part
        added = [jnp.sum(part, axis=0, keepdims=True) for part in totals]
        nothing = jnp.zeros((3, LEAF), jnp.float32)
        flux_sums[other] = flux_sums[other] + jnp.concatenate(added + [nothing], axis=0)

    lay_planes(0, planes_one)

    def two_tiles(step, carry):
        lay_planes(2 * step + 1, planes_two)
        add_fluxes(2 * step, planes_one, far_rows.at[0])
        lay_planes(2 * step + 2, planes_one)
        add_fluxes(2 * step + 1, planes_two, far_rows.at[1])
        return carry

    lax.fori_loop(0, (filled + 1) // 2, two_tiles, 0)
    ones = jnp.ones((8, LEAF), jnp.float32)

    def close_home(place, carry):
        taken = []
        for k in range(5):
            total = lax.dot_general(
                ones,
                row_sums[place, k].reshape(LEAF, LEAF),
                (((1,), (1,)), ((), ())),
                precision=HIGHEST,
                preferred_element_type=jnp.float32,
            )
            taken.append(total[0:1])
        nothing = jnp.zeros((3, LEAF), jnp.float32)
        leaf = own_first + place
        flux_sums[leaf] = flux_sums[leaf] - jnp.concatenate(taken + [nothing], axis=0)
        return carry

    lax.fori_loop(0, homes, close_home, 0)
    for k in range(homes + 1):
        own_out[k] = flux_sums[own_first + k]
        own_out[k, 5:6, :] = numbers[own_first + k, 0:1, :]
    for k in range(homes + 2):
        above_out[k] = flux_sums[above_first + k]


def pair_sums(tables, counts, windows, slabs, subs):
    homes = counts.shape[0] // subs
    leaves = LEVELS * WIN
    return pl.pallas_call(
        functools.partial(pair_kernel, slabs, subs),
        out_shape=(
            jax.ShapeDtypeStruct((homes + 1, 8, LEAF), jnp.float32),
            jax.ShapeDtypeStruct((homes + 2, 8, LEAF), jnp.float32),
        ),
        in_specs=[SMEM] * 2 + [VMEM] * 4,
        out_specs=(VMEM, VMEM),
        scratch_shapes=[
            pltpu.VMEM((leaves, 8, LEAF), jnp.float32),
            pltpu.VMEM((leaves, 8, LEAF), jnp.float32),
            pltpu.VMEM((leaves, 8, 8, LEAF), jnp.float32),
            pltpu.VMEM((leaves, 8, 64, LEAF), jnp.bfloat16),
            pltpu.VMEM((homes, 9, LEAF, LEAF), jnp.bfloat16),
            pltpu.VMEM((homes, 5, LEAF // 8, 8, LEAF), jnp.float32),
            pltpu.VMEM((2, 5, 8, LEAF), jnp.float32),
            pltpu.VMEM((PLANES, LEAF // 8, 8, LEAF), jnp.float32),
            pltpu.VMEM((PLANES, LEAF // 8, 8, LEAF), jnp.float32),
            pltpu.VMEM((homes, 5, LEAF // 8, 8, LEAF), jnp.float32),
            pltpu.VMEM((leaves, 8, LEAF), jnp.float32),
            pltpu.SMEM((homes * KINDS + 8,), jnp.int32),
        ],
        name="pair_sums",
    )(tables, counts, *windows)


def collect_kernel(
    slabs, subs, own, above, all_own, all_below, up_sem, ring_send, ring_recv, core_send, core_recv
):
    slab = lax.axis_index("slab")
    sub = lax.axis_index("sub")
    chips = subs // 2
    chip, core = sub // 2, lax.rem(sub, 2)
    partner = 1 - core
    ahead, behind = around(chip + 1, chips), around(chip - 1, chips)
    right_hops = chips // 2
    left_hops = chips - 1 - right_hops
    barrier = pltpu.get_barrier_semaphore()
    for peer in (
        (around(slab + 1, slabs), sub),
        (around(slab - 1, slabs), sub),
        (slab, 2 * ahead + core),
        (slab, 2 * behind + core),
        (slab, 2 * chip + partner),
    ):
        pl.semaphore_signal(barrier, inc=1, device_id=peer, device_id_type=MESH)
    pl.semaphore_wait(barrier, 5)

    upward = pltpu.make_async_remote_copy(
        src_ref=above,
        dst_ref=all_below.at[sub],
        send_sem=up_sem.at[0],
        recv_sem=up_sem.at[1],
        device_id=(around(slab + 1, slabs), sub),
        device_id_type=MESH,
    )
    upward.start()
    mine = pltpu.make_async_copy(own, all_own.at[sub], up_sem.at[2])
    mine.start()

    def ring(which, source, buffer, owner_chip, hop, to_right):
        slot = 2 * owner_chip + core
        place = (hop - 1) if to_right else (right_hops + hop - 1)
        return pltpu.make_async_remote_copy(
            src_ref=source if source is not None else buffer.at[slot],
            dst_ref=buffer.at[slot],
            send_sem=ring_send.at[which, place],
            recv_sem=ring_recv.at[which, place],
            device_id=(slab, 2 * (ahead if to_right else behind) + core),
            device_id_type=MESH,
        )

    def across(which, source, buffer, owner_chip, place):
        slot = 2 * owner_chip + core
        return pltpu.make_async_remote_copy(
            src_ref=source if source is not None else buffer.at[slot],
            dst_ref=buffer.at[slot],
            send_sem=core_send.at[which, place],
            recv_sem=core_recv.at[which, place],
            device_id=(slab, 2 * chip + partner),
            device_id_type=MESH,
        )

    started, expected = [], []

    def launch(which, source, buffer):
        for to_right, hops in ((True, right_hops), (False, left_hops)):
            if hops > 0:
                one = ring(which, source, buffer, chip, 1, to_right)
                one.start()
                started.append(one)
        one = across(which, source, buffer, chip, 0)
        one.start()
        started.append(one)
        expected.append(one)

    launch(0, own, all_own)
    upward.wait()
    launch(1, None, all_below)
    mine.wait()
    for hop in range(1, right_hops + 1):
        for which, buffer in ((0, all_own), (1, all_below)):
            for to_right, hops in ((True, right_hops), (False, left_hops)):
                if hop > hops:
                    continue
                owner = around(chip - hop, chips) if to_right else around(chip + hop, chips)
                ring(which, None, buffer, owner, hop, to_right).wait_recv()
                if hop < hops:
                    one = ring(which, None, buffer, owner, hop + 1, to_right)
                    one.start()
                    started.append(one)
                place = hop if to_right else right_hops + hop
                one = across(which, None, buffer, owner, place)
                one.start()
                started.append(one)
                expected.append(one)
    for one in expected:
        one.wait_recv()
    for one in started:
        one.wait_send()


def collect_sums(own, above, slabs, subs):
    chips = subs // 2
    return pl.pallas_call(
        functools.partial(collect_kernel, slabs, subs),
        out_shape=(
            jax.ShapeDtypeStruct((subs,) + own.shape, jnp.float32),
            jax.ShapeDtypeStruct((subs,) + above.shape, jnp.float32),
        ),
        in_specs=[VMEM, VMEM],
        out_specs=(VMEM, VMEM),
        scratch_shapes=[
            pltpu.SemaphoreType.DMA((3,)),
            pltpu.SemaphoreType.DMA((2, chips)),
            pltpu.SemaphoreType.DMA((2, chips)),
            pltpu.SemaphoreType.DMA((2, chips)),
            pltpu.SemaphoreType.DMA((2, chips)),
        ],
        compiler_params=pltpu.CompilerParams(collective_id=2, has_side_effects=True),
        name="collect_sums",
    )(own, above)


def total_kernel(subs, tables, all_own, all_below, out):
    homes = all_own.shape[1] - 1
    slab_leaves = subs * homes

    def most(k, value):
        return jnp.maximum(value, tables[k, 2 * homes * KINDS])

    shear = lax.fori_loop(0, 4 * subs, most, jnp.int32(0))
    shear = jnp.where(lax.axis_index("slab") == 0, shear, 0)

    def one(column, carry):
        device, place = column // homes, lax.rem(column, homes)
        mine = all_own[device, place]
        before = all_own[lax.rem(device + subs - 1, subs), homes]
        total = mine + jnp.where(place == 0, 1.0, 0.0).astype(jnp.float32) * before
        source = lax.rem(column - shear + slab_leaves, slab_leaves)
        device, place = source // homes, lax.rem(source, homes)
        total = total + all_below[device, place + 1]
        nearer = all_below[lax.rem(device + subs - 1, subs), homes + 1]
        later = all_below[lax.rem(device + 1, subs), 0]
        total = total + jnp.where(place == 0, 1.0, 0.0).astype(jnp.float32) * nearer
        total = total + jnp.where(place == homes - 1, 1.0, 0.0).astype(jnp.float32) * later
        start = pl.multiple_of(column * LEAF, LEAF)
        out[:, pl.ds(start, LEAF)] = total[0:5] * mine[5:6]
        return carry

    lax.fori_loop(0, slab_leaves, one, 0, unroll=8)


def total_rates(tables, all_own, all_below, subs):
    homes = all_own.shape[1] - 1
    return pl.pallas_call(
        functools.partial(total_kernel, subs),
        out_shape=jax.ShapeDtypeStruct((5, subs * homes * LEAF), jnp.float32),
        in_specs=[SMEM, VMEM, VMEM],
        out_specs=VMEM,
        name="total_rates",
    )(tables, all_own, all_below)


def shards(slabs, subs, positions, velocity, density, pressure, counts, pair_list):
    slab_leaves = counts.shape[0]
    slab = lax.axis_index("slab")
    row = table_row(pair_list, slab, slabs, slab_leaves, slab_leaves // subs)
    tables, own, below, above, beyond = exchange(
        row,
        counts,
        positions,
        velocity,
        density.reshape(slab_leaves, LEAF),
        pressure.reshape(slab_leaves, LEAF),
        slabs,
        subs,
    )
    tables = tables.reshape(4 * subs, LEAF)
    own_part, above_part = pair_sums(tables, counts, (below, own, above, beyond), slabs, subs)
    all_own, all_below = collect_sums(own_part, above_part, slabs, subs)
    return total_rates(tables, all_own, all_below, subs)


def solution(mesh):
    placed = (
        P(None, "slab"),
        P(None, "slab"),
        P("slab"),
        P("slab"),
        P("slab"),
        P(None, ("slab", "sub")),
    )
    return jax.shard_map(
        functools.partial(shards, mesh.shape["slab"], mesh.shape["sub"]),
        mesh=mesh,
        in_specs=placed,
        out_specs=P(None, "slab"),
        check_vma=False,
    )
```

```python
import functools
import math

import jax
import jax.numpy as jnp
from jax import lax
from jax.experimental import pallas as pl
from jax.experimental.pallas import tpu as pltpu
from jax.sharding import PartitionSpec as P

LEAF = 128
KINDS = 5
WIN = 12
LEVELS = 4
GAMMA = 5.0 / 3.0
SUPPORT = 1.5
KERNEL_NORM = 4.0 * 21.0 / (2.0 * math.pi * SUPPORT**3)
MOMENT_REG = 0.05
AREA_FLOOR = 0.0001
FAR_AWAY = 1.0e6
DEAD_ABOVE = 1.0e5
TINY = 1.2e-38
BLOCK = 2
MESH = pl.DeviceIdType.MESH
VMEM = pl.BlockSpec(memory_space=pltpu.VMEM)
SMEM = pl.BlockSpec(memory_space=pltpu.SMEM)
HIGHEST = lax.Precision.HIGHEST


def around(value, size):
    return lax.rem(value + size, size)


def table_row(pair_list, slab, slabs, slab_leaves, homes):
    home, other, offset = pair_list[0], pair_list[1], pair_list[2]
    occupied = home >= 0
    crossing = occupied & (home // slab_leaves != other // slab_leaves)
    step = (other - home + offset + 1) & (slab_leaves - 1)
    kind = jnp.where(other == home, 0, jnp.where(crossing, 2 + step, 1))
    key = jnp.where(occupied & (kind < KINDS), (home & (homes - 1)) * KINDS + kind, -1)
    shear = jnp.where(crossing & (slab == slabs - 1), (-offset) & (slab_leaves - 1), 0)
    lane = jnp.arange(LEAF, dtype=jnp.int32)[:, None]
    size = homes * KINDS
    number = jnp.where(key[None] == lane, 1, 0)
    moved = jnp.where(key[None] == lane - size, offset[None], 0)
    shears = jnp.where(lane == 2 * size, shear[None], 0)
    signed = jnp.where((lane >= size) & (lane < 2 * size) & (moved < 0), moved, 0)
    row = jnp.sum(number, axis=1) + jnp.max(moved + shears, axis=1) + jnp.min(signed, axis=1)
    return row.reshape(1, 1, LEAF)


def exchange_kernel(
    slabs,
    subs,
    row_ref,
    counts,
    positions,
    velocity,
    density,
    pressure,
    lists,
    own,
    below,
    above,
    beyond,
    to_up,
    to_down,
    to_second,
    records,
    list_sems,
    window_sems,
):
    slab = lax.axis_index("slab")
    sub = lax.axis_index("sub")
    slab_leaves = counts.shape[0]
    homes = slab_leaves // subs
    barrier = pltpu.get_barrier_semaphore()

    def each_sub(first, body):
        def one(k, carry):
            body(k)
            return carry

        lax.fori_loop(first, subs, one, 0, unroll=4 if first == 0 else 5)

    for shift in (-2, -1, 0, 1, 2):
        peer_slab = (slab + shift + slabs) & (slabs - 1)

        def greet(k, peer_slab=peer_slab):
            pl.semaphore_signal(
                barrier,
                inc=1,
                device_id=(peer_slab, (sub + k) & (subs - 1)),
                device_id_type=MESH,
            )

        each_sub(1 if shift == 0 else 0, greet)

    lane = lax.broadcasted_iota(jnp.int32, (1, LEAF), 1)
    row = lax.broadcasted_iota(jnp.int32, (3, LEAF), 0)

    def record(leaf, carry):
        start = pl.multiple_of(leaf * LEAF, LEAF)
        live = lane < counts[leaf]
        centre = jnp.where(
            row == 0,
            slab.astype(jnp.float32) + 0.5,
            jnp.where(row == 1, leaf.astype(jnp.float32) + 0.5, 0.5),
        )
        place = (positions[:, pl.ds(start, LEAF)] - centre) * (1.0 / SUPPORT)
        records[leaf, 0:3, :] = jnp.where((row > 0) | live, place, FAR_AWAY)
        records[leaf, 3:6, :] = velocity[:, pl.ds(start, LEAF)]
        records[leaf, 6:7, :] = density[pl.ds(leaf, 1), :]
        records[leaf, 7:8, :] = pressure[pl.ds(leaf, 1), :]
        return carry

    lax.fori_loop(0, slab_leaves, record, 0, unroll=4)

    def fill(target, shift):
        first = sub * homes - 2 + shift + 2 * slab_leaves
        for slot in range(WIN):
            target[slot] = records[(first + slot) & (slab_leaves - 1)]

    fill(own, 0)
    pl.semaphore_wait(barrier, 5 * subs - 1)
    mine = pltpu.make_async_copy(
        row_ref, lists.at[pl.ds(2 * subs + sub, 1)], list_sems.at[2]
    )
    mine.start()
    for shift in (-2, 1, -1, 0):
        peer_slab = (slab - shift + slabs) & (slabs - 1)

        def send(k, shift=shift, peer_slab=peer_slab):
            pltpu.make_async_remote_copy(
                src_ref=row_ref,
                dst_ref=lists.at[pl.ds((shift + 2) * subs + sub, 1)],
                send_sem=list_sems.at[0],
                recv_sem=list_sems.at[1],
                device_id=(peer_slab, (sub + k) & (subs - 1)),
                device_id_type=MESH,
            ).start()

        each_sub(1 if shift == 0 else 0, send)
    mine.wait()
    rest = lists.at[pl.ds(0, 4 * subs - 1)]
    everything = pltpu.make_async_remote_copy(
        src_ref=rest,
        dst_ref=rest,
        send_sem=list_sems.at[0],
        recv_sem=list_sems.at[1],
        device_id=((slab + 1) & (slabs - 1), sub),
        device_id_type=MESH,
    )
    everything.wait_recv()
    everything.wait_send()
    shear = jnp.max(
        jnp.where(
            lax.broadcasted_iota(jnp.int32, (4 * subs, 1, LEAF), 2) == 2 * homes * KINDS,
            lists[...],
            0,
        )
    )
    copies = []
    for k, (shift, source, target) in enumerate(
        ((-2, to_second, beyond), (-1, to_down, above), (1, to_up, below))
    ):
        copies.append(
            pltpu.make_async_remote_copy(
                src_ref=source,
                dst_ref=target,
                send_sem=window_sems.at[k],
                recv_sem=window_sems.at[3 + k],
                device_id=((slab + shift + slabs) & (slabs - 1), sub),
                device_id_type=MESH,
            )
        )
    none = jnp.int32(0)
    fill(to_second, jnp.where(slab <= 1, shear, none))
    fill(to_down, jnp.where(slab == 0, shear, none))
    copies[0].start()
    fill(to_up, jnp.where(slab == slabs - 1, -shear, none))
    copies[1].start()
    copies[2].start()
    for one in copies:
        one.wait()


def exchange(row, counts, positions, velocity, density, pressure, slabs, subs):
    window = jax.ShapeDtypeStruct((WIN, 8, LEAF), jnp.float32)
    return pl.pallas_call(
        functools.partial(exchange_kernel, slabs, subs),
        out_shape=(jax.ShapeDtypeStruct((4 * subs, 1, LEAF), jnp.int32),) + (window,) * 4,
        in_specs=[VMEM, SMEM, VMEM, VMEM, VMEM, VMEM],
        out_specs=(VMEM,) * 5,
        scratch_shapes=[pltpu.VMEM((WIN, 8, LEAF), jnp.float32)] * 3
        + [pltpu.VMEM((counts.shape[0], 8, LEAF), jnp.float32)]
        + [pltpu.SemaphoreType.DMA((3,)), pltpu.SemaphoreType.DMA((6,))],
        compiler_params=pltpu.CompilerParams(collective_id=0, has_side_effects=True),
        name="exchange",
    )(row, counts, positions, velocity, density, pressure)


def three_parts(full):
    first = full.astype(jnp.bfloat16).astype(jnp.float32)
    rest = full - first
    second = rest.astype(jnp.bfloat16).astype(jnp.float32)
    return first, second, rest - second


def left_stack(full):
    first, second, third = three_parts(full)
    return jnp.concatenate([first, first, second, second, first, third], axis=0).astype(
        jnp.bfloat16
    )


def right_stack(full):
    first, second, third = three_parts(full)
    return jnp.concatenate([first, second, first, second, third, first], axis=0).astype(
        jnp.bfloat16
    )


def features(entries, scale, row):
    scaled = scale * entries
    full = jnp.concatenate(
        [
            scaled,
            entries[0:1] * scaled,
            jnp.where(row == 0, scale, entries[1:2] * scaled),
            entries[2:3] * scaled,
        ],
        axis=0,
    )
    return jnp.concatenate(three_parts(full), axis=0).astype(jnp.bfloat16)


def moment_rows(sums, entries, row):
    sums = KERNEL_NORM * (sums[0:32] + sums[32:64] + sums[64:96])
    plain, total = sums[0:8], sums[16:17]
    times = (sums[8:16], jnp.where(row == 0, sums[9:10], sums[16:24]), sums[24:32])
    parts = []
    for k in range(3):
        own = entries[k : k + 1]
        parts.append(
            times[k] - own * plain - entries * sums[k : k + 1] + own * (entries * total)
        )
    return parts, total


def displaced(entries, row, gap_x, gap_y, gap_v):
    entries = jnp.where(entries > DEAD_ABOVE, -entries, entries)
    return entries + jnp.where(
        row == 0, gap_x, jnp.where(row == 1, gap_y, jnp.where(row == 4, gap_v, 0.0))
    )


def length_sq(entries):
    x, y, z = entries[0:1], entries[1:2], entries[2:3]
    return x * x + y * y + z * z


def weights(dist_sq):
    dist_sq = jnp.maximum(dist_sq, TINY)
    inside = jnp.maximum(1.0 - dist_sq * lax.rsqrt(dist_sq), 0.0)
    square = inside * inside
    return square * square * (1.25 - inside)


def finish(parts, total, entries):
    live = (entries[0:1] < DEAD_ABOVE).astype(jnp.float32)
    number = total + 1.0 - live
    inverse = 1.0 / number
    area = inverse * SUPPORT**2
    mx, my, mz = parts
    xx = mx[0:1] * area + MOMENT_REG
    xy = mx[1:2] * area
    xz = mx[2:3] * area
    yy = my[1:2] * area + MOMENT_REG
    yz = my[2:3] * area
    zz = mz[2:3] * area + MOMENT_REG
    minor_xx = yy * zz - yz * yz
    minor_xy = xz * yz - xy * zz
    minor_xz = xy * yz - xz * yy
    minor_yy = xx * zz - xz * xz
    minor_yz = xy * xz - xx * yz
    minor_zz = xx * yy - xy * xy
    unit = 1.0 / (xx * minor_xx + xy * minor_xy + xz * minor_xz)
    ixx, ixy, ixz = minor_xx * unit, minor_xy * unit, minor_xz * unit
    iyy, iyz, izz = minor_yy * unit, minor_yz * unit, minor_zz * unit
    half = 0.5 * area
    mx, my, mz = mx * half, my * half, mz * half
    slope_x = ixx * mx + ixy * my + ixz * mz
    slope_y = ixy * mx + iyy * my + iyz * mz
    slope_z = ixz * mx + iyz * my + izz * mz
    scale = (KERNEL_NORM * SUPPORT) * inverse * inverse
    inverse_rows = [k * scale for k in (ixx, ixy, ixz, iyy, iyz, izz)]
    return number, (slope_x, slope_y, slope_z), inverse_rows


def flux_base(entries, row, last):
    return jnp.where(row < 6, entries, jnp.where(row == 6, 1.0, last))


def flux_coefficients(entries, slopes, inverse_rows, row):
    x, y, z = entries[0:1], entries[1:2], entries[2:3]
    constant = entries - slopes[0] * x - slopes[1] * y - slopes[2] * z
    planes = []
    for q in range(5):
        at = slice(3 + q, 4 + q)
        plane = jnp.where(
            row == 0,
            slopes[0][at],
            jnp.where(
                row == 1,
                slopes[1][at],
                jnp.where(row == 2, slopes[2][at], jnp.where(row == 6, constant[at], 0.0)),
            ),
        )
        if q < 3:
            plane = jnp.where(row == 3 + q, -1.0, plane)
        planes.append(plane)
    ixx, ixy, ixz, iyy, iyz, izz = inverse_rows
    for a, b, c in ((ixx, ixy, ixz), (ixy, iyy, iyz), (ixz, iyz, izz)):
        rest = -(a * x + b * y + c * z)
        planes.append(
            jnp.where(
                row == 0,
                a,
                jnp.where(row == 1, b, jnp.where(row == 2, c, jnp.where(row == 6, rest, 0.0))),
            )
        )
    return planes


PLANES = 14


def flux_terms(plane, near, far, weight):
    smooth = weights(plane(13))
    area = [smooth * plane(10 + k) for k in range(3)]
    area_sq = area[0] * area[0] + area[1] * area[1] + area[2] * area[2]
    root = lax.rsqrt(jnp.maximum(area_sq, TINY))
    size = area_sq * root * weight
    root = jnp.minimum(root, 1.0 / AREA_FLOOR)
    normal = [area[k] * root for k in range(3)]
    left_vel, right_vel, face = [], [], []
    for q in range(3):
        a, b = near(q), far(q)
        face.append(a + b)
        high = jnp.abs(b - a)
        low = -high
        left_vel.append(jnp.minimum(jnp.maximum(plane(q), low), high))
        right_vel.append(jnp.minimum(jnp.maximum(plane(5 + q), low), high))
    states = []
    for q in (3, 4):
        a, b = near(q), far(q)
        low, high = jnp.minimum(a, b), jnp.maximum(a, b)
        states.append(jnp.minimum(jnp.maximum(plane(q), low), high))
        states.append(jnp.minimum(jnp.maximum(plane(5 + q), low), high))
    left_rho, right_rho, left_p, right_p = states
    left_un = left_vel[0] * normal[0] + left_vel[1] * normal[1] + left_vel[2] * normal[2]
    right_un = right_vel[0] * normal[0] + right_vel[1] * normal[1] + right_vel[2] * normal[2]
    root_gamma = math.sqrt(GAMMA)
    left_c = root_gamma * left_p * lax.rsqrt(left_p * left_rho)
    right_c = root_gamma * right_p * lax.rsqrt(right_p * right_rho)
    speed_left = jnp.minimum(left_un - left_c, right_un - right_c)
    speed_right = jnp.maximum(left_un + left_c, right_un + right_c)
    left_m = left_rho * (speed_left - left_un)
    right_m = right_rho * (speed_right - right_un)
    top = right_p - left_p + left_m * left_un - right_m * right_un
    bottom = left_m - right_m
    is_left = top <= 0.0

    def pick(left, right):
        return jnp.where(is_left, left, right)

    rho, p, un = pick(left_rho, right_rho), pick(left_p, right_p), pick(left_un, right_un)
    m, c, speed = pick(left_m, right_m), pick(left_c, right_c), pick(speed_left, speed_right)
    wave = pick(jnp.minimum(speed_left, 0.0), jnp.maximum(speed_right, 0.0))
    lab = [pick(left_vel[k], right_vel[k]) + face[k] for k in range(3)]
    lead = speed * bottom - top
    joint = 1.0 / (bottom * lead)
    contact = top * (lead * joint)
    spread = bottom * (bottom * joint)
    push = wave * ((contact - un) * spread)
    mass = (rho * un + wave * (m * spread - rho)) * size
    thrust = (p + push * m) * size
    carried = (1.5 / GAMMA) * (c * c) + 0.5 * (
        lab[0] * lab[0] + lab[1] * lab[1] + lab[2] * lab[2]
    )
    drift = face[0] * normal[0] + face[1] * normal[1] + face[2] * normal[2]
    energy = mass * carried + drift * thrust + size * (p * un + push * (m * contact + p))
    return [mass] + [lab[k] * mass + normal[k] * thrust for k in range(3)] + [energy]


def pair_kernel(
    slabs,
    subs,
    tables,
    counts,
    below,
    own,
    above,
    beyond,
    own_out,
    above_out,
    store,
    numbers,
    coefficients,
    right_parts,
    left_parts,
    near_rows,
    far_rows,
    planes_one,
    planes_two,
    row_sums,
    flux_sums,
    tiles,
    tile_gaps,
):
    slab = lax.axis_index("slab")
    sub = lax.axis_index("sub")
    slab_leaves = counts.shape[0]
    homes = slab_leaves // subs
    table_size = homes * KINDS
    row = lax.broadcasted_iota(jnp.int32, (8, LEAF), 0)
    for level, source in enumerate((below, own, above, beyond)):
        store[pl.ds(level * WIN, WIN)] = source[...]
    flux_sums[...] = jnp.zeros_like(flux_sums)

    def most(k, value):
        return jnp.maximum(value, tables[k, 2 * table_size])

    shear = lax.fori_loop(0, 4 * subs, most, jnp.int32(0))

    def home_facts(level, place):
        shift = jnp.where(
            (level == 0) & (slab == 0),
            -shear,
            jnp.where((level == 2) & (slab == slabs - 1), shear, 0),
        )
        column = (sub * homes + place + shift + 2 * slab_leaves) & (slab_leaves - 1)
        level_slab = (slab - 1 + level + slabs) & (slabs - 1)
        return level, column, level_slab == slabs - 1

    def pair_facts(facts, kind):
        level, column, last = facts
        device = (level + 1) * subs + column // homes
        entry = (column & (homes - 1)) * KINDS + kind
        crossing = kind >= 2
        step = jnp.where(crossing, kind - 3, jnp.where(kind == 1, 1, 0))
        wraps = crossing & last
        other_column = (
            column + step + jnp.where(wraps, shear, 0) + slab_leaves
        ) & (slab_leaves - 1)
        gap_x = jnp.where(crossing, 1.0 / SUPPORT, 0.0).astype(jnp.float32)
        gap_y = (other_column + tables[device, table_size + entry] - column).astype(
            jnp.float32
        ) * (1.0 / SUPPORT)
        gap_v = jnp.where(wraps, -1.0, 0.0).astype(jnp.float32)
        return tables[device, entry], step + jnp.where(crossing, WIN, 0), gap_x, gap_y, gap_v

    own_first, above_first = WIN + 2, 2 * WIN + 1
    halves = jnp.where((row >= 3) & (row < 6), 0.5, 1.0).astype(jnp.float32)

    def finish_one(k, carry):
        level = jnp.where(k <= homes, 1, 2)
        place = jnp.where(k <= homes, k, k - (homes + 2))
        leaf = level * WIN + place + 2
        mine = store[leaf]
        near_sq = length_sq(mine)
        left = jnp.where(
            row < 3, -2.0 * mine, jnp.where(row == 3, 1.0, jnp.where(row == 4, near_sq, 0.0))
        )
        left = jnp.transpose(left_stack(left).astype(jnp.float32)).astype(jnp.bfloat16)
        here = home_facts(level, place)
        pairs = [(here, kind, 1) for kind in range(KINDS)]
        pairs.append((home_facts(level, place - 1), 1, -1))
        pairs += [(home_facts(level - 1, place + 3 - kind), kind, -1) for kind in (2, 3, 4)]
        sums = None
        for first in range(0, len(pairs), 2):
            rows, rights = [], []
            for facts, kind, sign in pairs[first : first + 2]:
                number, away, gap_x, gap_y, gap_v = pair_facts(facts, kind)
                theirs = displaced(
                    store[leaf + sign * away], row, sign * gap_x, sign * gap_y, sign * gap_v
                )
                right = jnp.where(
                    row < 3,
                    theirs,
                    jnp.where(row == 3, length_sq(theirs), jnp.where(row == 4, 1.0, 0.0)),
                )
                rights.append(right_stack(right))
                rows.append(features(theirs, number.astype(jnp.float32), row))
            smooth = weights(
                lax.dot_general(
                    left,
                    jnp.concatenate(rights, axis=1),
                    (((1,), (0,)), ((), ())),
                    preferred_element_type=jnp.float32,
                )
            )
            high = smooth.astype(jnp.bfloat16)
            low = (smooth - high.astype(jnp.float32)).astype(jnp.bfloat16)
            part = lax.dot_general(
                jnp.concatenate(rows + rows, axis=1),
                jnp.concatenate([high, low], axis=1),
                (((1,), (1,)), ((), ())),
                preferred_element_type=jnp.float32,
            )
            sums = part if sums is None else sums + part
        parts, total = moment_rows(sums, mine, row)
        number, slopes, inverse_rows = finish(parts, total, mine)
        halved = mine * halves
        numbers[leaf] = jnp.broadcast_to(number, (8, LEAF))
        pad = jnp.zeros((16, LEAF), jnp.bfloat16)
        for k, plane in enumerate(flux_coefficients(halved, slopes, inverse_rows, row)):
            coefficients[leaf, k] = plane
            part = right_stack(plane if k < 5 else -plane)
            right_parts[leaf, k] = jnp.concatenate([part, pad], axis=0)
        return carry

    lax.fori_loop(0, 2 * homes + 3, finish_one, 0)

    blank = jnp.zeros((LEAF, LEAF), jnp.float32)

    def turned_left(full, first):
        stack = left_stack(full).astype(jnp.float32)
        parts = ([blank[:first]] if first else []) + [stack, blank[: LEAF - 48 - first]]
        return jnp.transpose(jnp.concatenate(parts, axis=0)).astype(jnp.bfloat16)

    def prepare_home(place, carry):
        leaf = own_first + place
        mine = store[leaf] * halves
        for k in range(8):
            left_parts[place, k] = turned_left(coefficients[leaf, k], 0)
        distance = jnp.where(
            row < 3,
            -2.0 * mine,
            jnp.where(row < 6, 0.0, jnp.where(row == 6, length_sq(mine), 1.0)),
        )
        left_parts[place, 8] = turned_left(distance, 0)
        turned = jnp.transpose(mine)
        for k in range(5):
            near_rows[place, k] = jnp.broadcast_to(
                turned[:, 3 + k : 4 + k], (LEAF, LEAF)
            ).reshape(LEAF // 8, 8, LEAF)
        row_sums[place] = jnp.zeros((5, LEAF // 8, 8, LEAF), jnp.float32)
        return carry

    lax.fori_loop(0, homes, prepare_home, 0, unroll=2)

    def put_tile(index, place, other, gap_x, gap_y, gap_v, scale):
        tiles[2 * index] = place
        tiles[2 * index + 1] = other
        for k, value in enumerate((gap_x, gap_y, gap_v, scale)):
            tile_gaps[4 * index + k] = value

    def list_tile(entry, filled):
        place = entry // KINDS
        kind = entry - place * KINDS
        number, away, gap_x, gap_y, gap_v = pair_facts(home_facts(1, place), kind)
        scale = number.astype(jnp.float32) * jnp.where(kind == 0, 0.5, 1.0).astype(jnp.float32)
        put_tile(filled, place, own_first + place + away, gap_x, gap_y, 0.5 * gap_v, scale)
        return filled + jnp.where(number > 0, 1, 0)

    filled = lax.fori_loop(0, table_size, list_tile, jnp.int32(0))
    nought = jnp.float32(0.0)
    for k in range(3):
        put_tile(filled + k, jnp.int32(0), jnp.int32(own_first), nought, nought, nought, nought)

    def tile_facts(index):
        place = tiles[2 * index]
        gaps = [tile_gaps[4 * index + k] for k in range(4)]
        return (place, own_first + place, tiles[2 * index + 1], *gaps)

    def lay_planes(index, planes):
        place, leaf, other, gap_x, gap_y, gap_v, _ = tile_facts(index)
        theirs = displaced(store[other] * halves, row, gap_x, gap_y, gap_v)
        base = right_stack(flux_base(theirs, row, length_sq(theirs)))
        base = jnp.concatenate([base, jnp.zeros((16, LEAF), jnp.bfloat16)], axis=0)
        mine = store[leaf] * halves - jnp.where(
            row == 0, gap_x, jnp.where(row == 1, gap_y, jnp.where(row == 4, gap_v, 0.0))
        )
        mine = turned_left(flux_base(mine, row, 0.0), 64)
        for k in range(8):
            right = jnp.concatenate([base, right_parts[other, k]], axis=0)
            left = left_parts[place, k]
            if k < 5:
                parts = [left, mine] + ([left_parts[place, 8]] if k == 0 else [])
                targets = [k, 5 + k] + ([13] if k == 0 else [])
            else:
                parts = [left + mine]
                targets = [5 + k]
            for part, target in zip(parts, targets):
                planes[target] = lax.dot_general(
                    part,
                    right,
                    (((1,), (0,)), ((), ())),
                    preferred_element_type=jnp.float32,
                ).reshape(LEAF // 8, 8, LEAF)

    def add_fluxes(index, planes, far_rows):
        place, _, other, gap_x, gap_y, gap_v, scale = tile_facts(index)
        theirs = displaced(store[other] * halves, row, gap_x, gap_y, gap_v)
        for k in range(5):
            far_rows[k] = jnp.broadcast_to(theirs[3 + k : 4 + k], (8, LEAF))
        totals = [None] * 5
        for first in range(0, LEAF // 8, BLOCK):
            terms = flux_terms(
                lambda k: planes[k, first : first + BLOCK],
                lambda k: near_rows[place, k, first : first + BLOCK],
                lambda k: far_rows[k][None],
                scale,
            )
            for k in range(5):
                row_sums[place, k, first : first + BLOCK] += terms[k]
                part = jnp.sum(terms[k], axis=0)
                totals[k] = part if totals[k] is None else totals[k] + part
        added = [jnp.sum(part, axis=0, keepdims=True) for part in totals]
        nothing = jnp.zeros((3, LEAF), jnp.float32)
        flux_sums[other] = flux_sums[other] + jnp.concatenate(added + [nothing], axis=0)

    lay_planes(0, planes_one)

    def two_tiles(step, carry):
        lay_planes(2 * step + 1, planes_two)
        add_fluxes(2 * step, planes_one, far_rows.at[0])
        lay_planes(2 * step + 2, planes_one)
        add_fluxes(2 * step + 1, planes_two, far_rows.at[1])
        return carry

    lax.fori_loop(0, (filled + 1) // 2, two_tiles, 0)
    def close_home(place, carry):
        leaf = own_first + place
        taken = []
        for k in range(5):
            turned = jnp.transpose(row_sums[place, k].reshape(LEAF, LEAF))
            taken.append(jnp.sum(turned, axis=0, keepdims=True))
        nothing = jnp.zeros((3, LEAF), jnp.float32)
        flux_sums[leaf] = flux_sums[leaf] - jnp.concatenate(taken + [nothing], axis=0)
        return carry

    lax.fori_loop(0, homes, close_home, 0, unroll=2)
    for out, first, size in (
        (own_out, own_first, homes + 1),
        (above_out, above_first, homes + 2),
    ):
        out[5 * size :, :] = jnp.zeros((out.shape[0] - 5 * size, LEAF), jnp.float32)
        for k in range(size):
            rates = flux_sums[first + k] * numbers[first + k]
            out[5 * k : 5 * k + 5, :] = rates[0:5]


def packed_rows(leaves):
    return -(-5 * leaves // 8) * 8


def pair_sums(tables, counts, windows, slabs, subs):
    homes = counts.shape[0] // subs
    leaves = LEVELS * WIN
    return pl.pallas_call(
        functools.partial(pair_kernel, slabs, subs),
        out_shape=(
            jax.ShapeDtypeStruct((packed_rows(homes + 1), LEAF), jnp.float32),
            jax.ShapeDtypeStruct((packed_rows(homes + 2), LEAF), jnp.float32),
        ),
        in_specs=[SMEM] * 2 + [VMEM] * 4,
        out_specs=(VMEM, VMEM),
        scratch_shapes=[
            pltpu.VMEM((leaves, 8, LEAF), jnp.float32),
            pltpu.VMEM((leaves, 8, LEAF), jnp.float32),
            pltpu.VMEM((leaves, 8, 8, LEAF), jnp.float32),
            pltpu.VMEM((leaves, 8, 64, LEAF), jnp.bfloat16),
            pltpu.VMEM((homes, 9, LEAF, LEAF), jnp.bfloat16),
            pltpu.VMEM((homes, 5, LEAF // 8, 8, LEAF), jnp.float32),
            pltpu.VMEM((2, 5, 8, LEAF), jnp.float32),
            pltpu.VMEM((PLANES, LEAF // 8, 8, LEAF), jnp.float32),
            pltpu.VMEM((PLANES, LEAF // 8, 8, LEAF), jnp.float32),
            pltpu.VMEM((homes, 5, LEAF // 8, 8, LEAF), jnp.float32),
            pltpu.VMEM((leaves, 8, LEAF), jnp.float32),
            pltpu.SMEM((2 * homes * KINDS + 8,), jnp.int32),
            pltpu.SMEM((4 * homes * KINDS + 16,), jnp.float32),
        ],
        name="pair_sums",
    )(tables, counts, *windows)


def collect_kernel(
    slabs, subs, chunks, own, above, gathered, up_sem, ring_send, ring_recv, core_send, core_recv
):
    slab = lax.axis_index("slab")
    sub = lax.axis_index("sub")
    own_size, above_size = own.shape[0], above.shape[0]
    chips = subs // 2
    chip, core = sub // 2, lax.rem(sub, 2)
    partner = 1 - core
    ahead, behind = around(chip + 1, chips), around(chip - 1, chips)
    right_hops = chips // 2
    left_hops = chips - 1 - right_hops
    barrier = pltpu.get_barrier_semaphore()
    for peer in (
        (around(slab + 1, slabs), sub),
        (around(slab - 1, slabs), sub),
        (slab, 2 * ahead + core),
        (slab, 2 * behind + core),
        (slab, 2 * chip + partner),
    ):
        pl.semaphore_signal(barrier, inc=1, device_id=peer, device_id_type=MESH)
    pl.semaphore_wait(barrier, 5)

    upward = pltpu.make_async_remote_copy(
        src_ref=above,
        dst_ref=gathered.at[sub, pl.ds(own_size, above_size)],
        send_sem=up_sem.at[0],
        recv_sem=up_sem.at[1],
        device_id=(around(slab + 1, slabs), sub),
        device_id_type=MESH,
    )
    upward.start()
    mine = pltpu.make_async_copy(own, gathered.at[sub, pl.ds(0, own_size)], up_sem.at[2])
    mine.start()

    def transfer(which, owner_chip, first, peer, send_sem, recv_sem):
        start, size = chunks[which]
        target = gathered.at[2 * owner_chip + core, pl.ds(start, size)]
        source = own.at[pl.ds(start, size)] if first and start < own_size else target
        return pltpu.make_async_remote_copy(
            src_ref=source,
            dst_ref=target,
            send_sem=send_sem,
            recv_sem=recv_sem,
            device_id=(slab, peer),
            device_id_type=MESH,
        )

    def ring(which, owner_chip, hop, to_right):
        place = (hop - 1) if to_right else (right_hops + hop - 1)
        return transfer(
            which,
            owner_chip,
            hop == 1,
            2 * (ahead if to_right else behind) + core,
            ring_send.at[which, place],
            ring_recv.at[which, place],
        )

    def across(which, owner_chip, place):
        return transfer(
            which,
            owner_chip,
            place == 0,
            2 * chip + partner,
            core_send.at[which, place],
            core_recv.at[which, place],
        )

    started, expected = [], []

    def launch(which):
        for to_right, hops in ((True, right_hops), (False, left_hops)):
            if hops > 0:
                one = ring(which, chip, 1, to_right)
                one.start()
                started.append(one)
        one = across(which, chip, 0)
        one.start()
        started.append(one)
        expected.append(one)

    def forward(which, hop):
        for to_right, hops in ((True, right_hops), (False, left_hops)):
            if hop > hops:
                continue
            owner = around(chip - hop, chips) if to_right else around(chip + hop, chips)
            ring(which, owner, hop, to_right).wait_recv()
            if hop < hops:
                one = ring(which, owner, hop + 1, to_right)
                one.start()
                started.append(one)
            one = across(which, owner, hop if to_right else right_hops + hop)
            one.start()
            started.append(one)
            expected.append(one)

    early = [k for k, (start, _) in enumerate(chunks) if start < own_size]
    late = [k for k, (start, _) in enumerate(chunks) if start >= own_size]
    for which in early:
        launch(which)
    upward.wait()
    for which in late:
        launch(which)
    mine.wait()
    for hop in range(1, right_hops + 1):
        for which in early + late:
            forward(which, hop)
    for one in expected:
        one.wait_recv()
    for one in started:
        one.wait_send()


def collect_sums(own, above, slabs, subs):
    chips = subs // 2
    own_size, above_size = own.shape[0], above.shape[0]
    chunks = (
        (0, own_size // 16 * 8),
        (own_size // 16 * 8, own_size - own_size // 16 * 8),
        (own_size, above_size // 16 * 8),
        (own_size + above_size // 16 * 8, above_size - above_size // 16 * 8),
    )
    sems = pltpu.SemaphoreType.DMA((len(chunks), chips))
    return pl.pallas_call(
        functools.partial(collect_kernel, slabs, subs, chunks),
        out_shape=jax.ShapeDtypeStruct((subs, own_size + above_size, LEAF), jnp.float32),
        in_specs=[VMEM, VMEM],
        out_specs=VMEM,
        scratch_shapes=[pltpu.SemaphoreType.DMA((3,)), sems, sems, sems, sems],
        compiler_params=pltpu.CompilerParams(collective_id=2, has_side_effects=True),
        name="collect_sums",
    )(own, above)


def total_kernel(subs, homes, tables, gathered, out, joined):
    own_size = packed_rows(homes + 1)
    slab_leaves = subs * homes

    def most(k, value):
        return jnp.maximum(value, tables[k, 2 * homes * KINDS])

    shear = lax.fori_loop(0, 4 * subs, most, jnp.int32(0), unroll=8)
    shear = jnp.where(lax.axis_index("slab") == 0, shear, 0)

    def part(device, first):
        return gathered[device, first : first + 5, :]

    def join(device, carry):
        nearer, later = (device + subs - 1) & (subs - 1), (device + 1) & (subs - 1)
        for place in range(homes):
            total = part(device, own_size + 5 * (place + 1))
            if place == 0:
                total = total + part(nearer, own_size + 5 * (homes + 1))
            if place == homes - 1:
                total = total + part(later, own_size)
            joined[device * homes + place, 0:5, :] = total
        return carry

    lax.fori_loop(0, subs, join, 0)

    def add(device, carry):
        nearer = (device + subs - 1) & (subs - 1)
        for place in range(homes):
            total = part(device, 5 * place)
            if place == 0:
                total = total + part(nearer, 5 * homes)
            column = device * homes + place
            source = (column - shear + slab_leaves) & (slab_leaves - 1)
            start = pl.multiple_of(column * LEAF, LEAF)
            out[:, pl.ds(start, LEAF)] = total + joined[source, 0:5, :]
        return carry

    lax.fori_loop(0, subs, add, 0)


def total_rates(tables, gathered, subs, homes):
    return pl.pallas_call(
        functools.partial(total_kernel, subs, homes),
        out_shape=jax.ShapeDtypeStruct((5, subs * homes * LEAF), jnp.float32),
        in_specs=[SMEM, VMEM],
        out_specs=VMEM,
        scratch_shapes=[pltpu.VMEM((subs * homes, 8, LEAF), jnp.float32)],
        name="total_rates",
    )(tables, gathered)


def shards(slabs, subs, positions, velocity, density, pressure, counts, pair_list):
    slab_leaves = counts.shape[0]
    slab = lax.axis_index("slab")
    row = table_row(pair_list, slab, slabs, slab_leaves, slab_leaves // subs)
    tables, own, below, above, beyond = exchange(
        row,
        counts,
        positions,
        velocity,
        density.reshape(slab_leaves, LEAF),
        pressure.reshape(slab_leaves, LEAF),
        slabs,
        subs,
    )
    tables = tables.reshape(4 * subs, LEAF)
    own_part, above_part = pair_sums(tables, counts, (below, own, above, beyond), slabs, subs)
    gathered = collect_sums(own_part, above_part, slabs, subs)
    return total_rates(tables, gathered, subs, slab_leaves // subs)


def solution(mesh):
    placed = (
        P(None, "slab"),
        P(None, "slab"),
        P("slab"),
        P("slab"),
        P("slab"),
        P(None, ("slab", "sub")),
    )
    return jax.shard_map(
        functools.partial(shards, mesh.shape["slab"], mesh.shape["sub"]),
        mesh=mesh,
        in_specs=placed,
        out_specs=P(None, "slab"),
        check_vma=False,
    )
```

```python
import functools
import math

import jax
import jax.numpy as jnp
from jax import lax
from jax.experimental import pallas as pl
from jax.experimental.pallas import tpu as pltpu
from jax.sharding import PartitionSpec as P

LEAF = 128
KINDS = 5
WIN = 12
LEVELS = 4
GAMMA = 5.0 / 3.0
SUPPORT = 1.5
KERNEL_NORM = 4.0 * 21.0 / (2.0 * math.pi * SUPPORT**3)
MOMENT_REG = 0.05
AREA_FLOOR = 0.0001
FAR_AWAY = 1.0e6
DEAD_ABOVE = 1.0e5
TINY = 1.2e-38
BLOCK = 2
MESH = pl.DeviceIdType.MESH
VMEM = pl.BlockSpec(memory_space=pltpu.VMEM)
SMEM = pl.BlockSpec(memory_space=pltpu.SMEM)
HIGHEST = lax.Precision.HIGHEST


def table_row(pair_list, slab, slabs, slab_leaves, homes):
    home, other, offset = pair_list[0], pair_list[1], pair_list[2]
    occupied = home >= 0
    crossing = occupied & (home // slab_leaves != other // slab_leaves)
    step = (other - home + offset + 1) & (slab_leaves - 1)
    kind = jnp.where(other == home, 0, jnp.where(crossing, 2 + step, 1))
    key = jnp.where(occupied & (kind < KINDS), (home & (homes - 1)) * KINDS + kind, -1)
    shear = jnp.where(crossing & (slab == slabs - 1), (-offset) & (slab_leaves - 1), 0)
    lane = jnp.arange(LEAF, dtype=jnp.int32)[:, None]
    size = homes * KINDS
    number = jnp.where(key[None] == lane, 1, 0)
    moved = jnp.where(key[None] == lane - size, offset[None], 0)
    shears = jnp.where(lane == 2 * size, shear[None], 0)
    signed = jnp.where((lane >= size) & (lane < 2 * size) & (moved < 0), moved, 0)
    row = jnp.sum(number, axis=1) + jnp.max(moved + shears, axis=1) + jnp.min(signed, axis=1)
    return row.reshape(1, 1, LEAF)


def exchange_kernel(
    slabs,
    subs,
    row_ref,
    counts,
    positions,
    velocity,
    density,
    pressure,
    lists,
    own,
    below,
    above,
    beyond,
    to_up,
    to_down,
    to_second,
    records,
    list_sems,
    window_sems,
):
    slab = lax.axis_index("slab")
    sub = lax.axis_index("sub")
    slab_leaves = counts.shape[0]
    homes = slab_leaves // subs
    barrier = pltpu.get_barrier_semaphore()

    def each_sub(first, body):
        def one(k, carry):
            body(k)
            return carry

        lax.fori_loop(first, subs, one, 0, unroll=4 if first == 0 else 5)

    for shift in (-2, -1, 0, 1, 2):
        peer_slab = (slab + shift + slabs) & (slabs - 1)

        def greet(k, peer_slab=peer_slab):
            pl.semaphore_signal(
                barrier,
                inc=1,
                device_id=(peer_slab, (sub + k) & (subs - 1)),
                device_id_type=MESH,
            )

        each_sub(1 if shift == 0 else 0, greet)

    lane = lax.broadcasted_iota(jnp.int32, (1, LEAF), 1)
    row = lax.broadcasted_iota(jnp.int32, (3, LEAF), 0)

    def record(leaf, carry):
        start = pl.multiple_of(leaf * LEAF, LEAF)
        live = lane < counts[leaf]
        centre = jnp.where(
            row == 0,
            slab.astype(jnp.float32) + 0.5,
            jnp.where(row == 1, leaf.astype(jnp.float32) + 0.5, 0.5),
        )
        place = (positions[:, pl.ds(start, LEAF)] - centre) * (1.0 / SUPPORT)
        records[leaf, 0:3, :] = jnp.where((row > 0) | live, place, FAR_AWAY)
        records[leaf, 3:6, :] = velocity[:, pl.ds(start, LEAF)]
        records[leaf, 6:7, :] = density[pl.ds(leaf, 1), :]
        records[leaf, 7:8, :] = pressure[pl.ds(leaf, 1), :]
        return carry

    lax.fori_loop(0, slab_leaves, record, 0, unroll=4)

    def fill(target, shift):
        first = sub * homes - 2 + shift + 2 * slab_leaves
        for slot in range(WIN):
            target[slot] = records[(first + slot) & (slab_leaves - 1)]

    fill(own, 0)
    pl.semaphore_wait(barrier, 5 * subs - 1)
    mine = pltpu.make_async_copy(
        row_ref, lists.at[pl.ds(2 * subs + sub, 1)], list_sems.at[2]
    )
    mine.start()
    for shift in (-2, 1, -1, 0):
        peer_slab = (slab - shift + slabs) & (slabs - 1)

        def send(k, shift=shift, peer_slab=peer_slab):
            pltpu.make_async_remote_copy(
                src_ref=row_ref,
                dst_ref=lists.at[pl.ds((shift + 2) * subs + sub, 1)],
                send_sem=list_sems.at[0],
                recv_sem=list_sems.at[1],
                device_id=(peer_slab, (sub + k) & (subs - 1)),
                device_id_type=MESH,
            ).start()

        each_sub(1 if shift == 0 else 0, send)
    mine.wait()
    rest = lists.at[pl.ds(0, 4 * subs - 1)]
    everything = pltpu.make_async_remote_copy(
        src_ref=rest,
        dst_ref=rest,
        send_sem=list_sems.at[0],
        recv_sem=list_sems.at[1],
        device_id=((slab + 1) & (slabs - 1), sub),
        device_id_type=MESH,
    )
    everything.wait_recv()
    everything.wait_send()
    shear = jnp.max(
        jnp.where(
            lax.broadcasted_iota(jnp.int32, (4 * subs, 1, LEAF), 2) == 2 * homes * KINDS,
            lists[...],
            0,
        )
    )
    copies = []
    for k, (shift, source, target) in enumerate(
        ((-2, to_second, beyond), (-1, to_down, above), (1, to_up, below))
    ):
        copies.append(
            pltpu.make_async_remote_copy(
                src_ref=source,
                dst_ref=target,
                send_sem=window_sems.at[k],
                recv_sem=window_sems.at[3 + k],
                device_id=((slab + shift + slabs) & (slabs - 1), sub),
                device_id_type=MESH,
            )
        )
    none = jnp.int32(0)
    fill(to_second, jnp.where(slab <= 1, shear, none))
    fill(to_down, jnp.where(slab == 0, shear, none))
    copies[0].start()
    fill(to_up, jnp.where(slab == slabs - 1, -shear, none))
    copies[1].start()
    copies[2].start()
    for one in copies:
        one.wait()


def exchange(row, counts, positions, velocity, density, pressure, slabs, subs):
    window = jax.ShapeDtypeStruct((WIN, 8, LEAF), jnp.float32)
    return pl.pallas_call(
        functools.partial(exchange_kernel, slabs, subs),
        out_shape=(jax.ShapeDtypeStruct((4 * subs, 1, LEAF), jnp.int32),) + (window,) * 4,
        in_specs=[VMEM, SMEM, VMEM, VMEM, VMEM, VMEM],
        out_specs=(VMEM,) * 5,
        scratch_shapes=[pltpu.VMEM((WIN, 8, LEAF), jnp.float32)] * 3
        + [pltpu.VMEM((counts.shape[0], 8, LEAF), jnp.float32)]
        + [pltpu.SemaphoreType.DMA((3,)), pltpu.SemaphoreType.DMA((6,))],
        compiler_params=pltpu.CompilerParams(collective_id=0, has_side_effects=True),
        name="exchange",
    )(row, counts, positions, velocity, density, pressure)


def three_parts(full):
    first = full.astype(jnp.bfloat16).astype(jnp.float32)
    rest = full - first
    second = rest.astype(jnp.bfloat16).astype(jnp.float32)
    return first, second, rest - second


def left_stack(full):
    first, second, third = three_parts(full)
    return jnp.concatenate([first, first, second, second, first, third], axis=0).astype(
        jnp.bfloat16
    )


def right_stack(full):
    first, second, third = three_parts(full)
    return jnp.concatenate([first, second, first, second, third, first], axis=0).astype(
        jnp.bfloat16
    )


def features(entries, scale, row):
    scaled = scale * entries
    full = jnp.concatenate(
        [
            scaled,
            entries[0:1] * scaled,
            jnp.where(row == 0, scale, entries[1:2] * scaled),
            entries[2:3] * scaled,
        ],
        axis=0,
    )
    return jnp.concatenate(three_parts(full), axis=0).astype(jnp.bfloat16)


def moment_rows(sums, entries, row):
    sums = KERNEL_NORM * (sums[0:32] + sums[32:64] + sums[64:96])
    plain, total = sums[0:8], sums[16:17]
    times = (sums[8:16], jnp.where(row == 0, sums[9:10], sums[16:24]), sums[24:32])
    parts = []
    for k in range(3):
        own = entries[k : k + 1]
        parts.append(
            times[k] - own * plain - entries * sums[k : k + 1] + own * (entries * total)
        )
    return parts, total


def displaced(entries, row, gap_x, gap_y, gap_v):
    entries = jnp.where(entries > DEAD_ABOVE, -entries, entries)
    return entries + jnp.where(
        row == 0, gap_x, jnp.where(row == 1, gap_y, jnp.where(row == 4, gap_v, 0.0))
    )


def length_sq(entries):
    x, y, z = entries[0:1], entries[1:2], entries[2:3]
    return x * x + y * y + z * z


def weights(dist_sq):
    dist_sq = jnp.maximum(dist_sq, TINY)
    inside = jnp.maximum(1.0 - dist_sq * lax.rsqrt(dist_sq), 0.0)
    square = inside * inside
    return square * square * (1.25 - inside)


def finish(parts, total, entries):
    live = (entries[0:1] < DEAD_ABOVE).astype(jnp.float32)
    number = total + 1.0 - live
    inverse = 1.0 / number
    area = inverse * SUPPORT**2
    mx, my, mz = parts
    xx = mx[0:1] * area + MOMENT_REG
    xy = mx[1:2] * area
    xz = mx[2:3] * area
    yy = my[1:2] * area + MOMENT_REG
    yz = my[2:3] * area
    zz = mz[2:3] * area + MOMENT_REG
    minor_xx = yy * zz - yz * yz
    minor_xy = xz * yz - xy * zz
    minor_xz = xy * yz - xz * yy
    minor_yy = xx * zz - xz * xz
    minor_yz = xy * xz - xx * yz
    minor_zz = xx * yy - xy * xy
    unit = 1.0 / (xx * minor_xx + xy * minor_xy + xz * minor_xz)
    ixx, ixy, ixz = minor_xx * unit, minor_xy * unit, minor_xz * unit
    iyy, iyz, izz = minor_yy * unit, minor_yz * unit, minor_zz * unit
    half = 0.5 * area
    mx, my, mz = mx * half, my * half, mz * half
    slope_x = ixx * mx + ixy * my + ixz * mz
    slope_y = ixy * mx + iyy * my + iyz * mz
    slope_z = ixz * mx + iyz * my + izz * mz
    scale = (KERNEL_NORM * SUPPORT) * inverse * inverse
    inverse_rows = [k * scale for k in (ixx, ixy, ixz, iyy, iyz, izz)]
    return number, (slope_x, slope_y, slope_z), inverse_rows


def flux_base(entries, row, last):
    return jnp.where(row < 6, entries, jnp.where(row == 6, 1.0, last))


def flux_coefficients(entries, slopes, inverse_rows, row):
    x, y, z = entries[0:1], entries[1:2], entries[2:3]
    constant = entries - slopes[0] * x - slopes[1] * y - slopes[2] * z
    planes = []
    for q in range(5):
        at = slice(3 + q, 4 + q)
        plane = jnp.where(
            row == 0,
            slopes[0][at],
            jnp.where(
                row == 1,
                slopes[1][at],
                jnp.where(row == 2, slopes[2][at], jnp.where(row == 6, constant[at], 0.0)),
            ),
        )
        if q < 3:
            plane = jnp.where(row == 3 + q, -1.0, plane)
        planes.append(plane)
    ixx, ixy, ixz, iyy, iyz, izz = inverse_rows
    for a, b, c in ((ixx, ixy, ixz), (ixy, iyy, iyz), (ixz, iyz, izz)):
        rest = -(a * x + b * y + c * z)
        planes.append(
            jnp.where(
                row == 0,
                a,
                jnp.where(row == 1, b, jnp.where(row == 2, c, jnp.where(row == 6, rest, 0.0))),
            )
        )
    return planes


PLANES = 14


def flux_terms(plane, near, far, weight):
    smooth = weights(plane(13))
    area = [smooth * plane(10 + k) for k in range(3)]
    area_sq = area[0] * area[0] + area[1] * area[1] + area[2] * area[2]
    root = lax.rsqrt(jnp.maximum(area_sq, TINY))
    size = area_sq * root * weight
    root = jnp.minimum(root, 1.0 / AREA_FLOOR)
    normal = [area[k] * root for k in range(3)]
    left_vel, right_vel, face = [], [], []
    for q in range(3):
        a, b = near(q), far(q)
        face.append(a + b)
        high = jnp.abs(b - a)
        low = -high
        left_vel.append(jnp.minimum(jnp.maximum(plane(q), low), high))
        right_vel.append(jnp.minimum(jnp.maximum(plane(5 + q), low), high))
    states = []
    for q in (3, 4):
        a, b = near(q), far(q)
        low, high = jnp.minimum(a, b), jnp.maximum(a, b)
        states.append(jnp.minimum(jnp.maximum(plane(q), low), high))
        states.append(jnp.minimum(jnp.maximum(plane(5 + q), low), high))
    left_rho, right_rho, left_p, right_p = states
    left_un = left_vel[0] * normal[0] + left_vel[1] * normal[1] + left_vel[2] * normal[2]
    right_un = right_vel[0] * normal[0] + right_vel[1] * normal[1] + right_vel[2] * normal[2]
    root_gamma = math.sqrt(GAMMA)
    left_c = root_gamma * left_p * lax.rsqrt(left_p * left_rho)
    right_c = root_gamma * right_p * lax.rsqrt(right_p * right_rho)
    speed_left = jnp.minimum(left_un - left_c, right_un - right_c)
    speed_right = jnp.maximum(left_un + left_c, right_un + right_c)
    left_m = left_rho * (speed_left - left_un)
    right_m = right_rho * (speed_right - right_un)
    top = right_p - left_p + left_m * left_un - right_m * right_un
    bottom = left_m - right_m
    is_left = top <= 0.0

    def pick(left, right):
        return jnp.where(is_left, left, right)

    rho, p, un = pick(left_rho, right_rho), pick(left_p, right_p), pick(left_un, right_un)
    m, c, speed = pick(left_m, right_m), pick(left_c, right_c), pick(speed_left, speed_right)
    wave = pick(jnp.minimum(speed_left, 0.0), jnp.maximum(speed_right, 0.0))
    lab = [pick(left_vel[k], right_vel[k]) + face[k] for k in range(3)]
    lead = speed * bottom - top
    joint = 1.0 / (bottom * lead)
    contact = top * (lead * joint)
    spread = bottom * (bottom * joint)
    push = wave * ((contact - un) * spread)
    mass = (rho * un + wave * (m * spread - rho)) * size
    thrust = (p + push * m) * size
    carried = (1.5 / GAMMA) * (c * c) + 0.5 * (
        lab[0] * lab[0] + lab[1] * lab[1] + lab[2] * lab[2]
    )
    drift = face[0] * normal[0] + face[1] * normal[1] + face[2] * normal[2]
    energy = mass * carried + drift * thrust + size * (p * un + push * (m * contact + p))
    return [mass] + [lab[k] * mass + normal[k] * thrust for k in range(3)] + [energy]


def pair_kernel(
    slabs,
    subs,
    tables,
    counts,
    below,
    own,
    above,
    beyond,
    own_out,
    above_out,
    store,
    numbers,
    coefficients,
    right_parts,
    left_parts,
    near_rows,
    far_rows,
    planes_one,
    planes_two,
    row_sums,
    flux_sums,
    bases,
    mine_one,
    mine_two,
    tiles,
    tile_gaps,
):
    slab = lax.axis_index("slab")
    sub = lax.axis_index("sub")
    slab_leaves = counts.shape[0]
    homes = slab_leaves // subs
    table_size = homes * KINDS
    row = lax.broadcasted_iota(jnp.int32, (8, LEAF), 0)
    for level, source in enumerate((below, own, above, beyond)):
        store[pl.ds(level * WIN, WIN)] = source[...]
    flux_sums[...] = jnp.zeros_like(flux_sums)

    def most(k, value):
        return jnp.maximum(value, tables[k, 2 * table_size])

    shear = lax.fori_loop(0, 4 * subs, most, jnp.int32(0))

    def home_facts(level, place):
        shift = jnp.where(
            (level == 0) & (slab == 0),
            -shear,
            jnp.where((level == 2) & (slab == slabs - 1), shear, 0),
        )
        column = (sub * homes + place + shift + 2 * slab_leaves) & (slab_leaves - 1)
        level_slab = (slab - 1 + level + slabs) & (slabs - 1)
        return level, column, level_slab == slabs - 1

    def pair_facts(facts, kind):
        level, column, last = facts
        device = (level + 1) * subs + column // homes
        entry = (column & (homes - 1)) * KINDS + kind
        crossing = kind >= 2
        step = jnp.where(crossing, kind - 3, jnp.where(kind == 1, 1, 0))
        wraps = crossing & last
        other_column = (
            column + step + jnp.where(wraps, shear, 0) + slab_leaves
        ) & (slab_leaves - 1)
        gap_x = jnp.where(crossing, 1.0 / SUPPORT, 0.0).astype(jnp.float32)
        gap_y = (other_column + tables[device, table_size + entry] - column).astype(
            jnp.float32
        ) * (1.0 / SUPPORT)
        gap_v = jnp.where(wraps, -1.0, 0.0).astype(jnp.float32)
        return tables[device, entry], step + jnp.where(crossing, WIN, 0), gap_x, gap_y, gap_v

    own_first, above_first = WIN + 2, 2 * WIN + 1
    halves = jnp.where((row >= 3) & (row < 6), 0.5, 1.0).astype(jnp.float32)

    def finish_one(k, carry):
        k = jnp.minimum(k, 2 * homes + 2)
        level = jnp.where(k <= homes, 1, 2)
        place = jnp.where(k <= homes, k, k - (homes + 2))
        leaf = level * WIN + place + 2
        mine = store[leaf]
        near_sq = length_sq(mine)
        left = jnp.where(
            row < 3, -2.0 * mine, jnp.where(row == 3, 1.0, jnp.where(row == 4, near_sq, 0.0))
        )
        left = jnp.transpose(left_stack(left).astype(jnp.float32)).astype(jnp.bfloat16)
        here = home_facts(level, place)
        pairs = [(here, kind, 1) for kind in range(KINDS)]
        pairs.append((home_facts(level, place - 1), 1, -1))
        pairs += [(home_facts(level - 1, place + 3 - kind), kind, -1) for kind in (2, 3, 4)]
        sums = None
        for first in range(0, len(pairs), 2):
            rows, rights = [], []
            for facts, kind, sign in pairs[first : first + 2]:
                number, away, gap_x, gap_y, gap_v = pair_facts(facts, kind)
                theirs = displaced(
                    store[leaf + sign * away], row, sign * gap_x, sign * gap_y, sign * gap_v
                )
                right = jnp.where(
                    row < 3,
                    theirs,
                    jnp.where(row == 3, length_sq(theirs), jnp.where(row == 4, 1.0, 0.0)),
                )
                rights.append(right_stack(right))
                rows.append(features(theirs, number.astype(jnp.float32), row))
            smooth = weights(
                lax.dot_general(
                    left,
                    jnp.concatenate(rights, axis=1),
                    (((1,), (0,)), ((), ())),
                    preferred_element_type=jnp.float32,
                )
            )
            high = smooth.astype(jnp.bfloat16)
            low = (smooth - high.astype(jnp.float32)).astype(jnp.bfloat16)
            part = lax.dot_general(
                jnp.concatenate(rows + rows, axis=1),
                jnp.concatenate([high, low], axis=1),
                (((1,), (1,)), ((), ())),
                preferred_element_type=jnp.float32,
            )
            sums = part if sums is None else sums + part
        parts, total = moment_rows(sums, mine, row)
        number, slopes, inverse_rows = finish(parts, total, mine)
        halved = mine * halves
        numbers[leaf] = jnp.broadcast_to(number, (8, LEAF))
        pad = jnp.zeros((16, LEAF), jnp.bfloat16)
        for k, plane in enumerate(flux_coefficients(halved, slopes, inverse_rows, row)):
            coefficients[leaf, k] = plane
            part = right_stack(plane if k < 5 else -plane)
            right_parts[leaf, k] = jnp.concatenate([part, pad], axis=0)
        return carry

    lax.fori_loop(0, 2 * homes + 4, finish_one, 0, unroll=2)

    blank = jnp.zeros((LEAF, LEAF), jnp.float32)

    def turned_left(full):
        stack = left_stack(full).astype(jnp.float32)
        return jnp.transpose(jnp.concatenate([stack, blank[:80]], axis=0)).astype(jnp.bfloat16)

    def prepare_home(place, carry):
        leaf = own_first + place
        mine = store[leaf] * halves
        for k in range(8):
            left_parts[place, k] = turned_left(coefficients[leaf, k])
        distance = jnp.where(
            row < 3,
            -2.0 * mine,
            jnp.where(row < 6, 0.0, jnp.where(row == 6, length_sq(mine), 1.0)),
        )
        left_parts[place, 8] = turned_left(distance)
        turned = jnp.transpose(mine)
        for k in range(5):
            near_rows[place, k] = jnp.broadcast_to(
                turned[:, 3 + k : 4 + k], (LEAF, LEAF)
            ).reshape(LEAF // 8, 8, LEAF)
        row_sums[place] = jnp.zeros((5, LEAF // 8, 8, LEAF), jnp.float32)
        return carry

    lax.fori_loop(0, homes, prepare_home, 0, unroll=2)

    def put_tile(index, place, other, gap_x, gap_y, gap_v, scale):
        tiles[2 * index] = place
        tiles[2 * index + 1] = other
        for k, value in enumerate((gap_x, gap_y, gap_v, scale)):
            tile_gaps[4 * index + k] = value

    def list_tile(entry, filled):
        place = entry // KINDS
        kind = entry - place * KINDS
        number, away, gap_x, gap_y, gap_v = pair_facts(home_facts(1, place), kind)
        scale = number.astype(jnp.float32) * jnp.where(kind == 0, 0.5, 1.0).astype(jnp.float32)
        put_tile(filled, place, own_first + place + away, gap_x, gap_y, 0.5 * gap_v, scale)
        return filled + jnp.where(number > 0, 1, 0)

    filled = lax.fori_loop(0, table_size, list_tile, jnp.int32(0))
    nought = jnp.float32(0.0)
    for k in range(3):
        put_tile(filled + k, jnp.int32(0), jnp.int32(own_first), nought, nought, nought, nought)

    def tile_facts(index):
        place = tiles[2 * index]
        gaps = [tile_gaps[4 * index + k] for k in range(4)]
        return (place, own_first + place, tiles[2 * index + 1], *gaps)

    def ready_tile(index, base_rows, mine_rows):
        place, leaf, other, gap_x, gap_y, gap_v, _ = tile_facts(index)
        theirs = displaced(store[other] * halves, row, gap_x, gap_y, gap_v)
        base = right_stack(flux_base(theirs, row, length_sq(theirs)))
        base_rows[...] = jnp.concatenate([base, jnp.zeros((16, LEAF), jnp.bfloat16)], axis=0)
        mine = store[leaf] * halves - jnp.where(
            row == 0, gap_x, jnp.where(row == 1, gap_y, jnp.where(row == 4, gap_v, 0.0))
        )
        stack = left_stack(flux_base(mine, row, 0.0)).astype(jnp.float32)
        mine_rows[...] = jnp.transpose(
            jnp.concatenate([blank[:64], stack, blank[:16]], axis=0)
        ).astype(jnp.bfloat16)

    def lay_planes(index, planes, base_rows, mine_rows):
        place, _, other = tile_facts(index)[:3]
        base, mine = base_rows[...], mine_rows[...]

        def lay(k):
            right = jnp.concatenate([base, right_parts[other, k]], axis=0)
            left = left_parts[place, k]
            if k < 5:
                parts = [left, mine] + ([left_parts[place, 8]] if k == 0 else [])
                targets = [k, 5 + k] + ([13] if k == 0 else [])
            else:
                parts = [left + mine]
                targets = [5 + k]
            for part, target in zip(parts, targets):
                planes[target] = lax.dot_general(
                    part,
                    right,
                    (((1,), (0,)), ((), ())),
                    preferred_element_type=jnp.float32,
                ).reshape(LEAF // 8, 8, LEAF)

        return lay

    def add_fluxes(index, planes, far_rows):
        place, _, other, gap_x, gap_y, gap_v, scale = tile_facts(index)
        theirs = displaced(store[other] * halves, row, gap_x, gap_y, gap_v)
        for k in range(5):
            far_rows[k] = jnp.broadcast_to(theirs[3 + k : 4 + k], (8, LEAF))
        totals = [None] * 5

        def step(first):
            terms = flux_terms(
                lambda k: planes[k, first : first + BLOCK],
                lambda k: near_rows[place, k, first : first + BLOCK],
                lambda k: far_rows[k][None],
                scale,
            )
            for k in range(5):
                row_sums[place, k, first : first + BLOCK] += terms[k]
                part = jnp.sum(terms[k], axis=0)
                totals[k] = part if totals[k] is None else totals[k] + part

        def close():
            added = [jnp.sum(part, axis=0, keepdims=True) for part in totals]
            nothing = jnp.zeros((3, LEAF), jnp.float32)
            flux_sums[other] = flux_sums[other] + jnp.concatenate(added + [nothing], axis=0)

        return step, close

    slots = (
        (planes_one, bases.at[0], mine_one, far_rows.at[0]),
        (planes_two, bases.at[1], mine_two, far_rows.at[1]),
    )

    def both(index, this, that):
        lay = lay_planes(index + 1, *that[:3])
        step, close = add_fluxes(index, this[0], this[3])
        steps = list(range(0, LEAF // 8, BLOCK))
        pace = len(steps) / 8
        for k in range(8):
            lay(k)
            for first in steps[int(k * pace) : int((k + 1) * pace)]:
                step(first)
        close()
        ready_tile(index + 2, *this[1:3])

    ready_tile(0, *slots[0][1:3])
    ready_tile(1, *slots[1][1:3])
    first_lay = lay_planes(0, *slots[0][:3])
    for k in range(8):
        first_lay(k)

    def two_tiles(step, carry):
        both(2 * step, slots[0], slots[1])

        @pl.when(2 * step + 1 < filled)
        def _():
            both(2 * step + 1, slots[1], slots[0])

        return carry

    lax.fori_loop(0, (filled + 1) // 2, two_tiles, 0)
    def close_home(place, carry):
        leaf = own_first + place
        taken = []
        for k in range(5):
            turned = jnp.transpose(row_sums[place, k].reshape(LEAF, LEAF))
            taken.append(jnp.sum(turned, axis=0, keepdims=True))
        nothing = jnp.zeros((3, LEAF), jnp.float32)
        flux_sums[leaf] = flux_sums[leaf] - jnp.concatenate(taken + [nothing], axis=0)
        return carry

    lax.fori_loop(0, homes, close_home, 0, unroll=2)
    gap = jnp.zeros((3, LEAF), jnp.float32)

    def put(out, start, leaf, padded):
        rates = (flux_sums[leaf] * numbers[leaf])[0:5]
        if padded:
            out[start : start + 8, :] = jnp.concatenate([rates, gap], axis=0)
        else:
            out[start : start + 5, :] = rates

    for k in range(homes):
        put(own_out, 5 * k, own_first + k, False)
        put(above_out, 5 * k, above_first + 1 + k, False)
    put(own_out, 5 * homes, own_first + homes, True)
    put(above_out, 5 * homes, above_first, True)
    put(above_out, 5 * homes + 8, above_first + homes + 1, True)


def pair_sums(tables, counts, windows, slabs, subs):
    homes = counts.shape[0] // subs
    leaves = LEVELS * WIN
    return pl.pallas_call(
        functools.partial(pair_kernel, slabs, subs),
        out_shape=(
            jax.ShapeDtypeStruct((5 * homes + 8, LEAF), jnp.float32),
            jax.ShapeDtypeStruct((5 * homes + 16, LEAF), jnp.float32),
        ),
        in_specs=[SMEM] * 2 + [VMEM] * 4,
        out_specs=(VMEM, VMEM),
        scratch_shapes=[
            pltpu.VMEM((leaves, 8, LEAF), jnp.float32),
            pltpu.VMEM((leaves, 8, LEAF), jnp.float32),
            pltpu.VMEM((leaves, 8, 8, LEAF), jnp.float32),
            pltpu.VMEM((leaves, 8, 64, LEAF), jnp.bfloat16),
            pltpu.VMEM((homes, 9, LEAF, LEAF), jnp.bfloat16),
            pltpu.VMEM((homes, 5, LEAF // 8, 8, LEAF), jnp.float32),
            pltpu.VMEM((2, 5, 8, LEAF), jnp.float32),
            pltpu.VMEM((PLANES, LEAF // 8, 8, LEAF), jnp.float32),
            pltpu.VMEM((PLANES, LEAF // 8, 8, LEAF), jnp.float32),
            pltpu.VMEM((homes, 5, LEAF // 8, 8, LEAF), jnp.float32),
            pltpu.VMEM((leaves, 8, LEAF), jnp.float32),
            pltpu.VMEM((2, 64, LEAF), jnp.bfloat16),
            pltpu.VMEM((LEAF, LEAF), jnp.bfloat16),
            pltpu.VMEM((LEAF, LEAF), jnp.bfloat16),
            pltpu.SMEM((2 * homes * KINDS + 8,), jnp.int32),
            pltpu.SMEM((4 * homes * KINDS + 16,), jnp.float32),
        ],
        name="pair_sums",
    )(tables, counts, *windows)


def collect_kernel(
    slabs,
    subs,
    own,
    above,
    gathered,
    sheared,
    got_main,
    got_edges,
    near_send,
    near_recv,
    chip_send,
    chip_recv,
    core_send,
    core_recv,
    far_send,
    far_recv,
    pass_send,
    pass_recv,
):
    slab = lax.axis_index("slab")
    sub = lax.axis_index("sub")
    main = gathered.shape[1]
    chips = subs // 2
    partner = sub + 1 - 2 * (sub & 1)
    up, down = (slab + 1) & (slabs - 1), (slab - 1 + slabs) & (slabs - 1)
    after, before = (sub + 1) & (subs - 1), (sub - 1 + subs) & (subs - 1)

    def same_core(k):
        return (sub + 2 * k + subs) & (subs - 1)

    barrier = pltpu.get_barrier_semaphore()

    def greet(*peer):
        pl.semaphore_signal(barrier, inc=1, device_id=peer, device_id_type=MESH)

    for peer_slab in (up, down):
        for peer_sub in (before, sub, after):
            greet(peer_slab, peer_sub)
    greet(slab, before)
    greet(slab, after)
    for k in range(1, chips):
        greet(slab, same_core(k))
    at_seam = (slab == 0) | (slab == slabs - 1)

    @pl.when(at_seam)
    def _():
        for k in range(1, chips):
            greet(slabs - 1 - slab, same_core(k))

    extra = jnp.where(at_seam, chips - 1, 0)
    pl.semaphore_wait(barrier, 7 + chips + extra)

    def remote(source, target, sems, place, peer):
        return pltpu.make_async_remote_copy(
            src_ref=source,
            dst_ref=target,
            send_sem=sems[0].at[place],
            recv_sem=sems[1].at[place],
            device_id=peer,
            device_id_type=MESH,
        )

    near = (near_send, near_recv)
    edge = pl.ds(main, 8)
    last_edge = pl.ds(main + 8, 8)
    right = remote(own.at[edge], got_edges.at[0], near, 0, (slab, after))
    right.start()
    upward = (
        remote(above.at[pl.ds(0, main)], got_main, near, 1, (up, sub)),
        remote(above.at[edge], got_edges.at[1], near, 2, (up, before)),
        remote(above.at[last_edge], got_edges.at[2], near, 3, (up, after)),
    )

    def far(k):
        return remote(above, sheared.at[sub], (far_send, far_recv), k, (up, same_core(k)))

    def far_arrival(k):
        return remote(
            above, sheared.at[same_core(-k)], (far_send, far_recv), k, (up, same_core(k))
        )

    @pl.when(slab != slabs - 1)
    def _():
        for one in upward:
            one.start()

    @pl.when(slab == slabs - 1)
    def _():
        for k in range(chips):
            far(k).start()

    right.wait_recv()

    @pl.when(slab != 0)
    def _():
        for one in upward:
            one.wait_recv()
        gathered[sub] = own[0:main] + got_main[...]
        gathered[sub, 0:5] = gathered[sub, 0:5] + (got_edges[0, 0:5] + got_edges[2, 0:5])
        gathered[sub, main - 5 : main] = gathered[sub, main - 5 : main] + got_edges[1, 0:5]

    @pl.when(slab == 0)
    def _():
        gathered[sub] = own[0:main]
        gathered[sub, 0:5] = gathered[sub, 0:5] + got_edges[0, 0:5]

    def to_chip(k, slot):
        return remote(
            gathered.at[sub],
            gathered.at[slot],
            (chip_send, chip_recv),
            k,
            (slab, same_core(k)),
        )

    def to_core(k):
        block = gathered.at[same_core(-k)]
        return remote(block, block, (core_send, core_recv), k, (slab, partner))

    def pass_on(k):
        block = sheared.at[same_core(-k)]
        return remote(block, block, (pass_send, pass_recv), k, (slab, partner))

    order = sorted(range(1, chips), key=lambda k: -min(k, chips - k))
    for k in order:
        to_chip(k, sub).start()
    to_core(0).start()
    for k in reversed(order):
        to_chip(k, same_core(-k)).wait_recv()
        to_core(k).start()

    @pl.when(slab == 0)
    def _():
        for k in [0] + order[::-1]:
            far_arrival(k).wait_recv()
            pass_on(k).start()
        for k in range(chips):
            pass_on(k).wait_recv()
            pass_on(k).wait_send()

    for k in range(chips):
        to_core(k).wait_recv()
        to_core(k).wait_send()
    for k in order:
        to_chip(k, sub).wait_send()
    right.wait_send()

    @pl.when(slab != slabs - 1)
    def _():
        for one in upward:
            one.wait_send()

    @pl.when(slab == slabs - 1)
    def _():
        for k in range(chips):
            far(k).wait_send()


def collect_sums(own, above, slabs, subs):
    chips = subs // 2
    main = own.shape[0] - 8
    return pl.pallas_call(
        functools.partial(collect_kernel, slabs, subs),
        out_shape=(
            jax.ShapeDtypeStruct((subs, main, LEAF), jnp.float32),
            jax.ShapeDtypeStruct((subs, main + 16, LEAF), jnp.float32),
        ),
        in_specs=[VMEM, VMEM],
        out_specs=(VMEM, VMEM),
        scratch_shapes=[
            pltpu.VMEM((main, LEAF), jnp.float32),
            pltpu.VMEM((3, 8, LEAF), jnp.float32),
            pltpu.SemaphoreType.DMA((4,)),
            pltpu.SemaphoreType.DMA((4,)),
        ]
        + [pltpu.SemaphoreType.DMA((chips,))] * 8,
        compiler_params=pltpu.CompilerParams(collective_id=2, has_side_effects=True),
        name="collect_sums",
    )(own, above)


def total_kernel(subs, homes, tables, gathered, sheared, out, joined):
    slab_leaves = subs * homes
    main = 5 * homes
    first_slab = lax.axis_index("slab") == 0

    def place_all(extra):
        def one(device, carry):
            for place in range(homes):
                column = device * homes + place
                start = pl.multiple_of(column * LEAF, LEAF)
                total = gathered[device, 5 * place : 5 * place + 5, :]
                if extra is not None:
                    total = total + extra(column)
                out[:, pl.ds(start, LEAF)] = total
            return carry

        lax.fori_loop(0, subs, one, 0)

    @pl.when(jnp.logical_not(first_slab))
    def _():
        place_all(None)

    @pl.when(first_slab)
    def _():
        def most(k, value):
            return jnp.maximum(value, tables[k, 2 * homes * KINDS])

        shear = lax.fori_loop(0, 4 * subs, most, jnp.int32(0), unroll=8)

        def join(device, carry):
            nearer, later = (device + subs - 1) & (subs - 1), (device + 1) & (subs - 1)
            for place in range(homes):
                total = sheared[device, 5 * place : 5 * place + 5, :]
                if place == 0:
                    total = total + sheared[nearer, main + 8 : main + 13, :]
                if place == homes - 1:
                    total = total + sheared[later, main : main + 5, :]
                joined[device * homes + place, 0:5, :] = total
            return carry

        lax.fori_loop(0, subs, join, 0)
        place_all(
            lambda column: joined[(column - shear + slab_leaves) & (slab_leaves - 1), 0:5, :]
        )


def total_rates(tables, gathered, sheared, subs, homes):
    return pl.pallas_call(
        functools.partial(total_kernel, subs, homes),
        out_shape=jax.ShapeDtypeStruct((5, subs * homes * LEAF), jnp.float32),
        in_specs=[SMEM, VMEM, VMEM],
        out_specs=VMEM,
        scratch_shapes=[pltpu.VMEM((subs * homes, 8, LEAF), jnp.float32)],
        name="total_rates",
    )(tables, gathered, sheared)


def shards(slabs, subs, positions, velocity, density, pressure, counts, pair_list):
    slab_leaves = counts.shape[0]
    slab = lax.axis_index("slab")
    row = table_row(pair_list, slab, slabs, slab_leaves, slab_leaves // subs)
    tables, own, below, above, beyond = exchange(
        row,
        counts,
        positions,
        velocity,
        density.reshape(slab_leaves, LEAF),
        pressure.reshape(slab_leaves, LEAF),
        slabs,
        subs,
    )
    tables = tables.reshape(4 * subs, LEAF)
    own_part, above_part = pair_sums(tables, counts, (below, own, above, beyond), slabs, subs)
    gathered, sheared = collect_sums(own_part, above_part, slabs, subs)
    return total_rates(tables, gathered, sheared, subs, slab_leaves // subs)


def solution(mesh):
    placed = (
        P(None, "slab"),
        P(None, "slab"),
        P("slab"),
        P("slab"),
        P("slab"),
        P(None, ("slab", "sub")),
    )
    return jax.shard_map(
        functools.partial(shards, mesh.shape["slab"], mesh.shape["sub"]),
        mesh=mesh,
        in_specs=placed,
        out_specs=P(None, "slab"),
        check_vma=False,
    )
```

```python
import functools
import math

import jax
import jax.numpy as jnp
from jax import lax
from jax.experimental import pallas as pl
from jax.experimental.pallas import tpu as pltpu
from jax.sharding import PartitionSpec as P

LEAF = 128
KINDS = 5
WIN = 12
LEVELS = 4
GAMMA = 5.0 / 3.0
SUPPORT = 1.5
KERNEL_NORM = 4.0 * 21.0 / (2.0 * math.pi * SUPPORT**3)
MOMENT_REG = 0.05
AREA_FLOOR = 0.0001
FAR_AWAY = 1.0e6
DEAD_ABOVE = 1.0e5
TINY = 1.2e-38
BLOCK = 2
MESH = pl.DeviceIdType.MESH
VMEM = pl.BlockSpec(memory_space=pltpu.VMEM)
SMEM = pl.BlockSpec(memory_space=pltpu.SMEM)
HIGHEST = lax.Precision.HIGHEST


def table_row(pair_list, slab, slabs, slab_leaves, homes):
    home, other, offset = pair_list[0], pair_list[1], pair_list[2]
    occupied = home >= 0
    crossing = occupied & (home // slab_leaves != other // slab_leaves)
    step = (other - home + offset + 1) & (slab_leaves - 1)
    kind = jnp.where(other == home, 0, jnp.where(crossing, 2 + step, 1))
    key = jnp.where(occupied & (kind < KINDS), (home & (homes - 1)) * KINDS + kind, -1)
    shear = jnp.where(crossing & (slab == slabs - 1), (-offset) & (slab_leaves - 1), 0)
    lane = jnp.arange(LEAF, dtype=jnp.int32)[:, None]
    size = homes * KINDS
    number = jnp.where(key[None] == lane, 1, 0)
    moved = jnp.where(key[None] == lane - size, offset[None], 0)
    shears = jnp.where(lane == 2 * size, shear[None], 0)
    signed = jnp.where((lane >= size) & (lane < 2 * size) & (moved < 0), moved, 0)
    row = jnp.sum(number, axis=1) + jnp.max(moved + shears, axis=1) + jnp.min(signed, axis=1)
    return row.reshape(1, 1, LEAF)


def exchange_kernel(
    slabs,
    subs,
    row_ref,
    counts,
    positions,
    velocity,
    density,
    pressure,
    lists,
    own,
    below,
    above,
    beyond,
    to_up,
    to_down,
    to_second,
    records,
    list_sems,
    window_sems,
):
    slab = lax.axis_index("slab")
    sub = lax.axis_index("sub")
    slab_leaves = counts.shape[0]
    homes = slab_leaves // subs
    barrier = pltpu.get_barrier_semaphore()

    def each_sub(first, body):
        def one(k, carry):
            body(k)
            return carry

        lax.fori_loop(first, subs, one, 0, unroll=4 if first == 0 else 5)

    for shift in (-2, -1, 0, 1, 2):
        peer_slab = (slab + shift + slabs) & (slabs - 1)

        def greet(k, peer_slab=peer_slab):
            pl.semaphore_signal(
                barrier,
                inc=1,
                device_id=(peer_slab, (sub + k) & (subs - 1)),
                device_id_type=MESH,
            )

        each_sub(1 if shift == 0 else 0, greet)

    lane = lax.broadcasted_iota(jnp.int32, (1, LEAF), 1)
    row = lax.broadcasted_iota(jnp.int32, (3, LEAF), 0)

    def record(leaf, carry):
        start = pl.multiple_of(leaf * LEAF, LEAF)
        live = lane < counts[leaf]
        centre = jnp.where(
            row == 0,
            slab.astype(jnp.float32) + 0.5,
            jnp.where(row == 1, leaf.astype(jnp.float32) + 0.5, 0.5),
        )
        place = (positions[:, pl.ds(start, LEAF)] - centre) * (1.0 / SUPPORT)
        records[leaf, 0:3, :] = jnp.where((row > 0) | live, place, FAR_AWAY)
        records[leaf, 3:6, :] = velocity[:, pl.ds(start, LEAF)]
        records[leaf, 6:7, :] = density[pl.ds(leaf, 1), :]
        records[leaf, 7:8, :] = pressure[pl.ds(leaf, 1), :]
        return carry

    lax.fori_loop(0, slab_leaves, record, 0, unroll=4)

    def fill(target, shift):
        first = sub * homes - 2 + shift + 2 * slab_leaves
        for slot in range(WIN):
            target[slot] = records[(first + slot) & (slab_leaves - 1)]

    fill(own, 0)
    pl.semaphore_wait(barrier, 5 * subs - 1)
    mine = pltpu.make_async_copy(
        row_ref, lists.at[pl.ds(2 * subs + sub, 1)], list_sems.at[2]
    )
    mine.start()
    for shift in (-2, 1, -1, 0):
        peer_slab = (slab - shift + slabs) & (slabs - 1)

        def send(k, shift=shift, peer_slab=peer_slab):
            pltpu.make_async_remote_copy(
                src_ref=row_ref,
                dst_ref=lists.at[pl.ds((shift + 2) * subs + sub, 1)],
                send_sem=list_sems.at[0],
                recv_sem=list_sems.at[1],
                device_id=(peer_slab, (sub + k) & (subs - 1)),
                device_id_type=MESH,
            ).start()

        each_sub(1 if shift == 0 else 0, send)
    mine.wait()
    rest = lists.at[pl.ds(0, 4 * subs - 1)]
    everything = pltpu.make_async_remote_copy(
        src_ref=rest,
        dst_ref=rest,
        send_sem=list_sems.at[0],
        recv_sem=list_sems.at[1],
        device_id=((slab + 1) & (slabs - 1), sub),
        device_id_type=MESH,
    )
    everything.wait_recv()
    everything.wait_send()
    shear = jnp.max(
        jnp.where(
            lax.broadcasted_iota(jnp.int32, (4 * subs, 1, LEAF), 2) == 2 * homes * KINDS,
            lists[...],
            0,
        )
    )
    copies = []
    for k, (shift, source, target) in enumerate(
        ((-2, to_second, beyond), (-1, to_down, above), (1, to_up, below))
    ):
        copies.append(
            pltpu.make_async_remote_copy(
                src_ref=source,
                dst_ref=target,
                send_sem=window_sems.at[k],
                recv_sem=window_sems.at[3 + k],
                device_id=((slab + shift + slabs) & (slabs - 1), sub),
                device_id_type=MESH,
            )
        )
    none = jnp.int32(0)
    fill(to_second, jnp.where(slab <= 1, shear, none))
    fill(to_down, jnp.where(slab == 0, shear, none))
    copies[0].start()
    fill(to_up, jnp.where(slab == slabs - 1, -shear, none))
    copies[1].start()
    copies[2].start()
    for one in copies:
        one.wait()


def exchange(row, counts, positions, velocity, density, pressure, slabs, subs):
    window = jax.ShapeDtypeStruct((WIN, 8, LEAF), jnp.float32)
    return pl.pallas_call(
        functools.partial(exchange_kernel, slabs, subs),
        out_shape=(jax.ShapeDtypeStruct((4 * subs, 1, LEAF), jnp.int32),) + (window,) * 4,
        in_specs=[VMEM, SMEM, VMEM, VMEM, VMEM, VMEM],
        out_specs=(VMEM,) * 5,
        scratch_shapes=[pltpu.VMEM((WIN, 8, LEAF), jnp.float32)] * 3
        + [pltpu.VMEM((counts.shape[0], 8, LEAF), jnp.float32)]
        + [pltpu.SemaphoreType.DMA((3,)), pltpu.SemaphoreType.DMA((6,))],
        compiler_params=pltpu.CompilerParams(collective_id=0, has_side_effects=True),
        name="exchange",
    )(row, counts, positions, velocity, density, pressure)


def three_parts(full):
    first = full.astype(jnp.bfloat16).astype(jnp.float32)
    rest = full - first
    second = rest.astype(jnp.bfloat16).astype(jnp.float32)
    return first, second, rest - second


def left_stack(full):
    first, second, third = three_parts(full)
    return jnp.concatenate([first, first, second, second, first, third], axis=0).astype(
        jnp.bfloat16
    )


def right_stack(full):
    first, second, third = three_parts(full)
    return jnp.concatenate([first, second, first, second, third, first], axis=0).astype(
        jnp.bfloat16
    )


def features(entries, scale, row):
    scaled = scale * entries
    full = jnp.concatenate(
        [
            scaled,
            entries[0:1] * scaled,
            jnp.where(row == 0, scale, entries[1:2] * scaled),
            entries[2:3] * scaled,
        ],
        axis=0,
    )
    return jnp.concatenate(three_parts(full), axis=0).astype(jnp.bfloat16)


def moment_rows(sums, entries, row):
    sums = KERNEL_NORM * (sums[0:32] + sums[32:64] + sums[64:96])
    plain, total = sums[0:8], sums[16:17]
    times = (sums[8:16], jnp.where(row == 0, sums[9:10], sums[16:24]), sums[24:32])
    parts = []
    for k in range(3):
        own = entries[k : k + 1]
        parts.append(
            times[k] - own * plain - entries * sums[k : k + 1] + own * (entries * total)
        )
    return parts, total


def displaced(entries, row, gap_x, gap_y, gap_v):
    entries = jnp.where(entries > DEAD_ABOVE, -entries, entries)
    return entries + jnp.where(
        row == 0, gap_x, jnp.where(row == 1, gap_y, jnp.where(row == 4, gap_v, 0.0))
    )


def length_sq(entries):
    x, y, z = entries[0:1], entries[1:2], entries[2:3]
    return x * x + y * y + z * z


def weights(dist_sq):
    dist_sq = jnp.maximum(dist_sq, TINY)
    inside = jnp.maximum(1.0 - dist_sq * lax.rsqrt(dist_sq), 0.0)
    square = inside * inside
    return square * square * (1.25 - inside)


def finish(parts, total, entries):
    live = (entries[0:1] < DEAD_ABOVE).astype(jnp.float32)
    number = total + 1.0 - live
    inverse = 1.0 / number
    area = inverse * SUPPORT**2
    mx, my, mz = parts
    xx = mx[0:1] * area + MOMENT_REG
    xy = mx[1:2] * area
    xz = mx[2:3] * area
    yy = my[1:2] * area + MOMENT_REG
    yz = my[2:3] * area
    zz = mz[2:3] * area + MOMENT_REG
    minor_xx = yy * zz - yz * yz
    minor_xy = xz * yz - xy * zz
    minor_xz = xy * yz - xz * yy
    minor_yy = xx * zz - xz * xz
    minor_yz = xy * xz - xx * yz
    minor_zz = xx * yy - xy * xy
    unit = 1.0 / (xx * minor_xx + xy * minor_xy + xz * minor_xz)
    ixx, ixy, ixz = minor_xx * unit, minor_xy * unit, minor_xz * unit
    iyy, iyz, izz = minor_yy * unit, minor_yz * unit, minor_zz * unit
    half = 0.5 * area
    mx, my, mz = mx * half, my * half, mz * half
    slope_x = ixx * mx + ixy * my + ixz * mz
    slope_y = ixy * mx + iyy * my + iyz * mz
    slope_z = ixz * mx + iyz * my + izz * mz
    scale = (KERNEL_NORM * SUPPORT) * inverse * inverse
    inverse_rows = [k * scale for k in (ixx, ixy, ixz, iyy, iyz, izz)]
    return number, (slope_x, slope_y, slope_z), inverse_rows


def flux_base(entries, row, last):
    return jnp.where(row < 6, entries, jnp.where(row == 6, 1.0, last))


def flux_coefficients(entries, slopes, inverse_rows, row):
    x, y, z = entries[0:1], entries[1:2], entries[2:3]
    constant = entries - slopes[0] * x - slopes[1] * y - slopes[2] * z
    planes = []
    for q in range(5):
        at = slice(3 + q, 4 + q)
        plane = jnp.where(
            row == 0,
            slopes[0][at],
            jnp.where(
                row == 1,
                slopes[1][at],
                jnp.where(row == 2, slopes[2][at], jnp.where(row == 6, constant[at], 0.0)),
            ),
        )
        if q < 3:
            plane = jnp.where(row == 3 + q, -1.0, plane)
        planes.append(plane)
    ixx, ixy, ixz, iyy, iyz, izz = inverse_rows
    for a, b, c in ((ixx, ixy, ixz), (ixy, iyy, iyz), (ixz, iyz, izz)):
        rest = -(a * x + b * y + c * z)
        planes.append(
            jnp.where(
                row == 0,
                a,
                jnp.where(row == 1, b, jnp.where(row == 2, c, jnp.where(row == 6, rest, 0.0))),
            )
        )
    return planes


PLANES = 14


def flux_terms(plane, near, far, weight):
    smooth = weights(plane(13))
    area = [smooth * plane(10 + k) for k in range(3)]
    area_sq = area[0] * area[0] + area[1] * area[1] + area[2] * area[2]
    root = lax.rsqrt(jnp.maximum(area_sq, TINY))
    size = area_sq * root * weight
    root = jnp.minimum(root, 1.0 / AREA_FLOOR)
    normal = [area[k] * root for k in range(3)]
    left_vel, right_vel, face = [], [], []
    for q in range(3):
        a, b = near(q), far(q)
        face.append(a + b)
        high = jnp.abs(b - a)
        low = -high
        left_vel.append(jnp.minimum(jnp.maximum(plane(q), low), high))
        right_vel.append(jnp.minimum(jnp.maximum(plane(5 + q), low), high))
    states = []
    for q in (3, 4):
        a, b = near(q), far(q)
        low, high = jnp.minimum(a, b), jnp.maximum(a, b)
        states.append(jnp.minimum(jnp.maximum(plane(q), low), high))
        states.append(jnp.minimum(jnp.maximum(plane(5 + q), low), high))
    left_rho, right_rho, left_p, right_p = states
    left_un = left_vel[0] * normal[0] + left_vel[1] * normal[1] + left_vel[2] * normal[2]
    right_un = right_vel[0] * normal[0] + right_vel[1] * normal[1] + right_vel[2] * normal[2]
    root_gamma = math.sqrt(GAMMA)
    left_c = root_gamma * left_p * lax.rsqrt(left_p * left_rho)
    right_c = root_gamma * right_p * lax.rsqrt(right_p * right_rho)
    speed_left = jnp.minimum(left_un - left_c, right_un - right_c)
    speed_right = jnp.maximum(left_un + left_c, right_un + right_c)
    left_m = left_rho * (speed_left - left_un)
    right_m = right_rho * (speed_right - right_un)
    top = right_p - left_p + left_m * left_un - right_m * right_un
    bottom = left_m - right_m
    is_left = top <= 0.0

    def pick(left, right):
        return jnp.where(is_left, left, right)

    rho, p, un = pick(left_rho, right_rho), pick(left_p, right_p), pick(left_un, right_un)
    m, c, speed = pick(left_m, right_m), pick(left_c, right_c), pick(speed_left, speed_right)
    wave = pick(jnp.minimum(speed_left, 0.0), jnp.maximum(speed_right, 0.0))
    lab = [pick(left_vel[k], right_vel[k]) + face[k] for k in range(3)]
    lead = speed * bottom - top
    joint = 1.0 / (bottom * lead)
    contact = top * (lead * joint)
    spread = bottom * (bottom * joint)
    push = wave * ((contact - un) * spread)
    mass = (rho * un + wave * (m * spread - rho)) * size
    thrust = (p + push * m) * size
    carried = (1.5 / GAMMA) * (c * c) + 0.5 * (
        lab[0] * lab[0] + lab[1] * lab[1] + lab[2] * lab[2]
    )
    drift = face[0] * normal[0] + face[1] * normal[1] + face[2] * normal[2]
    energy = mass * carried + drift * thrust + size * (p * un + push * (m * contact + p))
    return [mass] + [lab[k] * mass + normal[k] * thrust for k in range(3)] + [energy]


def pair_kernel(
    slabs,
    subs,
    tables,
    counts,
    below,
    own,
    above,
    beyond,
    own_out,
    above_out,
    store,
    numbers,
    coefficients,
    right_parts,
    left_parts,
    near_rows,
    far_rows,
    planes_one,
    planes_two,
    row_sums,
    flux_sums,
    bases,
    mine_one,
    mine_two,
    tiles,
    tile_gaps,
):
    slab = lax.axis_index("slab")
    sub = lax.axis_index("sub")
    slab_leaves = counts.shape[0]
    homes = slab_leaves // subs
    table_size = homes * KINDS
    row = lax.broadcasted_iota(jnp.int32, (8, LEAF), 0)
    for level, source in enumerate((below, own, above, beyond)):
        store[pl.ds(level * WIN, WIN)] = source[...]
    flux_sums[...] = jnp.zeros_like(flux_sums)

    def most(k, value):
        return jnp.maximum(value, tables[k, 2 * table_size])

    shear = lax.fori_loop(0, 4 * subs, most, jnp.int32(0), unroll=8)

    def home_facts(level, place):
        shift = jnp.where(
            (level == 0) & (slab == 0),
            -shear,
            jnp.where((level == 2) & (slab == slabs - 1), shear, 0),
        )
        column = (sub * homes + place + shift + 2 * slab_leaves) & (slab_leaves - 1)
        level_slab = (slab - 1 + level + slabs) & (slabs - 1)
        return level, column, level_slab == slabs - 1

    def pair_facts(facts, kind):
        level, column, last = facts
        device = (level + 1) * subs + column // homes
        entry = (column & (homes - 1)) * KINDS + kind
        crossing = kind >= 2
        step = jnp.where(crossing, kind - 3, jnp.where(kind == 1, 1, 0))
        wraps = crossing & last
        other_column = (
            column + step + jnp.where(wraps, shear, 0) + slab_leaves
        ) & (slab_leaves - 1)
        gap_x = jnp.where(crossing, 1.0 / SUPPORT, 0.0).astype(jnp.float32)
        gap_y = (other_column + tables[device, table_size + entry] - column).astype(
            jnp.float32
        ) * (1.0 / SUPPORT)
        gap_v = jnp.where(wraps, -1.0, 0.0).astype(jnp.float32)
        return tables[device, entry], step + jnp.where(crossing, WIN, 0), gap_x, gap_y, gap_v

    own_first, above_first = WIN + 2, 2 * WIN + 1
    halves = jnp.where((row >= 3) & (row < 6), 0.5, 1.0).astype(jnp.float32)

    def finish_one(k, carry):
        k = jnp.minimum(k, 2 * homes + 2)
        level = jnp.where(k <= homes, 1, 2)
        place = jnp.where(k <= homes, k, k - (homes + 2))
        leaf = level * WIN + place + 2
        mine = store[leaf]
        near_sq = length_sq(mine)
        left = jnp.where(
            row < 3, -2.0 * mine, jnp.where(row == 3, 1.0, jnp.where(row == 4, near_sq, 0.0))
        )
        left = jnp.transpose(left_stack(left).astype(jnp.float32)).astype(jnp.bfloat16)
        here = home_facts(level, place)
        pairs = [(here, kind, 1) for kind in range(KINDS)]
        pairs.append((home_facts(level, place - 1), 1, -1))
        pairs += [(home_facts(level - 1, place + 3 - kind), kind, -1) for kind in (2, 3, 4)]
        sums = None
        for first in range(0, len(pairs), 2):
            rows, rights = [], []
            for facts, kind, sign in pairs[first : first + 2]:
                number, away, gap_x, gap_y, gap_v = pair_facts(facts, kind)
                theirs = displaced(
                    store[leaf + sign * away], row, sign * gap_x, sign * gap_y, sign * gap_v
                )
                right = jnp.where(
                    row < 3,
                    theirs,
                    jnp.where(row == 3, length_sq(theirs), jnp.where(row == 4, 1.0, 0.0)),
                )
                rights.append(right_stack(right))
                rows.append(features(theirs, number.astype(jnp.float32), row))
            smooth = weights(
                lax.dot_general(
                    left,
                    jnp.concatenate(rights, axis=1),
                    (((1,), (0,)), ((), ())),
                    preferred_element_type=jnp.float32,
                )
            )
            high = smooth.astype(jnp.bfloat16)
            low = (smooth - high.astype(jnp.float32)).astype(jnp.bfloat16)
            part = lax.dot_general(
                jnp.concatenate(rows + rows, axis=1),
                jnp.concatenate([high, low], axis=1),
                (((1,), (1,)), ((), ())),
                preferred_element_type=jnp.float32,
            )
            sums = part if sums is None else sums + part
        parts, total = moment_rows(sums, mine, row)
        number, slopes, inverse_rows = finish(parts, total, mine)
        halved = mine * halves
        numbers[leaf] = jnp.broadcast_to(number, (8, LEAF))
        pad = jnp.zeros((16, LEAF), jnp.bfloat16)
        for k, plane in enumerate(flux_coefficients(halved, slopes, inverse_rows, row)):
            coefficients[leaf, k] = plane
            part = right_stack(plane if k < 5 else -plane)
            right_parts[leaf, k] = jnp.concatenate([part, pad], axis=0)
        return carry

    lax.fori_loop(0, 2 * homes + 4, finish_one, 0, unroll=4)

    blank = jnp.zeros((LEAF, LEAF), jnp.float32)

    def turned_left(full):
        stack = left_stack(full).astype(jnp.float32)
        return jnp.transpose(jnp.concatenate([stack, blank[:80]], axis=0)).astype(jnp.bfloat16)

    deep = lax.broadcasted_iota(jnp.int32, (LEAF, LEAF), 0)
    pickers = [
        jnp.where((deep < 24) & ((deep & 7) == 3 + k), 1.0, 0.0).astype(jnp.bfloat16)
        for k in range(5)
    ]

    def prepare_home(place, carry):
        leaf = own_first + place
        mine = store[leaf] * halves
        for k in range(8):
            left_parts[place, k] = turned_left(coefficients[leaf, k])
        distance = jnp.where(
            row < 3,
            -2.0 * mine,
            jnp.where(row < 6, 0.0, jnp.where(row == 6, length_sq(mine), 1.0)),
        )
        left_parts[place, 8] = turned_left(distance)
        parts = jnp.concatenate([*three_parts(mine), blank[:104]], axis=0)
        turned = jnp.transpose(parts).astype(jnp.bfloat16)
        for k in range(5):
            near_rows[place, k] = lax.dot_general(
                turned,
                pickers[k],
                (((1,), (0,)), ((), ())),
                preferred_element_type=jnp.float32,
            ).reshape(LEAF // 8, 8, LEAF)
        row_sums[place] = jnp.zeros((5, LEAF // 8, 8, LEAF), jnp.float32)
        return carry

    lax.fori_loop(0, homes, prepare_home, 0, unroll=4)

    def put_tile(index, place, other, gap_x, gap_y, gap_v, scale):
        tiles[2 * index] = place
        tiles[2 * index + 1] = other
        for k, value in enumerate((gap_x, gap_y, gap_v, scale)):
            tile_gaps[4 * index + k] = value

    filled = jnp.int32(0)
    for place in range(homes):
        facts = home_facts(1, place)
        for kind in range(KINDS):
            number, away, gap_x, gap_y, gap_v = pair_facts(facts, kind)
            scale = number.astype(jnp.float32) * (0.5 if kind == 0 else 1.0)
            other = jnp.int32(own_first + place) + away
            put_tile(filled, jnp.int32(place), other, gap_x, gap_y, 0.5 * gap_v, scale)
            filled = filled + jnp.where(number > 0, 1, 0)
    nought = jnp.float32(0.0)
    for k in range(3):
        put_tile(filled + k, jnp.int32(0), jnp.int32(own_first), nought, nought, nought, nought)

    def tile_facts(index):
        place = tiles[2 * index]
        gaps = [tile_gaps[4 * index + k] for k in range(4)]
        return (place, own_first + place, tiles[2 * index + 1], *gaps)

    def ready_tile(index, base_rows, mine_rows):
        place, leaf, other, gap_x, gap_y, gap_v, _ = tile_facts(index)
        theirs = displaced(store[other] * halves, row, gap_x, gap_y, gap_v)
        base = right_stack(flux_base(theirs, row, length_sq(theirs)))
        base_rows[...] = jnp.concatenate([base, jnp.zeros((16, LEAF), jnp.bfloat16)], axis=0)
        mine = store[leaf] * halves - jnp.where(
            row == 0, gap_x, jnp.where(row == 1, gap_y, jnp.where(row == 4, gap_v, 0.0))
        )
        stack = left_stack(flux_base(mine, row, 0.0)).astype(jnp.float32)
        mine_rows[...] = jnp.transpose(
            jnp.concatenate([blank[:64], stack, blank[:16]], axis=0)
        ).astype(jnp.bfloat16)

    def lay_planes(index, planes, base_rows, mine_rows):
        place, _, other = tile_facts(index)[:3]
        base, mine = base_rows[...], mine_rows[...]

        def lay(k):
            right = jnp.concatenate([base, right_parts[other, k]], axis=0)
            left = left_parts[place, k]
            if k < 5:
                parts = [left, mine] + ([left_parts[place, 8]] if k == 0 else [])
                targets = [k, 5 + k] + ([13] if k == 0 else [])
            else:
                parts = [left + mine]
                targets = [5 + k]
            for part, target in zip(parts, targets):
                planes[target] = lax.dot_general(
                    part,
                    right,
                    (((1,), (0,)), ((), ())),
                    preferred_element_type=jnp.float32,
                ).reshape(LEAF // 8, 8, LEAF)

        return lay

    def add_fluxes(index, planes, far_rows):
        place, _, other, gap_x, gap_y, gap_v, scale = tile_facts(index)
        theirs = displaced(store[other] * halves, row, gap_x, gap_y, gap_v)
        for k in range(5):
            far_rows[k] = jnp.broadcast_to(theirs[3 + k : 4 + k], (8, LEAF))
        totals = [None] * 5

        def step(first):
            terms = flux_terms(
                lambda k: planes[k, first : first + BLOCK],
                lambda k: near_rows[place, k, first : first + BLOCK],
                lambda k: far_rows[k][None],
                scale,
            )
            for k in range(5):
                row_sums[place, k, first : first + BLOCK] += terms[k]
                part = jnp.sum(terms[k], axis=0)
                totals[k] = part if totals[k] is None else totals[k] + part

        def close():
            added = [jnp.sum(part, axis=0, keepdims=True) for part in totals]
            nothing = jnp.zeros((3, LEAF), jnp.float32)
            flux_sums[other] = flux_sums[other] + jnp.concatenate(added + [nothing], axis=0)

        return step, close

    slots = (
        (planes_one, bases.at[0], mine_one, far_rows.at[0]),
        (planes_two, bases.at[1], mine_two, far_rows.at[1]),
    )

    def both(index, this, that):
        lay = lay_planes(index + 1, *that[:3])
        step, close = add_fluxes(index, this[0], this[3])
        steps = list(range(0, LEAF // 8, BLOCK))
        pace = len(steps) / 8
        for k in range(8):
            lay(k)
            for first in steps[int(k * pace) : int((k + 1) * pace)]:
                step(first)
        close()
        ready_tile(index + 2, *this[1:3])

    ready_tile(0, *slots[0][1:3])
    ready_tile(1, *slots[1][1:3])
    first_lay = lay_planes(0, *slots[0][:3])
    for k in range(8):
        first_lay(k)

    def two_tiles(step, carry):
        both(2 * step, slots[0], slots[1])

        @pl.when(2 * step + 1 < filled)
        def _():
            both(2 * step + 1, slots[1], slots[0])

        return carry

    lax.fori_loop(0, (filled + 1) // 2, two_tiles, 0)
    def close_home(place, carry):
        leaf = own_first + place
        taken = []
        for k in range(5):
            turned = jnp.transpose(row_sums[place, k].reshape(LEAF, LEAF))
            taken.append(jnp.sum(turned, axis=0, keepdims=True))
        nothing = jnp.zeros((3, LEAF), jnp.float32)
        flux_sums[leaf] = flux_sums[leaf] - jnp.concatenate(taken + [nothing], axis=0)
        return carry

    lax.fori_loop(0, homes, close_home, 0, unroll=4)
    gap = jnp.zeros((3, LEAF), jnp.float32)

    def put(out, start, leaf, padded):
        rates = (flux_sums[leaf] * numbers[leaf])[0:5]
        if padded:
            out[start : start + 8, :] = jnp.concatenate([rates, gap], axis=0)
        else:
            out[start : start + 5, :] = rates

    for k in range(homes):
        put(own_out, 5 * k, own_first + k, False)
        put(above_out, 5 * k, above_first + 1 + k, False)
    put(own_out, 5 * homes, own_first + homes, True)
    put(above_out, 5 * homes, above_first, True)
    put(above_out, 5 * homes + 8, above_first + homes + 1, True)


def pair_sums(tables, counts, windows, slabs, subs):
    homes = counts.shape[0] // subs
    leaves = LEVELS * WIN
    return pl.pallas_call(
        functools.partial(pair_kernel, slabs, subs),
        out_shape=(
            jax.ShapeDtypeStruct((5 * homes + 8, LEAF), jnp.float32),
            jax.ShapeDtypeStruct((5 * homes + 16, LEAF), jnp.float32),
        ),
        in_specs=[SMEM] * 2 + [VMEM] * 4,
        out_specs=(VMEM, VMEM),
        scratch_shapes=[
            pltpu.VMEM((leaves, 8, LEAF), jnp.float32),
            pltpu.VMEM((leaves, 8, LEAF), jnp.float32),
            pltpu.VMEM((leaves, 8, 8, LEAF), jnp.float32),
            pltpu.VMEM((leaves, 8, 64, LEAF), jnp.bfloat16),
            pltpu.VMEM((homes, 9, LEAF, LEAF), jnp.bfloat16),
            pltpu.VMEM((homes, 5, LEAF // 8, 8, LEAF), jnp.float32),
            pltpu.VMEM((2, 5, 8, LEAF), jnp.float32),
            pltpu.VMEM((PLANES, LEAF // 8, 8, LEAF), jnp.float32),
            pltpu.VMEM((PLANES, LEAF // 8, 8, LEAF), jnp.float32),
            pltpu.VMEM((homes, 5, LEAF // 8, 8, LEAF), jnp.float32),
            pltpu.VMEM((leaves, 8, LEAF), jnp.float32),
            pltpu.VMEM((2, 64, LEAF), jnp.bfloat16),
            pltpu.VMEM((LEAF, LEAF), jnp.bfloat16),
            pltpu.VMEM((LEAF, LEAF), jnp.bfloat16),
            pltpu.SMEM((2 * homes * KINDS + 8,), jnp.int32),
            pltpu.SMEM((4 * homes * KINDS + 16,), jnp.float32),
        ],
        compiler_params=pltpu.CompilerParams(

        ),
        name="pair_sums",
    )(tables, counts, *windows)


def collect_kernel(
    slabs,
    subs,
    own,
    above,
    gathered,
    sheared,
    got_main,
    got_edges,
    near_send,
    near_recv,
    chip_send,
    chip_recv,
    core_send,
    core_recv,
    far_send,
    far_recv,
    pass_send,
    pass_recv,
):
    slab = lax.axis_index("slab")
    sub = lax.axis_index("sub")
    main = gathered.shape[1]
    chips = subs // 2
    partner = sub + 1 - 2 * (sub & 1)
    up, down = (slab + 1) & (slabs - 1), (slab - 1 + slabs) & (slabs - 1)
    after, before = (sub + 1) & (subs - 1), (sub - 1 + subs) & (subs - 1)

    def same_core(k):
        return (sub + 2 * k + subs) & (subs - 1)

    barrier = pltpu.get_barrier_semaphore()

    def greet(*peer):
        pl.semaphore_signal(barrier, inc=1, device_id=peer, device_id_type=MESH)

    for peer_slab in (up, down):
        for peer_sub in (before, sub, after):
            greet(peer_slab, peer_sub)
    greet(slab, before)
    greet(slab, after)
    for k in range(1, chips):
        greet(slab, same_core(k))
    at_seam = (slab == 0) | (slab == slabs - 1)

    @pl.when(at_seam)
    def _():
        for k in range(1, chips):
            greet(slabs - 1 - slab, same_core(k))

    extra = jnp.where(at_seam, chips - 1, 0)
    pl.semaphore_wait(barrier, 7 + chips + extra)

    def remote(source, target, sems, place, peer):
        return pltpu.make_async_remote_copy(
            src_ref=source,
            dst_ref=target,
            send_sem=sems[0].at[place],
            recv_sem=sems[1].at[place],
            device_id=peer,
            device_id_type=MESH,
        )

    near = (near_send, near_recv)
    edge = pl.ds(main, 8)
    last_edge = pl.ds(main + 8, 8)
    right = remote(own.at[edge], got_edges.at[0], near, 0, (slab, after))
    right.start()
    upward = (
        remote(above.at[pl.ds(0, main)], got_main, near, 1, (up, sub)),
        remote(above.at[edge], got_edges.at[1], near, 2, (up, before)),
        remote(above.at[last_edge], got_edges.at[2], near, 3, (up, after)),
    )

    def far(k):
        return remote(above, sheared.at[sub], (far_send, far_recv), k, (up, same_core(k)))

    def far_arrival(k):
        return remote(
            above, sheared.at[same_core(-k)], (far_send, far_recv), k, (up, same_core(k))
        )

    @pl.when(slab != slabs - 1)
    def _():
        for one in upward:
            one.start()

    @pl.when(slab == slabs - 1)
    def _():
        for k in range(chips):
            far(k).start()

    right.wait_recv()

    @pl.when(slab != 0)
    def _():
        for one in upward:
            one.wait_recv()
        gathered[sub] = own[0:main] + got_main[...]
        gathered[sub, 0:5] = gathered[sub, 0:5] + (got_edges[0, 0:5] + got_edges[2, 0:5])
        gathered[sub, main - 5 : main] = gathered[sub, main - 5 : main] + got_edges[1, 0:5]

    @pl.when(slab == 0)
    def _():
        gathered[sub] = own[0:main]
        gathered[sub, 0:5] = gathered[sub, 0:5] + got_edges[0, 0:5]

    def to_chip(k, slot):
        return remote(
            gathered.at[sub],
            gathered.at[slot],
            (chip_send, chip_recv),
            k,
            (slab, same_core(k)),
        )

    def to_core(k):
        block = gathered.at[same_core(-k)]
        return remote(block, block, (core_send, core_recv), k, (slab, partner))

    def pass_on(k):
        block = sheared.at[same_core(-k)]
        return remote(block, block, (pass_send, pass_recv), k, (slab, partner))

    order = sorted(range(1, chips), key=lambda k: -min(k, chips - k))
    for k in order:
        to_chip(k, sub).start()
    to_core(0).start()
    for k in reversed(order):
        to_chip(k, same_core(-k)).wait_recv()
        to_core(k).start()

    @pl.when(slab == 0)
    def _():
        for k in [0] + order[::-1]:
            far_arrival(k).wait_recv()
            pass_on(k).start()
        for k in range(chips):
            pass_on(k).wait_recv()
            pass_on(k).wait_send()

    for k in range(chips):
        to_core(k).wait_recv()
        to_core(k).wait_send()
    for k in order:
        to_chip(k, sub).wait_send()
    right.wait_send()

    @pl.when(slab != slabs - 1)
    def _():
        for one in upward:
            one.wait_send()

    @pl.when(slab == slabs - 1)
    def _():
        for k in range(chips):
            far(k).wait_send()


def collect_sums(own, above, slabs, subs):
    chips = subs // 2
    main = own.shape[0] - 8
    return pl.pallas_call(
        functools.partial(collect_kernel, slabs, subs),
        out_shape=(
            jax.ShapeDtypeStruct((subs, main, LEAF), jnp.float32),
            jax.ShapeDtypeStruct((subs, main + 16, LEAF), jnp.float32),
        ),
        in_specs=[VMEM, VMEM],
        out_specs=(VMEM, VMEM),
        scratch_shapes=[
            pltpu.VMEM((main, LEAF), jnp.float32),
            pltpu.VMEM((3, 8, LEAF), jnp.float32),
            pltpu.SemaphoreType.DMA((4,)),
            pltpu.SemaphoreType.DMA((4,)),
        ]
        + [pltpu.SemaphoreType.DMA((chips,))] * 8,
        compiler_params=pltpu.CompilerParams(collective_id=2, has_side_effects=True),
        name="collect_sums",
    )(own, above)


def total_kernel(subs, homes, tables, gathered, sheared, out, joined):
    slab_leaves = subs * homes
    main = 5 * homes
    first_slab = lax.axis_index("slab") == 0

    def place_all(extra):
        def one(device, carry):
            for place in range(homes):
                column = device * homes + place
                start = pl.multiple_of(column * LEAF, LEAF)
                total = gathered[device, 5 * place : 5 * place + 5, :]
                if extra is not None:
                    total = total + extra(column)
                out[:, pl.ds(start, LEAF)] = total
            return carry

        lax.fori_loop(0, subs, one, 0)

    @pl.when(jnp.logical_not(first_slab))
    def _():
        place_all(None)

    @pl.when(first_slab)
    def _():
        def most(k, value):
            return jnp.maximum(value, tables[k, 2 * homes * KINDS])

        shear = lax.fori_loop(0, 4 * subs, most, jnp.int32(0), unroll=8)

        def join(device, carry):
            nearer, later = (device + subs - 1) & (subs - 1), (device + 1) & (subs - 1)
            for place in range(homes):
                total = sheared[device, 5 * place : 5 * place + 5, :]
                if place == 0:
                    total = total + sheared[nearer, main + 8 : main + 13, :]
                if place == homes - 1:
                    total = total + sheared[later, main : main + 5, :]
                joined[device * homes + place, 0:5, :] = total
            return carry

        lax.fori_loop(0, subs, join, 0)
        place_all(
            lambda column: joined[(column - shear + slab_leaves) & (slab_leaves - 1), 0:5, :]
        )


def total_rates(tables, gathered, sheared, subs, homes):
    return pl.pallas_call(
        functools.partial(total_kernel, subs, homes),
        out_shape=jax.ShapeDtypeStruct((5, subs * homes * LEAF), jnp.float32),
        in_specs=[SMEM, VMEM, VMEM],
        out_specs=VMEM,
        scratch_shapes=[pltpu.VMEM((subs * homes, 8, LEAF), jnp.float32)],
        name="total_rates",
    )(tables, gathered, sheared)


def shards(slabs, subs, positions, velocity, density, pressure, counts, pair_list):
    slab_leaves = counts.shape[0]
    slab = lax.axis_index("slab")
    row = table_row(pair_list, slab, slabs, slab_leaves, slab_leaves // subs)
    tables, own, below, above, beyond = exchange(
        row,
        counts,
        positions,
        velocity,
        density.reshape(slab_leaves, LEAF),
        pressure.reshape(slab_leaves, LEAF),
        slabs,
        subs,
    )
    tables = tables.reshape(4 * subs, LEAF)
    own_part, above_part = pair_sums(tables, counts, (below, own, above, beyond), slabs, subs)
    gathered, sheared = collect_sums(own_part, above_part, slabs, subs)
    return total_rates(tables, gathered, sheared, subs, slab_leaves // subs)


def solution(mesh):
    placed = (
        P(None, "slab"),
        P(None, "slab"),
        P("slab"),
        P("slab"),
        P("slab"),
        P(None, ("slab", "sub")),
    )
    return jax.shard_map(
        functools.partial(shards, mesh.shape["slab"], mesh.shape["sub"]),
        mesh=mesh,
        in_specs=placed,
        out_specs=P(None, "slab"),
        check_vma=False,
    )
```
